32 devices in a mesh: pair: 2 (over x), batch: 16 (over z, y, core).
Axes of the slice: x: 2, y: 2, z: 4, core: 2. Of those that a mesh axis runs over, the one named last changes fastest.
Arguments:
- frames: bfloat16 [2, 3584, 4, 84, 84], P('pair', 'batch'), may hold values from -4 to 4
- kernel_first: bfloat16 [2, 8, 8, 4, 32], P('pair'), may hold values from -0.5 to 0.5
- bias_first: bfloat16 [2, 32], P('pair'), may hold values from -1.5 to 1.5
- kernel_second: bfloat16 [2, 4, 4, 32, 64], P('pair'), may hold values from -0.375 to 0.375
- bias_second: bfloat16 [2, 64], P('pair'), may hold values from -1.5 to 1.5
- kernel_third: bfloat16 [2, 3, 3, 64, 64], P('pair'), may hold values from -0.375 to 0.375
- bias_third: bfloat16 [2, 64], P('pair'), may hold values from -1.5 to 1.5
- dense_weight: bfloat16 [2, 3136, 512], P('pair'), may hold values from -0.15625 to 0.15625
- dense_bias: bfloat16 [2, 512], P('pair'), may hold values from -1.5 to 1.5
- head_weight: bfloat16 [2, 512, 918], P('pair'), may hold values from -0.375 to 0.375
- head_bias: bfloat16 [2, 918], P('pair'), may hold values from -2.5 to 2.5
- taken_actions: int32 [3584], P('batch'), may hold values from 0 to 17
- greedy_actions: int32 [3584], P('batch'), may hold values from 0 to 17
- done_flags: int32 [3584], P('batch'), may hold values 0 or 1
- bin_lower: int32 [3584, 51], P('batch'), may hold values from 0 to 49
- bin_fraction: float32 [3584, 51], P('batch'), may hold values from 0 to 1
- owner_shard: int32 [3584, 1], P('batch'), may hold values from 0 to 15; in each aligned block of 224 rows (0 to 223, 224 to 447, ...) at most 28 rows name the same one
Outputs:
- first_kernel_grad: float32 [8, 8, 4, 32], P('pair')
- first_bias_grad: float32 [32], P('pair')
- second_kernel_grad: float32 [4, 4, 32, 64], P('pair')
- second_bias_grad: float32 [64], P('pair')
- third_kernel_grad: float32 [3, 3, 64, 64], P(None, None, None, 'pair')
- third_bias_grad: float32 [64], P('pair')
- dense_weight_grad: float32 [3136, 512], P(None, 'pair')
- dense_bias_grad: float32 [512], P('pair')
- head_weight_grad: float32 [512, 918], P('pair')
- head_bias_grad: float32 [918], P('pair')
- frame_grad: bfloat16 [3584, 4, 84, 84], P('batch', 'pair')
- priorities: float32 [16, 16, 28], P('batch', None, 'pair')
The draws below stay inside these ranges and needn't reach their ends.
Inputs may be any that keep to these rules, and one draw needn't show every extreme that they name: `owner_shard`: among the 224 rows of one index of batch (aligned blocks), at most 28 name the same shard, and in every draw some shard is named by exactly 28 of them.
All inputs are finite; a program needn't handle non-finite values. No bound on the sum of `done_flags` on one device may be relied on, other than what follows from the above.
Results may differ from the reference program's by a relative error of at most 0.013.
Values may be sent and summed in bfloat16 or wider, within the bound.
No kernel may reach another device: no remote copies, remote signals or barrier semaphores. Data moves between devices by JAX's collectives and lax.ppermute only.
A program may use at most 704 MiB of HBM per device.

```python
import math
import jax
import jax.numpy as jnp
import numpy as np
from jax import lax

SIDE = 84
FRAMES = 4
C1 = 32
C2 = 64
C3 = 64
HID = 512
ACT = 18
ATOMS = 51
LOSS_SCALE = 256
ROWS = 224
FLAT = 3136
TRANS = 3584
CAP = 28
N_BATCH = 16


def touch_ends(result, rng, smallest, high):
    longest = result.shape.index(max(result.shape))
    spots = []
    for shift in (0, 1):
        where = [jax.random.randint(jax.random.fold_in(rng, axis), (), 0, length) for axis, length in enumerate(result.shape)]
        where[longest] = (where[longest] + shift) % result.shape[longest]
        spots.append(tuple(where))
    return result.at[spots[0]].set(smallest).at[spots[1]].set(high)


def steps_of(rng, shape, cuts, smallest, top_value):
    def one(dim, parts):
        heights = jax.random.uniform(jax.random.fold_in(jax.random.fold_in(rng, 6), dim), (parts,), jnp.float32, smallest / len(cuts), top_value / len(cuts))
        return jnp.repeat(jnp.exp(heights), shape[dim] // parts).reshape((-1,) + (1,) * (len(shape) - dim - 1))

    loudness = one(*cuts[0])
    for cut in cuts[1:]:
        loudness = loudness * one(*cut)
    return loudness


def routed_block(stream_key, own, number, rows, amount, top, limit, lean):
    order = jax.random.permutation(stream_key, amount)
    crowded, common = load_shares(amount, rows * top, limit, lean, True), load_shares(amount, rows * top, limit, lean, False)
    places = jnp.arange(amount)

    def named(sizes, rotation):
        used = int((sizes > 0).sum())
        fixed = max(1, used // 4)
        passed = fixed + (places - fixed + rotation * (used - fixed)) % max(1, amount - fixed)
        return jnp.zeros((amount,), jnp.int32).at[order[jnp.where(places < fixed, places, passed)]].set(jnp.asarray(sizes, jnp.int32))

    sizes = jnp.where(number % 4 == 0, named(crowded, number // 4), named(common, number - number // 4 - 1))
    mixed = jax.random.permutation(jax.random.fold_in(own, 3), amount)
    donor, taker = mixed[0:amount // 2 * 2:2], mixed[1:amount // 2 * 2:2]
    room = jnp.minimum(sizes[donor] - 1, limit - sizes[taker]) // 2
    room = jnp.where((donor == order[0]) | (taker == order[0]) | (sizes[taker] == 0), 0, jnp.maximum(room, 0))
    passed = jax.random.randint(jax.random.fold_in(own, 4), (amount // 2,), 0, 1 << 20) % (room + 1)
    sizes = sizes.at[donor].add(-passed).at[taker].add(passed)
    members = jnp.searchsorted(jnp.cumsum(sizes), jnp.arange(rows * top), side="right").astype(jnp.int32)
    listing = members.reshape(top, rows).T
    listing = listing[jax.random.permutation(jax.random.fold_in(own, 1), rows)]
    rotation = jax.random.randint(jax.random.fold_in(own, 2), (rows, 1), 0, top)
    return jnp.take_along_axis(listing, (jnp.arange(top)[None, :] + rotation) % top, axis=1)


def load_shares(amount, total, limit, skew, full):
    portions = [(1 << 20) // math.isqrt(rank ** skew) + 1 for rank in range(1, amount + 1)]
    largest = limit if full else min(limit, max(-(-total // amount), total * portions[0] // sum(portions)))
    least = 1 if total - largest >= amount - 1 else 0
    holding, spare = [largest] + [least] * (amount - 1), total - largest - least * (amount - 1)
    while spare > 0:
        free = [i for i in range(1, amount) if holding[i] < largest] or [i for i in range(1, amount) if holding[i] < limit]
        pool, left = sum([portions[i] for i in free]), spare
        for i in free:
            more = min(limit - holding[i], max(1, left * portions[i] // pool), spare)
            holding[i] = holding[i] + more
            spare = spare - more
    return np.array(holding)


def noise(stream_key, shape, deviation, reach, cuts=(), kind=jnp.bfloat16):
    entries = deviation * jax.random.normal(stream_key, shape, jnp.float32)
    if cuts:
        entries = entries * steps_of(stream_key, shape, cuts, -0.22, 0.18)
    return jnp.clip(entries, -reach, reach).astype(kind)


def setup_inputs(seed: int = 0) -> dict:
    keys = jax.random.split(jax.random.key(seed), 18)
    frames = noise(keys[0], (2, TRANS, FRAMES, SIDE, SIDE), 1.0, 4.0, ((0, 2), (1, 16)))
    kernel_first = noise(keys[1], (2, 8, 8, FRAMES, C1), (32 * FRAMES) ** -0.5, 0.5, ((0, 2),))
    bias_first = noise(keys[2], (2, C1), 0.3, 1.5, ((0, 2),))
    kernel_second = noise(keys[3], (2, 4, 4, C1, C2), (8 * C1) ** -0.5, 0.375, ((0, 2),))
    bias_second = noise(keys[4], (2, C2), 0.3, 1.5, ((0, 2),))
    kernel_third = noise(keys[5], (2, 3, 3, C2, C3), (9 * C2 // 2) ** -0.5, 0.375, ((0, 2),))
    bias_third = noise(keys[6], (2, C3), 0.3, 1.5, ((0, 2),))
    dense_weight = noise(keys[7], (2, FLAT, HID), (FLAT // 2) ** -0.5, 0.15625, ((0, 2),))
    dense_bias = noise(keys[8], (2, HID), 0.3, 1.5, ((0, 2),))
    head_weight = noise(keys[9], (2, HID, ACT * ATOMS), (HID // 2) ** -0.5, 0.375, ((0, 2),))
    head_bias = noise(keys[10], (2, ACT * ATOMS), 0.5, 2.5, ((0, 2),))
    taken_actions = touch_ends(jax.random.randint(keys[11], (TRANS,), 0, ACT), jax.random.fold_in(keys[11], 1), 0, ACT - 1).astype(jnp.int32)
    greedy_actions = touch_ends(jax.random.randint(keys[12], (TRANS,), 0, ACT), jax.random.fold_in(keys[12], 1), 0, ACT - 1).astype(jnp.int32)
    done_flags = touch_ends((jax.random.randint(keys[13], (TRANS,), 0, 4) < 1).astype(jnp.int32), jax.random.fold_in(keys[13], 1), 0, 1)
    bin_lower = touch_ends(jax.random.randint(keys[14], (TRANS, ATOMS), 0, ATOMS - 1), jax.random.fold_in(keys[14], 1), 0, (ATOMS - 1) - 1).astype(jnp.int32)
    bin_fraction = jnp.clip(1.0 * jax.random.uniform(keys[15], (TRANS, ATOMS), jnp.float32) ** steps_of(keys[15], (TRANS, ATOMS), ((0, 16),), -0.2, 0.2), 0.0, 1.0)
    owner_shard_keys = jax.random.split(jax.random.fold_in(keys[16], 1), TRANS // ROWS)
    owner_shard_turns = jax.random.permutation(jax.random.fold_in(keys[16], 3), TRANS // ROWS)
    owner_shard = jax.vmap(lambda own, number: routed_block(jax.random.fold_in(keys[16], 2), own, number, ROWS, N_BATCH, 1, CAP, 1))(owner_shard_keys, owner_shard_turns).reshape((TRANS, 1))
    return {"frames": frames, "kernel_first": kernel_first, "bias_first": bias_first, "kernel_second": kernel_second, "bias_second": bias_second, "kernel_third": kernel_third, "bias_third": bias_third, "dense_weight": dense_weight, "dense_bias": dense_bias, "head_weight": head_weight, "head_bias": head_bias, "taken_actions": taken_actions, "greedy_actions": greedy_actions, "done_flags": done_flags, "bin_lower": bin_lower, "bin_fraction": bin_fraction, "owner_shard": owner_shard}


@jax.custom_vjp
def low(v):
    return lax.optimization_barrier(v.astype(jnp.bfloat16)).astype(jnp.float32)

@jax.custom_vjp
def low_back(v):
    return v

def low_keep(v):
    return (low(v), None)

def low_pass(kept, grad):
    return (grad,)

def back_keep(v):
    return (v, None)

def back_low(kept, grad):
    return (low(grad),)
low.defvjp(low_keep, low_pass)
low_back.defvjp(back_keep, back_low)

def convolve(inputs, kernel, stride):
    return lax.conv_general_dilated(inputs, kernel, (stride, stride), 'VALID', dimension_numbers=('NHWC', 'HWIO', 'NHWC'), precision=lax.Precision.HIGHEST)

def network(params, frame_rows):
    kernel_first, bias_first, kernel_second, bias_second, kernel_third, bias_third, dense_weight, dense_bias, head_weight, head_bias = params
    inputs = jnp.transpose(frame_rows, (0, 2, 3, 1))
    hidden = low(jax.nn.silu(low_back(convolve(inputs, kernel_first, 4)) + bias_first))
    hidden = low(jax.nn.silu(low_back(convolve(hidden, kernel_second, 2)) + bias_second))
    hidden = low(jax.nn.silu(low_back(convolve(hidden, kernel_third, 1)) + bias_third))
    flat_rows = hidden.reshape(hidden.shape[0], -1)
    dense_out = low_back(jnp.dot(flat_rows, dense_weight, precision=lax.Precision.HIGHEST))
    hidden = low(jax.nn.silu(dense_out + dense_bias))
    logits = low_back(jnp.dot(hidden, head_weight, precision=lax.Precision.HIGHEST)) + head_bias
    return logits.reshape(hidden.shape[0], ACT, ATOMS)

def project_mass(chosen, done_rows, lower_bins, fractions):
    atom_ids = jnp.arange(ATOMS, dtype=jnp.int32)
    first_atom = (atom_ids == 0).astype(jnp.float32)
    finished = done_rows.astype(jnp.float32)[:, None]
    atom_mass = (1.0 - finished) * chosen + finished * first_atom[None, :]
    lower_hot = (lower_bins[:, :, None] == atom_ids[None, None, :]).astype(jnp.float32)
    upper_hot = ((lower_bins + 1)[:, :, None] == atom_ids[None, None, :]).astype(jnp.float32)
    spread_table = (1.0 - fractions)[:, :, None] * lower_hot + fractions[:, :, None] * upper_hot
    return jnp.einsum('ri,rij->rj', atom_mass, spread_table, precision=lax.Precision.HIGHEST)

def reference(frames, kernel_first, bias_first, kernel_second, bias_second, kernel_third, bias_third, dense_weight, dense_bias, head_weight, head_bias, taken_actions, greedy_actions, done_flags, bin_lower, bin_fraction, owner_shard):
    stacked = (kernel_first, bias_first, kernel_second, bias_second, kernel_third, bias_third, dense_weight, dense_bias, head_weight, head_bias)
    online = tuple((tensor[0].astype(jnp.float32) for tensor in stacked))
    target = tuple((tensor[1].astype(jnp.float32) for tensor in stacked))
    shards = N_BATCH
    scan_items = (frames[0].reshape(shards, ROWS, FRAMES, SIDE, SIDE), frames[1].reshape(shards, ROWS, FRAMES, SIDE, SIDE), taken_actions.reshape(shards, ROWS), greedy_actions.reshape(shards, ROWS), done_flags.reshape(shards, ROWS), bin_lower.reshape(shards, ROWS, ATOMS), bin_fraction.reshape(shards, ROWS, ATOMS))

    def shard_step(summed, scan_item):
        observed, following, action_rows, greedy_rows, done_rows, lower_bins, fractions = scan_item
        following_rows = following.astype(jnp.float32)

        def loss_of(params, inputs):
            target_logits = network(target, following_rows)
            picked = jnp.take_along_axis(target_logits, greedy_rows[:, None, None], axis=1)[:, 0, :]
            chosen = low(jax.nn.softmax(picked, axis=-1))
            projected = project_mass(chosen, done_rows, lower_bins, fractions)
            logits = network(params, inputs)
            taken_row = jnp.take_along_axis(logits, action_rows[:, None, None], axis=1)[:, 0, :]
            row_loss = -lax.optimization_barrier(jnp.sum(projected * jax.nn.log_softmax(taken_row, axis=-1), axis=-1))
            return (jnp.sum(row_loss) * LOSS_SCALE, row_loss)
        loss_total, pullback, row_loss = jax.vjp(loss_of, online, observed.astype(jnp.float32), has_aux=True)
        param_grads, input_grad = pullback(jnp.ones_like(loss_total))
        summed = tuple((acc_val + new_val for acc_val, new_val in zip(summed, param_grads)))
        return (summed, (input_grad.astype(jnp.bfloat16), row_loss))
    initial = tuple((jnp.zeros_like(tensor) for tensor in online))
    param_grads, (input_grads, row_losses) = lax.scan(shard_step, initial, scan_items)
    param_grads = tuple((gradient / LOSS_SCALE for gradient in param_grads))
    frame_grad = input_grads.reshape(TRANS, FRAMES, SIDE, SIDE)
    owner_rows = owner_shard.reshape(shards, ROWS)
    shard_ids = jnp.arange(shards, dtype=jnp.int32)
    owner_hot = (owner_rows[:, :, None] == shard_ids[None, None, :]).astype(jnp.int32)
    slot_ids = (lax.optimization_barrier(jnp.sum(jnp.cumsum(owner_hot, axis=1) * owner_hot, axis=2)) - 1).astype(jnp.int32)
    senders = jnp.broadcast_to(shard_ids[:, None], owner_rows.shape)
    priorities = jnp.zeros((shards, shards, CAP), jnp.float32).at[owner_rows, senders, slot_ids].set(row_losses)
    return (param_grads[0], param_grads[1], param_grads[2], param_grads[3], param_grads[4], param_grads[5], param_grads[6], param_grads[7], param_grads[8], param_grads[9], frame_grad, priorities)
```

```python
import functools

import jax
import jax.numpy as jnp
from jax import lax
from jax.experimental import pallas as pl
from jax.experimental.pallas import tpu as pltpu
from jax.sharding import PartitionSpec as P

ACT = 18
ATOMS = 51
LOGITS = ACT * ATOMS
LOSS_SCALE = 256
LANES = 256
BF = jnp.bfloat16
F32 = jnp.float32
VMEM_BIG = 60 << 20


def call(kernel, out, ins, outs, grid=None, scratch=(), flops=0, nbytes=0):
    return pl.pallas_call(
        kernel,
        out_shape=out,
        grid=() if grid is None else grid,
        in_specs=ins,
        out_specs=outs,
        scratch_shapes=list(scratch),
        compiler_params=pltpu.CompilerParams(vmem_limit_bytes=VMEM_BIG),
        cost_estimate=pl.CostEstimate(flops=flops, bytes_accessed=nbytes, transcendentals=0),
    )


def whole(shape):
    return pl.BlockSpec(shape, lambda *_: (0,) * len(shape))


def sds(shape, dtype):
    return jax.ShapeDtypeStruct(shape, dtype)


def dot(left, right):
    return jnp.dot(left, right, preferred_element_type=F32)


def dot_nt(left, right):
    return lax.dot_general(left, right, (((1,), (1,)), ((), ())), preferred_element_type=F32)


def act_slope(half):
    tan = jnp.tanh(half)
    up = 1.0 + tan
    act = half * up
    return act, up + act * (1.0 - tan)


def bands_kernel(k1t, b1c, k2t, k3t, b3c, k2n, k3n, k1h, t1, t2, t3, t3b, t2b, t1b, w1, w2, w3, w3b, w2b, w1b):
    for ref in (w1, w2, w3, w3b, w2b, w1b):
        ref[...] = jnp.zeros_like(ref)
    for jj in range(10):
        for dy in range(8):
            w1[32 * jj : 32 * jj + 32, 176 * dy + 16 * jj : 176 * dy + 16 * jj + 32] = k1t[:, 32 * dy : 32 * dy + 32]
        w1[32 * jj : 32 * jj + 32, 1408:1409] = b1c[...]
    for jj in range(3):
        for u in range(4):
            w2[64 * jj : 64 * jj + 64, 256 * u + 64 * jj : 256 * u + 64 * jj + 128] = k2t[:, 128 * u : 128 * u + 128]
    for j in range(7):
        for u in range(3):
            w3[64 * j : 64 * j + 64, 576 * u + 64 * j : 576 * u + 64 * j + 192] = k3t[:, 192 * u : 192 * u + 192]
            w3b[64 * j : 64 * j + 192, 448 * (2 - u) + 64 * j : 448 * (2 - u) + 64 * j + 64] = k3n[192 * u : 192 * u + 192, :]
        w3[64 * j : 64 * j + 64, 1728:1729] = b3c[...]
    for e in range(2):
        for t in range(2):
            u = 2 * t + e
            for j in range(6):
                lo = max(0, 2 * j - 2)
                hi = min(10, 2 * j + 2)
                v0 = lo - (2 * j - 2)
                w2b[320 * e + 32 * lo : 320 * e + 32 * hi, 384 * t + 64 * j : 384 * t + 64 * j + 64] = k2n[
                    128 * u + 32 * v0 : 128 * u + 32 * (v0 + hi - lo), :
                ]
    for dy in range(8):
        t, row = divmod(dy, 4)
        for j in range(8):
            lo = max(0, 4 * j - 4)
            hi = min(28, 4 * j + 4)
            d0 = lo - (4 * j - 4)
            w1b[56 * row + 2 * lo : 56 * row + 2 * hi, 256 * t + 32 * j : 256 * t + 32 * j + 32] = k1h[
                dy, 2 * d0 : 2 * (d0 + hi - lo), :
            ]
    t1[...] = (0.5 * w1[...]).astype(BF)
    t2[...] = (0.5 * w2[...]).astype(BF)
    t3[...] = (0.5 * w3[...]).astype(BF)
    t3b[...] = (0.5 * w3b[...]).astype(BF)
    t2b[...] = (0.5 * w2b[...]).astype(BF)
    t1b[...] = w1b[...].astype(BF)


def bands(k1, b1, k2, k3, b3, k1_half):
    f = lambda a: a.astype(F32)
    ins = (
        f(k1).transpose(3, 0, 1, 2).reshape(32, 256),
        f(b1)[:, None],
        f(k2).transpose(3, 0, 1, 2).reshape(64, 512),
        f(k3).transpose(3, 0, 1, 2).reshape(64, 576),
        f(b3)[:, None],
        f(k2).reshape(512, 64),
        f(k3).reshape(576, 64),
        f(k1_half).reshape(8, 16, 32),
    )
    shapes = ((320, 1424), (192, 1024), (448, 1744), (576, 1344), (640, 768), (224, 512))
    return call(
        bands_kernel,
        tuple(sds(s, BF) for s in shapes),
        [whole(a.shape) for a in ins],
        [whole(s) for s in shapes],
        scratch=[pltpu.VMEM(s, F32) for s in shapes],
        nbytes=6_000_000,
    )(*ins)


def conv1_kernel(rows, x_ref, t1_ref, ones_ref, a_ref, s_ref, xt_ref, cells):
    c = pl.program_id(0)
    slot = lax.rem(c, 2)

    @pl.when(c == 0)
    def _():
        cells[...] = jnp.zeros_like(cells)

    for dy in range(4):
        flat = x_ref[dy].reshape(336, rows)
        cells[slot, dy, :, :rows] = flat
        xt_ref[dy, :, :] = cells[slot, dy]

    @pl.when(c > 0)
    def _():
        for g in range(2):
            window = pl.ds(160 * g, 176)
            parts = [cells[1 - slot, dy, window, :] for dy in range(4)]
            parts += [cells[slot, dy, window, :] for dy in range(4)]
            half = dot(t1_ref[...], jnp.concatenate(parts + [ones_ref[...]], axis=0))
            act, slope = act_slope(half)
            a_ref[0, 320 * g : 320 * g + 320, :] = act.astype(BF)
            s_ref[0, 320 * g : 320 * g + 320, :] = slope.astype(BF)


def conv1(xv, t1, ones):
    rows = xv.shape[3]

    def out_map(c):
        i = jnp.maximum(c - 1, 0)
        return (lax.rem(i, 2), 0, i // 2)

    out = pl.BlockSpec((1, 640, LANES), out_map)
    return call(
        functools.partial(conv1_kernel, rows),
        (sds((2, 640, 10 * LANES), BF), sds((2, 640, 10 * LANES), BF), sds((4, 336, 21 * LANES), BF)),
        [pl.BlockSpec((4, 84, 4, rows), lambda c: (c, 0, 0, 0)), whole((320, 1424)), whole((16, LANES))],
        [out, out, pl.BlockSpec((4, 336, LANES), lambda c: (0, 0, c))],
        grid=(21,),
        scratch=[pltpu.VMEM((2, 4, 336, LANES), BF)],
        flops=2 * 40 * 320 * 1424 * LANES,
        nbytes=42_000_000,
    )(xv, t1, ones)


def conv2_kernel(r0_ref, r1_ref, t2_ref, b2_ref, a_ref, s_ref):
    for g in range(3):
        window = pl.ds(192 * g, 256)
        parts = [r0_ref[0, window, :], r0_ref[1, window, :], r1_ref[0, window, :], r1_ref[1, window, :]]
        half = dot(t2_ref[...], jnp.concatenate(parts, axis=0)) + b2_ref[...]
        act, slope = act_slope(half)
        a_ref[192 * g : 192 * g + 192, :] = act.astype(BF)
        s_ref[192 * g : 192 * g + 192, :] = slope.astype(BF)


def conv2(a1, t2, b2):
    out = pl.BlockSpec((576, LANES), lambda i: (0, i))
    return call(
        conv2_kernel,
        (sds((576, 9 * LANES), BF), sds((576, 9 * LANES), BF)),
        [
            pl.BlockSpec((2, 640, LANES), lambda i: (0, 0, i)),
            pl.BlockSpec((2, 640, LANES), lambda i: (0, 0, i + 1)),
            whole((192, 1024)),
            whole((192, 1)),
        ],
        [out, out],
        grid=(9,),
        flops=2 * 27 * 192 * 1024 * LANES,
        nbytes=18_000_000,
    )(a1, a1, t2, b2)


def conv3_kernel(r0_ref, r1_ref, r2_ref, t3_ref, ones_ref, a_ref, s_ref):
    half = dot(t3_ref[...], jnp.concatenate([r0_ref[...], r1_ref[...], r2_ref[...], ones_ref[...]], axis=0))
    act, slope = act_slope(half)
    a_ref[...] = act.astype(BF)
    s_ref[...] = slope.astype(BF)


def conv3(a2, t3, ones):
    out = pl.BlockSpec((448, LANES), lambda i: (i, 0))
    return call(
        conv3_kernel,
        (sds((3136, LANES), BF), sds((3136, LANES), BF)),
        [pl.BlockSpec((576, LANES), lambda i, u=u: (0, i + u)) for u in range(3)]
        + [whole((448, 1744)), whole((16, LANES))],
        [out, out],
        grid=(7,),
        flops=2 * 7 * 448 * 1744 * LANES,
        nbytes=8_000_000,
    )(a2, a2, a2, t3, ones)


def head_kernel(rows, pd_ref, bd_ref, wh_ref, bh_ref, sel_ref, act_ref, slope_ref, lp_ref, cho_ref, lg_ref):
    act, slope = act_slope((pd_ref[...] + bd_ref[...]) * 0.5)
    act_ref[...] = act.astype(BF)
    slope_ref[...] = slope.astype(BF)
    lg_ref[...] = dot(wh_ref[...], act_ref[...]) + bh_ref[...]
    sel = sel_ref[...]
    pick = jnp.zeros((ATOMS, rows), F32)
    for a in range(ACT):
        pick = jnp.where(sel == a, lg_ref[ATOMS * a : ATOMS * a + ATOMS, :rows], pick)
    shifted = pick - jnp.max(pick, axis=0, keepdims=True)
    grown = jnp.exp(shifted)
    total = jnp.sum(grown, axis=0, keepdims=True)
    cho_ref[...] = (grown / total).astype(BF)
    lp_ref[...] = shifted - jnp.log(total)


def head(pd, bd, wht, bh, sel):
    rows = sel.shape[1]
    ins = (pd, bd, wht, bh, sel)
    outs = (((512, LANES), BF), ((512, LANES), BF), ((ATOMS, rows), F32), ((ATOMS, rows), BF))
    return call(
        functools.partial(head_kernel, rows),
        tuple(sds(*o) for o in outs),
        [whole(a.shape) for a in ins],
        [whole(o[0]) for o in outs],
        scratch=[pltpu.VMEM((LOGITS, LANES), F32)],
        flops=2 * LOGITS * 512 * LANES,
        nbytes=2_000_000,
    )(*ins)


def loss_kernel(rows, cho_ref, done_ref, low_ref, frac_ref, lp_ref, taken_ref, loss_ref, rh_ref, hb_ref, d_ref):
    atoms = lax.broadcasted_iota(jnp.int32, (ATOMS, rows), 0)
    done = done_ref[...].astype(F32)
    mass = (1.0 - done) * cho_ref[...].astype(F32) + done * (atoms == 0).astype(F32)
    frac = frac_ref[...]
    stay = mass * (1.0 - frac)
    move = mass * frac
    low = low_ref[...]
    proj = jnp.zeros((ATOMS, rows), F32)
    for i in range(ATOMS):
        gap = atoms - low[i : i + 1, :]
        proj = proj + jnp.where(gap == 0, stay[i : i + 1, :], jnp.where(gap == 1, move[i : i + 1, :], 0.0))
    lp = lp_ref[...]
    loss_ref[...] = -jnp.sum(proj * lp, axis=0, keepdims=True)
    diff = (jnp.sum(proj, axis=0, keepdims=True) * jnp.exp(lp) - proj) * LOSS_SCALE
    taken = taken_ref[...]
    for a in range(ACT):
        d_ref[ATOMS * a : ATOMS * a + ATOMS, :] = jnp.where(taken == a, diff, 0.0)
    rh_ref[...] = jnp.zeros_like(rh_ref)
    rh_ref[:, :rows] = d_ref[...].astype(BF)
    hb_ref[...] = jnp.sum(d_ref[...], axis=1, keepdims=True) * (1.0 / LOSS_SCALE)


def loss(cho, done, low, frac, lp, taken):
    rows = taken.shape[1]
    ins = (cho, done, low, frac, lp, taken)
    outs = (((1, rows), F32), ((LOGITS, LANES), BF), ((LOGITS, 1), F32))
    return call(
        functools.partial(loss_kernel, rows),
        tuple(sds(*o) for o in outs),
        [whole(a.shape) for a in ins],
        [whole(o[0]) for o in outs],
        scratch=[pltpu.VMEM((LOGITS, rows), F32)],
        nbytes=1_000_000,
    )(*ins)


def dflat_kernel(w_ref, rd_ref, s_ref, r_ref, b_ref):
    @pl.when(pl.program_id(0) == 0)
    def _():
        b_ref[...] = jnp.zeros_like(b_ref)

    diff = dot(w_ref[...], rd_ref[...]) * (0.5 * s_ref[...].astype(F32))
    r_ref[...] = diff.astype(BF)
    b_ref[...] += jnp.sum(diff.reshape(7, 64, LANES), axis=0)


def dflat(wd, rd, s3):
    block = pl.BlockSpec((448, LANES), lambda i: (i, 0))
    return call(
        dflat_kernel,
        (sds((3136, LANES), BF), sds((64, LANES), F32)),
        [pl.BlockSpec((448, 512), lambda i: (i, 0)), whole((512, LANES)), block],
        [block, whole((64, LANES))],
        grid=(7,),
        flops=2 * 3136 * 512 * LANES,
        nbytes=6_500_000,
    )(wd, rd, s3)


def dconv3_kernel(r3_ref, t_ref, s_ref, r_ref, b_ref, pad):
    p = pl.program_id(0)

    @pl.when(p == 0)
    def _():
        b_ref[...] = jnp.zeros_like(b_ref)
        pad[:896, :] = jnp.zeros((896, LANES), BF)
        pad[896:4032, :] = r3_ref[...]
        pad[4032:, :] = jnp.zeros((896, LANES), BF)

    window = pl.ds(pl.multiple_of(448 * p, 64), 1344)
    diff = dot(t_ref[...], pad[window, :]) * s_ref[...].astype(F32)
    r_ref[...] = diff.astype(BF)
    b_ref[...] += jnp.sum(diff.reshape(9, 64, LANES), axis=0)


def dconv3(r3, t3b, s2):
    block = pl.BlockSpec((576, LANES), lambda p: (0, p))
    return call(
        dconv3_kernel,
        (sds((576, 9 * LANES), BF), sds((64, LANES), F32)),
        [whole((3136, LANES)), whole((576, 1344)), block],
        [block, whole((64, LANES))],
        grid=(9,),
        scratch=[pltpu.VMEM((4928, LANES), BF)],
        flops=2 * 9 * 576 * 1344 * LANES,
        nbytes=9_000_000,
    )(r3, t3b, s2)


def dconv2_kernel(cur_ref, prev_ref, t_ref, s_ref, r_ref, b_ref):
    m = pl.program_id(0)

    @pl.when(m == 0)
    def _():
        b_ref[...] = jnp.zeros_like(b_ref)

    none = jnp.zeros((64, LANES), BF)
    cur = jnp.where(m < 9, cur_ref[...], jnp.zeros((576, LANES), BF))
    prev = jnp.where(m > 0, prev_ref[...], jnp.zeros((576, LANES), BF))
    for h in range(2):
        if h == 0:
            parts = [none, cur[:320], none, prev[:320]]
        else:
            parts = [cur[256:], none, prev[256:], none]
        diff = dot(t_ref[...], jnp.concatenate(parts, axis=0))
        for e in range(2):
            rows = slice(320 * h, 320 * h + 320)
            part = diff[320 * e : 320 * e + 320] * s_ref[e, rows, :].astype(F32)
            r_ref[e, rows, :] = part.astype(BF)
            b_ref[...] += jnp.sum(part.reshape(10, 32, LANES), axis=0)


def dconv2(r2, t2b, s1):
    block = pl.BlockSpec((2, 640, LANES), lambda m: (0, 0, m))
    return call(
        dconv2_kernel,
        (sds((2, 640, 10 * LANES), BF), sds((32, LANES), F32)),
        [
            pl.BlockSpec((576, LANES), lambda m: (0, jnp.minimum(m, 8))),
            pl.BlockSpec((576, LANES), lambda m: (0, jnp.maximum(m - 1, 0))),
            whole((640, 768)),
            block,
        ],
        [block, whole((32, LANES))],
        grid=(10,),
        flops=2 * 20 * 640 * 768 * LANES,
        nbytes=16_000_000,
    )(r2, r2, t2b, s1)


def dframes_kernel(rows, flag_ref, own0_ref, own1_ref, got0_ref, got1_ref, t_ref, o_ref):
    c = pl.program_id(0)
    own = flag_ref[0] == 1
    zero = jnp.zeros((640, LANES), BF)
    r0 = jnp.where(c < 20, jnp.where(own, own0_ref[0], got0_ref[0]), zero)
    r1 = jnp.where(c > 0, jnp.where(own, own1_ref[0], got1_ref[0]), zero)
    none = jnp.zeros((32, LANES), BF)
    for g in range(3):
        if g == 0:
            parts = [none, r0[:224], none, r1[:224]]
        elif g == 1:
            parts = [r0[192:448], r1[192:448]]
        else:
            parts = [r0[416:], none, r1[416:], none]
        out = dot(t_ref[...], jnp.concatenate(parts, axis=0)).astype(BF)
        for dy in range(4):
            o_ref[dy, 28 * g : 28 * g + 28, :, :] = out[56 * dy : 56 * dy + 56, :rows].reshape(28, 2, rows)


def dframes(flag, own, got, t1b, rows):
    def place(i):
        return (lax.rem(i, 2), 0, i // 2)

    now = pl.BlockSpec((1, 640, LANES), lambda c, *_: place(jnp.minimum(c, 19)))
    before = pl.BlockSpec((1, 640, LANES), lambda c, *_: place(jnp.maximum(c - 1, 0)))
    return pl.pallas_call(
        functools.partial(dframes_kernel, rows),
        out_shape=sds((84, 84, 2, rows), BF),
        grid_spec=pltpu.PrefetchScalarGridSpec(
            num_scalar_prefetch=1,
            grid=(21,),
            in_specs=[now, before, now, before, pl.BlockSpec((224, 512), lambda c, *_: (0, 0))],
            out_specs=pl.BlockSpec((4, 84, 2, rows), lambda c, *_: (c, 0, 0, 0)),
        ),
        compiler_params=pltpu.CompilerParams(vmem_limit_bytes=VMEM_BIG),
        cost_estimate=pl.CostEstimate(flops=2 * 63 * 224 * 512 * LANES, bytes_accessed=33_000_000, transcendentals=0),
    )(flag, own, own, got, got, t1b)


def wdense_kernel(a_ref, rd_ref, g_ref):
    grad = (dot_nt(a_ref[...], rd_ref[...]) * (1.0 / LOSS_SCALE)).astype(BF)
    for half in range(2):
        for lane in range(2):
            g_ref[0, lane, half] = grad[:, 256 * half + 128 * lane : 256 * half + 128 * lane + 128]


def wdense(a, rd, block):
    return call(
        wdense_kernel,
        sds((8, 2, 2, block, 128), BF),
        [pl.BlockSpec((block, LANES), lambda i: (i, 0)), whole((512, LANES))],
        pl.BlockSpec((1, 2, 2, block, 128), lambda i: (i, 0, 0, 0, 0)),
        grid=(8,),
        flops=2 * 8 * block * 512 * LANES,
        nbytes=5_000_000,
    )(a, rd)


def wconv3_kernel(a_ref, r_ref, g_ref):
    acc = jnp.zeros((576, 64), F32)
    for j in range(7):
        left = jnp.concatenate(
            [a_ref[64 * j : 64 * j + 192, LANES * u : LANES * (u + 7)] for u in range(3)], axis=0
        )
        right = jnp.concatenate([r_ref[448 * i + 64 * j : 448 * i + 64 * j + 64, :] for i in range(7)], axis=1)
        acc = acc + dot_nt(left, right)
    g_ref[...] = acc * (1.0 / LOSS_SCALE)


def wconv3(a2, r3):
    return call(
        wconv3_kernel,
        sds((576, 64), F32),
        [whole(a2.shape), whole(r3.shape)],
        whole((576, 64)),
        flops=2 * 49 * 576 * 64 * LANES,
        nbytes=4_500_000,
    )(a2, r3)


def wconv2_kernel(a_ref, r_ref, g_ref):
    g_ref[...] = jnp.zeros_like(g_ref)

    def body(j, _):
        window = pl.ds(pl.multiple_of(64 * j, 64), 128)
        left = jnp.concatenate(
            [a_ref[e, window, LANES * t : LANES * (t + 9)] for t in range(2) for e in range(2)], axis=0
        )
        g_ref[...] += dot_nt(left, r_ref[pl.ds(pl.multiple_of(64 * j, 64), 64), :])
        return 0

    lax.fori_loop(0, 9, body, 0)
    g_ref[...] = g_ref[...] * (1.0 / LOSS_SCALE)


def wconv2(a1, r2):
    return call(
        wconv2_kernel,
        sds((512, 64), F32),
        [whole(a1.shape), whole(r2.shape)],
        whole((512, 64)),
        flops=2 * 81 * 512 * 64 * LANES,
        nbytes=9_500_000,
    )(a1, r2)


def wconv1_kernel(x_ref, n_ref, r_ref, g_ref, acc):
    step = pl.program_id(0)

    @pl.when(step == 0)
    def _():
        acc[...] = jnp.zeros_like(acc)

    def column(dy, rows, c):
        if c < 4:
            return x_ref[dy, rows, LANES * c : LANES * (c + 1)]
        return n_ref[dy, rows, :]

    total = acc[...]
    for g in range(5):
        rows = slice(64 * g, 64 * g + 80)
        left = jnp.concatenate(
            [
                jnp.concatenate([column(dy, rows, ii + t) for ii in range(4)], axis=1)
                for t in range(2)
                for dy in range(4)
            ],
            axis=0,
        )
        right = jnp.concatenate(
            [r_ref[ii % 2, 128 * g : 128 * g + 128, LANES * (ii // 2) : LANES * (ii // 2 + 1)] for ii in range(4)],
            axis=1,
        )
        total = total + dot_nt(left, right)
    acc[...] = total

    @pl.when(step == 4)
    def _():
        for dy in range(8):
            part = jnp.zeros((32, 32), F32)
            for jj in range(4):
                part = part + acc[80 * dy + 16 * jj : 80 * dy + 16 * jj + 32, 32 * jj : 32 * jj + 32]
            g_ref[32 * dy : 32 * dy + 32, :] = part * (1.0 / LOSS_SCALE)


def wconv1(xt, r1):
    return call(
        wconv1_kernel,
        sds((256, 32), F32),
        [
            pl.BlockSpec((4, 336, 4 * LANES), lambda s: (0, 0, s)),
            pl.BlockSpec((4, 336, LANES), lambda s: (0, 0, 4 * s + 4)),
            pl.BlockSpec((2, 640, 2 * LANES), lambda s: (0, 0, s)),
        ],
        whole((256, 32)),
        grid=(5,),
        scratch=[pltpu.VMEM((640, 128), F32)],
        flops=2 * 100 * 640 * 128 * LANES,
        nbytes=21_000_000,
    )(xt, xt, r1)


def to_chunks(grad, devices):
    split = devices // 16
    n = grad.shape[3] // split
    parts = grad.reshape(8, 2, 2, split, n, 128).transpose(0, 3, 1, 2, 4, 5)
    return parts.reshape(devices, 2, n, 128)


def from_chunks(parts):
    devices, n = parts.shape[0], parts.shape[1]
    return parts.reshape(devices // 2, 2, n, 128).transpose(0, 2, 1, 3).reshape(devices // 2 * n, 256)


def hand(value):
    return lax.ppermute(value, "pair", [(0, 1)])


def local(
    frames,
    kernel_first,
    bias_first,
    kernel_second,
    bias_second,
    kernel_third,
    bias_third,
    dense_weight,
    dense_bias,
    head_weight,
    head_bias,
    taken_actions,
    greedy_actions,
    done_flags,
    bin_lower,
    bin_fraction,
    owner_shard,
):
    online = lax.axis_index("pair") == 0
    shard_count = lax.axis_size("batch")
    rows = frames.shape[1]
    xv = frames[0].transpose(2, 3, 1, 0)
    k1, k2, k3 = kernel_first[0], kernel_second[0], kernel_third[0]
    k1_half = jnp.where(online, k1[:, :, :2], hand(k1[:, :, 2:]))
    ones = jnp.zeros((16, LANES), BF).at[0].set(1)
    t1, t2, t3, t3b, t2b, t1b = bands(k1, bias_first[0], k2, k3, bias_third[0], k1_half)

    a1, s1, xt = conv1(xv, t1, ones)
    b2 = jnp.tile(bias_second[0].astype(F32) * 0.5, 3)[:, None]
    a2, s2 = conv2(a1, t2, b2)
    a3, s3 = conv3(a2, t3, ones)
    wd = dense_weight[0]
    wht = head_weight[0].T
    pd = lax.dot_general(wd, a3, (((0,), (0,)), ((), ())), preferred_element_type=F32)
    taken = taken_actions[None, :]
    sel = jnp.where(online, taken, greedy_actions[None, :])
    h, sd, lp, cho = head(pd, dense_bias[0].astype(F32)[:, None], wht, head_bias[0].astype(F32)[:, None], sel)
    cho = lax.ppermute(cho, "pair", [(1, 0)])
    row_loss, rh, hb = loss(cho, done_flags[None, :], bin_lower.T, bin_fraction.T, lp, taken)

    diff_dense = lax.dot_general(wht, rh, (((0,), (0,)), ((), ())), preferred_element_type=F32)
    diff_dense = diff_dense * (0.5 * sd.astype(F32))
    rd = diff_dense.astype(BF)
    dense_bias_grad = jnp.sum(diff_dense, axis=1) * (1.0 / LOSS_SCALE)

    g_dense = wdense(a3, rd, 392)
    g_head = wdense(rh, h, 120)
    chunks = jnp.concatenate([to_chunks(g_dense, shard_count), to_chunks(g_head, shard_count)], axis=2)
    cut = g_dense.shape[3] * 16 // shard_count
    summed = lax.psum_scatter(chunks, "batch", scatter_dimension=0, tiled=False)
    mine = jnp.where(online, summed[0], hand(summed[1]))
    gathered = lax.all_gather(mine, "batch", axis=0, tiled=False)

    r3, b3g = dflat(wd, rd, s3)
    r2, b2g = dconv3(r3, t3b, s2)
    r1, b1g = dconv2(r2, t2b, s1)
    got = hand(r1)
    g3 = wconv3(a2, r3)
    g2 = wconv2(a1, r2)
    g1 = wconv1(xt, r1)
    scale = 1.0 / LOSS_SCALE
    small = (
        g1,
        jnp.sum(b1g, axis=1) * scale,
        g2,
        jnp.sum(b2g, axis=1) * scale,
        g3,
        jnp.sum(b3g, axis=1) * scale,
        dense_bias_grad,
        hb[:, 0],
    )
    small = lax.psum(small, "batch")
    small = [
        small[0].reshape(8, 8, 4, 32),
        small[1],
        small[2].reshape(4, 4, 32, 64),
        small[3],
        small[4].reshape(3, 3, 64, 64),
        small[5],
        small[6],
        small[7],
    ]
    dims = (0, 0, 0, 0, 3, 0, 0, 0)
    lower = [lax.slice_in_dim(v, 0, v.shape[d] // 2, axis=d) for v, d in zip(small, dims)]
    upper = [lax.slice_in_dim(v, v.shape[d] // 2, v.shape[d], axis=d) for v, d in zip(small, dims)]

    owner = owner_shard[:, 0]
    capacity = 2 * ((rows + shard_count - 1) // shard_count)
    earlier = jnp.arange(rows)[:, None] < jnp.arange(rows)[None, :]
    slot = jnp.sum(((owner[:, None] == owner[None, :]) & earlier).astype(jnp.int32), axis=0)
    owner_hot = (jnp.arange(shard_count)[:, None] == owner[None, :]).astype(F32)
    slot_hot = (slot[:, None] == jnp.arange(capacity)[None, :]).astype(F32)
    outgoing = jnp.dot(owner_hot * row_loss, slot_hot, precision=lax.Precision.HIGHEST)
    incoming = lax.all_to_all(outgoing, "batch", split_axis=0, concat_axis=0, tiled=True)
    upper.append(incoming[:, capacity // 2 :])
    lower.append(incoming[:, : capacity // 2])

    flat = hand(jnp.concatenate([v.astype(BF).reshape(-1) for v in upper]))
    finals = []
    start = 0
    for low_part in lower:
        size = low_part.size
        far = flat[start : start + size].reshape(low_part.shape).astype(F32)
        finals.append(jnp.where(online, low_part, far))
        start += size

    flag = online.astype(jnp.int32)[None]
    frame_out = dframes(flag, r1, got, t1b, rows).transpose(3, 2, 0, 1)
    dense_out = from_chunks(gathered[:, :cut]).astype(F32)
    head_out = from_chunks(gathered[:, cut:])[:LOGITS].astype(F32).T
    return (
        finals[0],
        finals[1],
        finals[2],
        finals[3],
        finals[4],
        finals[5],
        dense_out,
        finals[6],
        head_out,
        finals[7],
        frame_out,
        finals[8][None],
    )


def solution(mesh):
    return jax.shard_map(
        local,
        mesh=mesh,
        in_specs=(
            P("pair", "batch", None, None, None),
            P("pair", None, None, None, None),
            P("pair", None),
            P("pair", None, None, None, None),
            P("pair", None),
            P("pair", None, None, None, None),
            P("pair", None),
            P("pair", None, None),
            P("pair", None),
            P("pair", None, None),
            P("pair", None),
            P("batch"),
            P("batch"),
            P("batch"),
            P("batch", None),
            P("batch", None),
            P("batch", None),
        ),
        out_specs=(
            P("pair", None, None, None),
            P("pair"),
            P("pair", None, None, None),
            P("pair"),
            P(None, None, None, "pair"),
            P("pair"),
            P(None, "pair"),
            P("pair"),
            P("pair", None),
            P("pair"),
            P("batch", "pair", None, None),
            P("batch", None, "pair"),
        ),
        check_vma=False,
    )
```

```python
import functools

import jax
import jax.numpy as jnp
from jax import lax
from jax.experimental import pallas as pl
from jax.experimental.pallas import tpu as pltpu
from jax.sharding import PartitionSpec as P

ACT = 18
ATOMS = 51
LOGITS = ACT * ATOMS
LOSS_SCALE = 256
LANES = 256
BF = jnp.bfloat16
F32 = jnp.float32
VMEM_BIG = 60 << 20
FAR = 6
EARLY = 4
NEAR = ((6, 2), (8, 2))


def cost(us):
    return pl.CostEstimate(flops=int(us * 0.5e9), bytes_accessed=0, transcendentals=0)


def call(kernel, out, ins, outs, us, grid=None, scratch=()):
    return pl.pallas_call(
        kernel,
        out_shape=out,
        grid=() if grid is None else grid,
        in_specs=ins,
        out_specs=outs,
        scratch_shapes=list(scratch),
        compiler_params=pltpu.CompilerParams(vmem_limit_bytes=VMEM_BIG),
        cost_estimate=cost(us),
    )


def whole(shape):
    return pl.BlockSpec(shape, lambda *_: (0,) * len(shape))


def sds(shape, dtype):
    return jax.ShapeDtypeStruct(shape, dtype)


def dot(left, right):
    return jnp.dot(left, right, preferred_element_type=F32)


def dot_nt(left, right):
    return lax.dot_general(left, right, (((1,), (1,)), ((), ())), preferred_element_type=F32)


def act_slope(half):
    tan = jnp.tanh(half)
    up = 1.0 + tan
    act = half * up
    return act, up + act * (1.0 - tan)


def second_bands(k2n, w2b):
    for e in range(2):
        for t in range(2):
            u = 2 * t + e
            for j in range(6):
                lo = max(0, 2 * j - 2)
                hi = min(10, 2 * j + 2)
                v0 = lo - (2 * j - 2)
                w2b[320 * e + 32 * lo : 320 * e + 32 * hi, 384 * t + 64 * j : 384 * t + 64 * j + 64] = k2n[
                    128 * u + 32 * v0 : 128 * u + 32 * (v0 + hi - lo), :
                ]


def bands_kernel(k1, b1, k2, b2, k3, b3, t1, t2, t3, t3b, t2b, b2c, w1, w2, w3, w3b, w2b):
    for ref in (w1, w2, w3, w3b, w2b):
        ref[...] = jnp.zeros_like(ref)

    def turned(kernel, bias):
        flat = kernel[...].astype(F32)
        flat = flat.reshape(-1, flat.shape[-1])
        bias = jnp.broadcast_to(bias[...].astype(F32), (8, flat.shape[1]))
        return flat, flat.T, bias.T[:, :1]

    _, k1t, b1c = turned(k1, b1)
    k2n, k2t, b2t = turned(k2, b2)
    k3n, k3t, b3c = turned(k3, b3)
    for jj in range(10):
        for dy in range(8):
            w1[32 * jj : 32 * jj + 32, 176 * dy + 16 * jj : 176 * dy + 16 * jj + 32] = k1t[:, 32 * dy : 32 * dy + 32]
        w1[32 * jj : 32 * jj + 32, 1408:1409] = b1c
    for jj in range(3):
        for u in range(4):
            w2[64 * jj : 64 * jj + 64, 256 * u + 64 * jj : 256 * u + 64 * jj + 128] = k2t[:, 128 * u : 128 * u + 128]
        b2c[64 * jj : 64 * jj + 64, :] = 0.5 * b2t
    for j in range(7):
        for u in range(3):
            w3[64 * j : 64 * j + 64, 576 * u + 64 * j : 576 * u + 64 * j + 192] = k3t[:, 192 * u : 192 * u + 192]
            w3b[64 * j : 64 * j + 192, 448 * (2 - u) + 64 * j : 448 * (2 - u) + 64 * j + 64] = k3n[192 * u : 192 * u + 192, :]
        w3[64 * j : 64 * j + 64, 1728:1729] = b3c
    second_bands(k2n, w2b)
    t1[...] = (0.5 * w1[...]).astype(BF)
    t2[...] = (0.5 * w2[...]).astype(BF)
    t3[...] = (0.5 * w3[...]).astype(BF)
    t3b[...] = (0.5 * w3b[...]).astype(BF)
    t2b[...] = (0.5 * w2b[...]).astype(BF)


def bands(*ins):
    shapes = ((320, 1424), (192, 1024), (448, 1744), (576, 1344), (640, 768))
    return call(
        bands_kernel,
        tuple(sds(s, BF) for s in shapes) + (sds((192, 1), F32),),
        [whole(a.shape) for a in ins],
        [whole(s) for s in shapes] + [whole((192, 1))],
        scratch=[pltpu.VMEM(s, F32) for s in shapes],
        us=5,
    )(*ins)


def band_frames_kernel(flag_ref, k1, k1_got, k2, k2_got, t1b, t2b, w1b, w2b):
    own = flag_ref[0] == 1
    w1b[...] = jnp.zeros_like(w1b)
    w2b[...] = jnp.zeros_like(w2b)
    half = jnp.where(own, k1[:, :, :2, :].astype(F32), k1_got[...].astype(F32)).reshape(8, 16, 32)
    for dy in range(8):
        t, row = divmod(dy, 4)
        for j in range(8):
            lo = max(0, 4 * j - 4)
            hi = min(28, 4 * j + 4)
            d0 = lo - (4 * j - 4)
            w1b[56 * row + 2 * lo : 56 * row + 2 * hi, 256 * t + 32 * j : 256 * t + 32 * j + 32] = half[
                dy, 2 * d0 : 2 * (d0 + hi - lo), :
            ]
    second_bands(jnp.where(own, k2[...].astype(F32), k2_got[...].astype(F32)).reshape(512, 64), w2b)
    t1b[...] = w1b[...].astype(BF)
    t2b[...] = (0.5 * w2b[...]).astype(BF)


def band_frames(flag, *ins):
    shapes = ((224, 512), (640, 768))
    return call(
        band_frames_kernel,
        tuple(sds(s, BF) for s in shapes),
        [pl.BlockSpec(memory_space=pltpu.SMEM)] + [whole(a.shape) for a in ins],
        [whole(s) for s in shapes],
        scratch=[pltpu.VMEM(s, F32) for s in shapes],
        us=3,
    )(flag, *ins)


def pack_rows(part, n):
    lane = lax.broadcasted_iota(jnp.int32, (n // 4, 128), 1)
    tail = [part[n // 4 * k : n // 4 * (k + 1), 128:] for k in range(4)]
    packed = [jnp.where(lane < 96, tail[k], pltpu.roll(tail[3], 96 - 32 * k, 1)) for k in range(3)]
    return jnp.concatenate([part[:, :128]] + packed, axis=0)


def unpack_rows(packed, n):
    lane = lax.broadcasted_iota(jnp.int32, (n // 4, 128), 1)
    tail = [packed[n + n // 4 * k : n + n // 4 * (k + 1)] for k in range(3)]
    last = pltpu.roll(tail[0], 32, 1)
    last = jnp.where(lane < 32, last, jnp.where(lane < 64, pltpu.roll(tail[1], 64, 1), pltpu.roll(tail[2], 96, 1)))
    return jnp.concatenate([packed[:n], jnp.concatenate(tail + [last], axis=0)], axis=1)


def conv1_kernel(rows, start, packs, x_ref, t1_ref, ones_ref, *rest):
    cells = rest[-1]
    a_ref, s_ref, xt_ref, p_ref = rest[-5:-1]
    c = pl.program_id(0) + start
    slot = lax.rem(c, 2)

    @pl.when(c == start)
    def _():
        cells[...] = jnp.zeros_like(cells)

    for dy in range(4):
        flat = x_ref[dy].reshape(336, rows)
        cells[slot, dy, :, :rows] = flat
        xt_ref[dy, :, :] = cells[slot, dy]

    @pl.when(c > start)
    def _():
        slopes = []
        for g in range(2):
            window = pl.ds(160 * g, 176)
            parts = [cells[1 - slot, dy, window, :] for dy in range(4)]
            parts += [cells[slot, dy, window, :] for dy in range(4)]
            half = dot(t1_ref[...], jnp.concatenate(parts + [ones_ref[...]], axis=0))
            act, slope = act_slope(half)
            a_ref[0, 320 * g : 320 * g + 320, :] = act.astype(BF)
            s_ref[0, 320 * g : 320 * g + 320, :] = slope.astype(BF)
            slopes.append(slope)
        @pl.when(c <= packs)
        def _():
            p_ref[0, 0] = pack_rows(jnp.concatenate(slopes, axis=0), 640).astype(BF)


def conv1(xv, t1, ones, start, stop, before):
    rows = xv.shape[3]
    packs = min(stop, 2 * FAR)

    def place(c):
        i = jnp.maximum(c - 1 + start, start)
        return (lax.rem(i, 2), i // 2)

    out = pl.BlockSpec((1, 640, LANES), lambda c: (place(c)[0], 0, place(c)[1]))
    outs = [out, out, pl.BlockSpec((4, 336, LANES), lambda c: (0, 0, c + start))]
    shapes = [sds((2, 640, 10 * LANES), BF), sds((2, 640, 10 * LANES), BF), sds((4, 336, 21 * LANES), BF)]
    def packed_place(c):
        i = jnp.clip(c - 1, 0, packs - start - 1)
        return (i // 2, lax.rem(i, 2), 0, 0)

    outs.append(pl.BlockSpec((1, 1, 1120, 128), packed_place))
    shapes.append(sds(((packs - start) // 2, 2, 1120, 128), BF))
    return pl.pallas_call(
        functools.partial(conv1_kernel, rows, start, packs),
        out_shape=tuple(shapes),
        grid=(stop - start + 1,),
        in_specs=[pl.BlockSpec((4, 84, 4, rows), lambda c: (c + start, 0, 0, 0)), whole((320, 1424)), whole((16, LANES))]
        + [pl.BlockSpec(memory_space=pl.ANY)] * len(before),
        out_specs=outs,
        scratch_shapes=[pltpu.VMEM((2, 4, 336, LANES), BF)],
        input_output_aliases={3 + n: n for n in range(len(before))},
        compiler_params=pltpu.CompilerParams(vmem_limit_bytes=VMEM_BIG),
        cost_estimate=cost(0.1 * (stop - start)),
    )(xv, t1, ones, *before)


def conv2_kernel(r0_ref, r1_ref, t2_ref, b2_ref, a_ref, s_ref):
    for g in range(3):
        window = pl.ds(192 * g, 256)
        parts = [r0_ref[0, window, :], r0_ref[1, window, :], r1_ref[0, window, :], r1_ref[1, window, :]]
        half = dot(t2_ref[...], jnp.concatenate(parts, axis=0)) + b2_ref[...]
        act, slope = act_slope(half)
        a_ref[192 * g : 192 * g + 192, :] = act.astype(BF)
        s_ref[192 * g : 192 * g + 192, :] = slope.astype(BF)


def conv2(a1, t2, b2):
    out = pl.BlockSpec((576, LANES), lambda i: (0, i))
    return call(
        conv2_kernel,
        (sds((576, 9 * LANES), BF), sds((576, 9 * LANES), BF)),
        [
            pl.BlockSpec((2, 640, LANES), lambda i: (0, 0, i)),
            pl.BlockSpec((2, 640, LANES), lambda i: (0, 0, i + 1)),
            whole((192, 1024)),
            whole((192, 1)),
        ],
        [out, out],
        grid=(9,),
        us=1,
    )(a1, a1, t2, b2)


def conv3_kernel(r0_ref, r1_ref, r2_ref, t3_ref, ones_ref, a_ref, s_ref):
    half = dot(t3_ref[...], jnp.concatenate([r0_ref[...], r1_ref[...], r2_ref[...], ones_ref[...]], axis=0))
    act, slope = act_slope(half)
    a_ref[...] = act.astype(BF)
    s_ref[...] = slope.astype(BF)


def conv3(a2, t3, ones):
    out = pl.BlockSpec((448, LANES), lambda i: (i, 0))
    return call(
        conv3_kernel,
        (sds((3136, LANES), BF), sds((3136, LANES), BF)),
        [pl.BlockSpec((576, LANES), lambda i, u=u: (0, i + u)) for u in range(3)]
        + [whole((448, 1744)), whole((16, LANES))],
        [out, out],
        grid=(7,),
        us=1,
    )(a2, a2, a2, t3, ones)


def head_kernel(rows, pd_ref, bd_ref, wh_ref, bh_ref, sel_ref, act_ref, slope_ref, lp_ref, cho_ref, lg_ref):
    bd = jnp.broadcast_to(bd_ref[...].astype(F32), (8, 512)).T[:, :1]
    bh = jnp.broadcast_to(bh_ref[...].astype(F32), (8, LOGITS)).T[:, :1]
    act, slope = act_slope((pd_ref[...] + bd) * 0.5)
    act_ref[...] = act.astype(BF)
    slope_ref[...] = slope.astype(BF)
    lg_ref[...] = dot(wh_ref[...], act_ref[...]) + bh
    sel = sel_ref[...]
    pick = jnp.zeros((ATOMS, rows), F32)
    for a in range(ACT):
        pick = jnp.where(sel == a, lg_ref[ATOMS * a : ATOMS * a + ATOMS, :rows], pick)
    shifted = pick - jnp.max(pick, axis=0, keepdims=True)
    grown = jnp.exp(shifted)
    total = jnp.sum(grown, axis=0, keepdims=True)
    cho_ref[...] = (grown / total).astype(BF)
    lp_ref[...] = shifted - jnp.log(total)


def head(pd, bd, wht, bh, sel):
    rows = sel.shape[1]
    ins = (pd, bd, wht, bh, sel)
    outs = (((512, LANES), BF), ((512, LANES), BF), ((ATOMS, rows), F32), ((ATOMS, rows), BF))
    return call(
        functools.partial(head_kernel, rows),
        tuple(sds(*o) for o in outs),
        [whole(a.shape) for a in ins],
        [whole(o[0]) for o in outs],
        scratch=[pltpu.VMEM((LOGITS, LANES), F32)],
        us=0.5,
    )(*ins)


def loss_kernel(rows, cho_ref, done_ref, low_ref, frac_ref, lp_ref, taken_ref, loss_ref, rh_ref, hb_ref, d_ref):
    atoms = lax.broadcasted_iota(jnp.int32, (ATOMS, rows), 0)
    done = done_ref[...].astype(F32)
    mass = (1.0 - done) * cho_ref[...].astype(F32) + done * (atoms == 0).astype(F32)
    frac = frac_ref[...]
    stay = mass * (1.0 - frac)
    move = mass * frac
    low = low_ref[...]
    proj = jnp.zeros((ATOMS, rows), F32)
    for i in range(ATOMS):
        gap = atoms - low[i : i + 1, :]
        proj = proj + jnp.where(gap == 0, stay[i : i + 1, :], jnp.where(gap == 1, move[i : i + 1, :], 0.0))
    lp = lp_ref[...]
    loss_ref[...] = -jnp.sum(proj * lp, axis=0, keepdims=True)
    diff = (jnp.sum(proj, axis=0, keepdims=True) * jnp.exp(lp) - proj) * LOSS_SCALE
    taken = taken_ref[...]
    for a in range(ACT):
        d_ref[ATOMS * a : ATOMS * a + ATOMS, :] = jnp.where(taken == a, diff, 0.0)
    rh_ref[...] = jnp.zeros_like(rh_ref)
    rh_ref[:, :rows] = d_ref[...].astype(BF)
    hb_ref[...] = jnp.sum(d_ref[...], axis=1, keepdims=True) * (1.0 / LOSS_SCALE)


def loss(cho, done, low, frac, lp, taken):
    rows = taken.shape[1]
    ins = (cho, done, low, frac, lp, taken)
    outs = (((1, rows), F32), ((LOGITS, LANES), BF), ((LOGITS, 1), F32))
    return call(
        functools.partial(loss_kernel, rows),
        tuple(sds(*o) for o in outs),
        [whole(a.shape) for a in ins],
        [whole(o[0]) for o in outs],
        scratch=[pltpu.VMEM((LOGITS, rows), F32)],
        us=0.5,
    )(*ins)


def dflat_kernel(w_ref, rd_ref, s_ref, r_ref, b_ref):
    @pl.when(pl.program_id(0) == 0)
    def _():
        b_ref[...] = jnp.zeros_like(b_ref)

    diff = dot(w_ref[...], rd_ref[...]) * (0.5 * s_ref[...].astype(F32))
    r_ref[...] = diff.astype(BF)
    b_ref[...] += jnp.sum(diff.reshape(7, 64, LANES), axis=0)


def dflat(wd, rd, s3):
    block = pl.BlockSpec((448, LANES), lambda i: (i, 0))
    return call(
        dflat_kernel,
        (sds((3136, LANES), BF), sds((64, LANES), F32)),
        [pl.BlockSpec((448, 512), lambda i: (i, 0)), whole((512, LANES)), block],
        [block, whole((64, LANES))],
        grid=(7,),
        us=2,
    )(wd, rd, s3)


def dconv3_kernel(r3_ref, t_ref, s_ref, r_ref, p_ref, b_ref, pad):
    p = pl.program_id(0)

    @pl.when(p == 0)
    def _():
        b_ref[...] = jnp.zeros_like(b_ref)
        pad[:896, :] = jnp.zeros((896, LANES), BF)
        pad[896:4032, :] = r3_ref[...]
        pad[4032:, :] = jnp.zeros((896, LANES), BF)

    window = pl.ds(pl.multiple_of(448 * p, 64), 1344)
    diff = dot(t_ref[...], pad[window, :]) * s_ref[...].astype(F32)
    r_ref[...] = diff.astype(BF)
    b_ref[...] += jnp.sum(diff.reshape(9, 64, LANES), axis=0)

    @pl.when(p < FAR)
    def _():
        p_ref[0] = pack_rows(diff, 576).astype(BF)


def dconv3(r3, t3b, s2):
    block = pl.BlockSpec((576, LANES), lambda p: (0, p))
    return call(
        dconv3_kernel,
        (sds((576, 9 * LANES), BF), sds((FAR, 1008, 128), BF), sds((64, LANES), F32)),
        [whole((3136, LANES)), whole((576, 1344)), block],
        [block, pl.BlockSpec((1, 1008, 128), lambda p: (jnp.minimum(p, FAR - 1), 0, 0)), whole((64, LANES))],
        grid=(9,),
        scratch=[pltpu.VMEM((4928, LANES), BF)],
        us=11,
    )(r3, t3b, s2)


def first_diffs(t, cur, prev):
    none = jnp.zeros((64, LANES), BF)
    halves = []
    for h in range(2):
        if h == 0:
            parts = [none, cur[:320], none, prev[:320]]
        else:
            parts = [cur[256:], none, prev[256:], none]
        halves.append(dot(t, jnp.concatenate(parts, axis=0)))
    return [jnp.concatenate([half[320 * e : 320 * e + 320] for half in halves], axis=0) for e in range(2)]


def dconv2_kernel(first, packs, cur_ref, prev_ref, t_ref, s_ref, *rest):
    r_ref, b_ref = (rest[-3], rest[-1]) if packs else rest[-2:]
    m = pl.program_id(0) + first

    @pl.when(pl.program_id(0) == 0)
    def _():
        b_ref[...] = jnp.zeros_like(b_ref)

    cur = jnp.where(m < 9, cur_ref[...], jnp.zeros((576, LANES), BF))
    prev = jnp.where(m > 0, prev_ref[...], jnp.zeros((576, LANES), BF))
    for e, part in enumerate(first_diffs(t_ref[...], cur, prev)):
        part = part * s_ref[e].astype(F32)
        r_ref[e] = part.astype(BF)
        if packs:
            rest[-2][0, e] = pack_rows(part, 640).astype(BF)
        b_ref[...] += jnp.sum(part.reshape(20, 32, LANES), axis=0)


def dconv2(r2, t2b, s1, first, count, packs, r1):
    block = pl.BlockSpec((2, 640, LANES), lambda m: (0, 0, m + first))
    ins = [r2, r2, t2b, s1]
    in_specs = [
        pl.BlockSpec((576, LANES), lambda m: (0, jnp.minimum(m + first, 8))),
        pl.BlockSpec((576, LANES), lambda m: (0, jnp.maximum(m + first - 1, 0))),
        whole((640, 768)),
        block,
    ]
    aliases = {}
    if r1 is not None:
        ins.append(r1)
        in_specs.append(pl.BlockSpec(memory_space=pl.ANY))
        aliases = {4: 0}
    shapes = [sds((2, 640, 10 * LANES), BF), sds((count, 2, 1120, 128), BF), sds((32, LANES), F32)]
    outs = [block, pl.BlockSpec((1, 2, 1120, 128), lambda m: (m, 0, 0, 0)), whole((32, LANES))]
    if not packs:
        del shapes[1], outs[1]
    return pl.pallas_call(
        functools.partial(dconv2_kernel, first, packs),
        out_shape=tuple(shapes),
        grid=(count,),
        in_specs=in_specs,
        out_specs=outs,
        input_output_aliases=aliases,
        compiler_params=pltpu.CompilerParams(vmem_limit_bytes=VMEM_BIG),
        cost_estimate=cost(2 * count),
    )(*ins)


def frame_rows(r0, r1, t1b, o_ref, at, rows):
    none = jnp.zeros((32, LANES), BF)
    for g in range(3):
        if g == 0:
            parts = [none, r0[:224], none, r1[:224]]
        elif g == 1:
            parts = [r0[192:448], r1[192:448]]
        else:
            parts = [r0[416:], none, r1[416:], none]
        out = dot(t1b, jnp.concatenate(parts, axis=0)).astype(BF)
        for dy in range(4):
            o_ref[at + dy, 28 * g : 28 * g + 28, :, :] = out[56 * dy : 56 * dy + 56, :rows].reshape(28, 2, rows)


def dframes_kernel(rows, first, last, far, flag_ref, own_ref, *rest):
    edge_ref, pair = rest[-2:]
    o_ref = rest[-3]
    own = flag_ref[0] == 1
    m = pl.program_id(0)
    t1b = rest[4] if far else rest[1]

    @pl.when(m == 0)
    def _():
        edge_ref[...] = jnp.zeros_like(edge_ref) if first == 0 else rest[5 if far else 2][...]

    @pl.when(own)
    def _():
        for e in range(2):
            pair[e] = own_ref[e]

    @pl.when(jnp.logical_not(own))
    def _():
        if far:
            cur = unpack_rows(rest[0][0].astype(F32), 576).astype(BF)
            prev = unpack_rows(rest[1][0].astype(F32), 576).astype(BF)
            prev = jnp.where(m + first > 0, prev, jnp.zeros_like(prev))
            for e, part in enumerate(first_diffs(rest[3][...], cur, prev)):
                pair[e] = (part * unpack_rows(rest[2][0, e].astype(F32), 640)).astype(BF)
        else:
            for e in range(2):
                pair[e] = unpack_rows(rest[0][0, e].astype(F32), 640).astype(BF)

    if last:
        inside = m < pl.num_programs(0) - 1
        for e in range(2):
            pair[e] = jnp.where(inside, pair[e], jnp.zeros((640, LANES), BF))
    frame_rows(pair[0], edge_ref[...], t1b[...], o_ref, 0, rows)
    if last:

        @pl.when(inside)
        def _():
            frame_rows(pair[1], pair[0], t1b[...], o_ref, 4, rows)

    else:
        frame_rows(pair[1], pair[0], t1b[...], o_ref, 4, rows)
    edge_ref[...] = pair[1]


def dframes(flag, own, got, t1b, rows, first, count, edge, out):
    far = len(got) > 1
    last = first + count == 10
    at = lambda m: jnp.minimum(m, count - 1)
    fixed = lambda shape: pl.BlockSpec(shape, lambda *_: (0,) * len(shape))
    ins = [flag, own]
    in_specs = [pl.BlockSpec((2, 640, LANES), lambda m, *_: (0, 0, at(m) + first))]
    if far:
        r2p, s1p, t2b = got
        ins += [r2p, r2p, s1p, t2b]
        in_specs += [
            pl.BlockSpec((1, 1008, 128), lambda m, *_: (m + first, 0, 0)),
            pl.BlockSpec((1, 1008, 128), lambda m, *_: (jnp.maximum(m + first - 1, 0), 0, 0)),
            pl.BlockSpec((1, 2, 1120, 128), lambda m, *_: (m, 0, 0, 0)),
            fixed((640, 768)),
        ]
    else:
        ins.append(got[0])
        in_specs.append(pl.BlockSpec((1, 2, 1120, 128), lambda m, *_: (at(m), 0, 0, 0)))
    ins.append(t1b)
    in_specs.append(fixed((224, 512)))
    aliases = {}
    if first:
        ins += [edge, out]
        in_specs += [fixed((640, LANES)), pl.BlockSpec(memory_space=pl.ANY)]
        aliases = {len(ins) - 1: 0}
    return pl.pallas_call(
        functools.partial(dframes_kernel, rows, first, last, far),
        out_shape=(sds((84, 84, 2, rows), BF), sds((640, LANES), BF)),
        grid_spec=pltpu.PrefetchScalarGridSpec(
            num_scalar_prefetch=1,
            grid=(count + 1 if last else count,),
            in_specs=in_specs,
            out_specs=[pl.BlockSpec((8, 84, 2, rows), lambda m, *_: (m + first, 0, 0, 0)), fixed((640, LANES))],
            scratch_shapes=[pltpu.VMEM((2, 640, LANES), BF)],
        ),
        input_output_aliases=aliases,
        compiler_params=pltpu.CompilerParams(vmem_limit_bytes=VMEM_BIG),
        cost_estimate=cost(3 * count),
    )(*ins)


def wdense_kernel(flag_ref, a_ref, rd_ref, rh_ref, h_ref, keep_ref, send_ref):
    core = flag_ref[1]
    grads = []
    for left, right in ((a_ref, rd_ref), (rh_ref, h_ref)):
        grads.append((dot_nt(left[...], right[...]) * (1.0 / LOSS_SCALE)).astype(BF))
    start = 0
    for grad in grads:
        size = grad.shape[0]
        for half in range(2):
            tile0 = grad[:, 256 * half : 256 * half + 128]
            tile1 = grad[:, 256 * half + 128 : 256 * half + 256]
            keep_ref[0, half, start : start + size, :] = jnp.where(core == 0, tile0, tile1)
            send_ref[0, half, start : start + size, :] = jnp.where(core == 0, tile1, tile0)
        start += size


def wdense(flag, a3, rd, rh, h):
    out = pl.BlockSpec((1, 2, 512, 128), lambda i, *_: (i, 0, 0, 0))
    return pl.pallas_call(
        wdense_kernel,
        out_shape=(sds((8, 2, 512, 128), BF), sds((8, 2, 512, 128), BF)),
        grid_spec=pltpu.PrefetchScalarGridSpec(
            num_scalar_prefetch=1,
            grid=(8,),
            in_specs=[
                pl.BlockSpec((392, LANES), lambda i, *_: (i, 0)),
                whole((512, LANES)),
                pl.BlockSpec((120, LANES), lambda i, *_: (i, 0)),
                whole((512, LANES)),
            ],
            out_specs=[out, out],
        ),
        compiler_params=pltpu.CompilerParams(vmem_limit_bytes=VMEM_BIG),
        cost_estimate=cost(1),
    )(flag, a3, rd, rh, h)


def wconv3_kernel(a_ref, r_ref, g_ref):
    acc = jnp.zeros((64, 576), F32)
    for j in range(7):
        left = jnp.concatenate(
            [a_ref[64 * j : 64 * j + 192, LANES * u : LANES * (u + 7)] for u in range(3)], axis=0
        )
        right = jnp.concatenate([r_ref[448 * i + 64 * j : 448 * i + 64 * j + 64, :] for i in range(7)], axis=1)
        acc = acc + dot_nt(right, left)
    g_ref[...] = acc * (1.0 / LOSS_SCALE)


def wconv3(a2, r3):
    return call(
        wconv3_kernel,
        sds((64, 576), F32),
        [whole(a2.shape), whole(r3.shape)],
        whole((64, 576)),
        us=7,
    )(a2, r3)


def wconv2_kernel(a_ref, r_ref, g_ref):
    g_ref[...] = jnp.zeros_like(g_ref)

    def body(j, _):
        window = pl.ds(pl.multiple_of(64 * j, 64), 128)
        left = jnp.concatenate(
            [a_ref[e, window, LANES * t : LANES * (t + 9)] for t in range(2) for e in range(2)], axis=0
        )
        g_ref[...] += dot_nt(left, r_ref[pl.ds(pl.multiple_of(64 * j, 64), 64), :])
        return 0

    lax.fori_loop(0, 9, body, 0)
    g_ref[...] = g_ref[...] * (1.0 / LOSS_SCALE)


def wconv2(a1, r2):
    return call(
        wconv2_kernel,
        sds((512, 64), F32),
        [whole(a1.shape), whole(r2.shape)],
        whole((512, 64)),
        us=11,
    )(a1, r2)


def wconv1_kernel(x_ref, n_ref, r_ref, g_ref, acc):
    step = pl.program_id(0)

    @pl.when(step == 0)
    def _():
        acc[...] = jnp.zeros_like(acc)

    def column(dy, rows, c):
        if c < 4:
            return x_ref[dy, rows, LANES * c : LANES * (c + 1)]
        return n_ref[dy, rows, :]

    total = acc[...]
    for g in range(5):
        rows = slice(64 * g, 64 * g + 80)
        left = jnp.concatenate(
            [
                jnp.concatenate([column(dy, rows, ii + t) for ii in range(4)], axis=1)
                for t in range(2)
                for dy in range(4)
            ],
            axis=0,
        )
        right = jnp.concatenate(
            [r_ref[ii % 2, 128 * g : 128 * g + 128, LANES * (ii // 2) : LANES * (ii // 2 + 1)] for ii in range(4)],
            axis=1,
        )
        total = total + dot_nt(left, right)
    acc[...] = total

    @pl.when(step == 4)
    def _():
        for dy in range(8):
            part = jnp.zeros((32, 32), F32)
            for jj in range(4):
                part = part + acc[80 * dy + 16 * jj : 80 * dy + 16 * jj + 32, 32 * jj : 32 * jj + 32]
            g_ref[32 * dy : 32 * dy + 32, :] = part * (1.0 / LOSS_SCALE)


def wconv1(xt, r1):
    return call(
        wconv1_kernel,
        sds((256, 32), F32),
        [
            pl.BlockSpec((4, 336, 4 * LANES), lambda s: (0, 0, s)),
            pl.BlockSpec((4, 336, LANES), lambda s: (0, 0, 4 * s + 4)),
            pl.BlockSpec((2, 640, 2 * LANES), lambda s: (0, 0, s)),
        ],
        whole((256, 32)),
        grid=(5,),
        scratch=[pltpu.VMEM((640, 128), F32)],
        us=14,
    )(xt, xt, r1)


SMALL_ROWS = 704


def lanes_of(shards):
    return max(1, 128 // shards)


def slot_rows(capacity):
    return (capacity + 7) // 8 * 8


def pack_kernel(shards, capacity, flag_ref, *refs):
    b1_refs, (b2_ref, b3_ref, g1_ref, g2_ref, g3_ref, db_ref, hb_ref, loss_ref, owner_ref, p_ref, w) = refs[:-11], refs[-11:]
    scale = 1.0 / LOSS_SCALE
    w[...] = jnp.zeros_like(w)
    for k in range(4):
        w[64 * k : 64 * k + 64, :] = g3_ref[:, 128 * k : 128 * k + 128]
    w[256:320, :64] = g3_ref[:, 512:]
    w[320:576, :64] = g2_ref[:256, :]
    w[320:576, 64:] = g2_ref[256:, :]
    w[576:704, :32] = g1_ref[:128, :]
    w[576:704, 32:64] = g1_ref[128:, :]
    total = b1_refs[0][...]
    for ref in b1_refs[1:]:
        total = total + ref[...]
    for column, value in ((64, total), (65, b2_ref[...]), (66, b3_ref[...])):
        w[576 : 576 + value.shape[0], column : column + 1] = jnp.sum(value, axis=1, keepdims=True) * scale
    for k in range(4):
        w[576:704, 67 + k : 68 + k] = db_ref[128 * k : 128 * k + 128, :] * scale
    for half in range(2):
        for k in range(4):
            start = 459 * half + 128 * k
            size = min(128, 459 * (half + 1) - start)
            w[576 : 576 + size, 71 + 4 * half + k : 72 + 4 * half + k] = hb_ref[start : start + size, :]

    owner = owner_ref[...]
    rows = owner.shape[1]
    owner_f = owner.astype(F32)
    down = jnp.broadcast_to(owner_f, (8, rows)).T[:, :1]
    same = (down == owner_f) & (
        lax.broadcasted_iota(jnp.int32, (rows, rows), 0) < lax.broadcasted_iota(jnp.int32, (rows, rows), 1)
    )
    slot = jnp.sum(same.astype(F32), axis=0, keepdims=True)
    group, height = lanes_of(shards), slot_rows(capacity)
    place = lax.broadcasted_iota(jnp.int32, (height, rows), 0).astype(F32)
    spread = jnp.where(place == slot, loss_ref[...], 0.0).astype(BF)
    lane = lax.broadcasted_iota(jnp.int32, (128, rows), 0)
    here = shards * lax.rem(owner, group) + flag_ref[2]
    for g in range(shards // group):
        hot = ((lane == here) & (owner // group == g)).astype(BF)
        w[SMALL_ROWS + height * g : SMALL_ROWS + height * g + height, :] = dot_nt(spread, hot)
    p_ref[...] = w[...].astype(BF)


def pack(flag, b1s, shards, capacity, *ins):
    total = SMALL_ROWS + shards // lanes_of(shards) * slot_rows(capacity)
    ins = tuple(b1s) + ins
    return call(
        functools.partial(pack_kernel, shards, capacity),
        sds((total, 128), BF),
        [pl.BlockSpec(memory_space=pltpu.SMEM)] + [whole(a.shape) for a in ins],
        whole((total, 128)),
        scratch=[pltpu.VMEM((total, 128), F32)],
        us=3,
    )(flag, *ins)


def split_kernel(shards, capacity, flag_ref, own_ref, got_ref, k1, b1, k2, b2, k3, b3, db, hb, prio, w):
    own = flag_ref[0] == 1
    w[...] = jnp.where(own, own_ref[...].astype(F32), got_ref[...].astype(F32))

    def pick(low, high):
        return jnp.where(own, low, high)

    k1[...] = pick(w[576:704, :32], w[576:704, 32:64])
    k2[...] = pick(w[320:576, :64], w[320:576, 64:])
    for n in range(9):
        rows = slice(64 * (n // 2), 64 * (n // 2) + 64)
        part = w[rows, 64 * (n % 2) : 64 * (n % 2) + 64]
        k3[n] = pick(part[:32], part[32:])
    columns = w[576:704, :].T
    b1[...] = pick(columns[64:65, :16], columns[64:65, 16:32])
    for ref, at in ((b2, 65), (b3, 66)):
        ref[...] = pick(columns[at : at + 1, :32], columns[at : at + 1, 32:64])
    for k in range(2):
        db[:, 128 * k : 128 * k + 128] = pick(columns[67 + k : 68 + k], columns[69 + k : 70 + k])
    for k in range(4):
        size = min(128, 459 - 128 * k)
        hb[:, 128 * k : 128 * k + size] = pick(columns[71 + k : 72 + k, :size], columns[75 + k : 76 + k, :size])
    group, height = lanes_of(shards), slot_rows(capacity)
    me = flag_ref[2]
    block = w[pl.ds(pl.multiple_of(SMALL_ROWS + height * (me // group), 8), height), :]
    if group > 1:
        block = pltpu.roll(block, lax.rem(128 - shards * lax.rem(me, group), 128), 1)
    half = capacity // 2
    prio[:, 0, :] = pick(block[:half, :shards], block[half : 2 * half, :shards])


def split(flag, own, got, shards, capacity):
    shapes = (
        (128, 32),
        (1, 16),
        (256, 64),
        (1, 32),
        (9, 32, 64),
        (1, 32),
        (1, 256),
        (1, 459),
        (capacity // 2, 1, shards),
    )
    return call(
        functools.partial(split_kernel, shards, capacity),
        tuple(sds(s, F32) for s in shapes),
        [pl.BlockSpec(memory_space=pltpu.SMEM), whole(own.shape), whole(got.shape)],
        [whole(s) for s in shapes],
        scratch=[pltpu.VMEM(own.shape, F32)],
        us=2,
    )(flag, own, got)


def unchunk_kernel(flag_ref, cur_ref, other_ref, d_ref, h_ref):
    core = flag_ref[1]
    cur, other = cur_ref[0].astype(F32), other_ref[0].astype(F32)
    tile0 = jnp.where(core == 0, cur, other)
    tile1 = jnp.where(core == 0, other, cur)
    d_ref[:, :128] = tile0[:392]
    d_ref[:, 128:] = tile1[:392]
    h_ref[:, :128] = tile0[392:]
    h_ref[:, 128:] = tile1[392:]


def unchunk(flag, cur, other):
    part = pl.BlockSpec((1, 512, 128), lambda i, f: (i ^ f[3], 0, 0))
    return pl.pallas_call(
        unchunk_kernel,
        out_shape=(sds((3136, 256), F32), sds((LOGITS, 256), F32)),
        grid_spec=pltpu.PrefetchScalarGridSpec(
            num_scalar_prefetch=1,
            grid=(8,),
            in_specs=[part, part],
            out_specs=[
                pl.BlockSpec((392, 256), lambda i, *_: (i, 0)),
                pl.BlockSpec((120, 256), lambda i, *_: (i, 0)),
            ],
        ),
        compiler_params=pltpu.CompilerParams(vmem_limit_bytes=VMEM_BIG),
        cost_estimate=cost(7),
    )(flag, cur, other)


def after(value, *others):
    return lax.optimization_barrier((value,) + others)[0]


def hand(value):
    return lax.ppermute(value, "pair", [(0, 1)])


def swap(value, bit):
    devices = lax.axis_size("batch")
    return lax.ppermute(value, "batch", [(i, i ^ bit) for i in range(devices)])


def add(left, right):
    return (left.astype(F32) + right.astype(F32)).astype(BF)


def reduce_chunks(keep, send, me):
    devices = lax.axis_size("batch")
    got = swap(send, 1)
    cur = add(keep, got)
    blocks, spread = devices // 2, devices // 16
    if spread > 1:
        cur = cur.reshape(8, 2, spread, 512 // spread, 128).transpose(0, 2, 1, 3, 4)
        cur = cur.reshape(blocks, 2, 512 // spread, 128)
    bit = 2
    arrived = [got]
    while bit < devices:
        mine = (me // bit) % 2
        pairs = cur.reshape((cur.shape[0] // 2, 2) + cur.shape[1:])
        send = lax.dynamic_index_in_dim(pairs, 1 - mine, axis=1, keepdims=False)
        keep = lax.dynamic_index_in_dim(pairs, mine, axis=1, keepdims=False)
        got = swap(send, bit)
        arrived.append(got)
        cur = add(keep, got)
        bit *= 2
    return cur[0], arrived


def unmix(blocks, code):
    bit = 1
    while bit < blocks.shape[0]:
        pairs = blocks.reshape((-1, 2, bit) + blocks.shape[1:])
        blocks = jnp.where((code // bit) % 2 == 1, pairs[:, ::-1], pairs).reshape(blocks.shape)
        bit *= 2
    return blocks


def gather_chunks(mine, me, late):
    devices = lax.axis_size("batch")
    cur = mine[None]
    bit = devices // 2
    while bit > 1:
        if bit == 2:
            cur = after(cur, late)
        other = swap(cur, bit)
        cur = jnp.stack([cur, other], axis=1).reshape((2 * cur.shape[0],) + cur.shape[1:])
        bit //= 2
    other = swap(cur, 1)
    return cur, other


def local(
    frames,
    kernel_first,
    bias_first,
    kernel_second,
    bias_second,
    kernel_third,
    bias_third,
    dense_weight,
    dense_bias,
    head_weight,
    head_bias,
    taken_actions,
    greedy_actions,
    done_flags,
    bin_lower,
    bin_fraction,
    owner_shard,
):
    online = lax.axis_index("pair") == 0
    me = lax.axis_index("batch")
    shards = lax.axis_size("batch")
    rows = frames.shape[1]
    capacity = 2 * ((rows + shards - 1) // shards)
    block = me // 2 if shards == 16 else me * 0
    flag = jnp.stack([online.astype(jnp.int32), me % 2, me, block]).astype(jnp.int32)
    xv = frames[0].transpose(2, 3, 1, 0)
    k1, k2, k3 = kernel_first[0], kernel_second[0], kernel_third[0]
    ones = jnp.zeros((16, LANES), BF).at[0].set(1)
    t1, t2, t3, t3b, t2b, b2 = bands(k1, bias_first, k2, bias_second, k3, bias_third)

    k1_got, k2_got = hand(after(k1[:, :, 2:], t1)), hand(after(k2, t1))
    a1, s1, xt, early = conv1(xv, t1, ones, 0, 2 * EARLY, ())
    early = hand(after(early, k1_got, k2_got))
    a1, s1, xt, late = conv1(xv, t1, ones, 2 * EARLY, 20, (a1, s1, xt))
    late = hand(late)
    a2, s2 = conv2(a1, t2, b2)
    a3, s3 = conv3(a2, t3, ones)
    wd = dense_weight[0]
    wht = head_weight[0].T
    pd = lax.dot_general(wd, a3, (((0,), (0,)), ((), ())), preferred_element_type=F32)
    taken = taken_actions[None, :]
    sel = jnp.where(online, taken, greedy_actions[None, :])
    h, sd, lp, cho = head(pd, dense_bias, wht, head_bias, sel)
    cho = lax.ppermute(cho, "pair", [(1, 0)])
    row_loss, rh, hb = loss(cho, done_flags[None, :], bin_lower.T, bin_fraction.T, lp, taken)

    diff_dense = lax.dot_general(wht, rh, (((0,), (0,)), ((), ())), preferred_element_type=F32)
    diff_dense = diff_dense * (0.5 * sd.astype(F32))
    rd = diff_dense.astype(BF)
    db = jnp.sum(diff_dense, axis=1, keepdims=True)

    keep, send = wdense(flag, a3, after(rd, early), rh, h)
    chunk, arrived = reduce_chunks(keep, send, me)

    r3, b3g = dflat(wd, rd, s3)
    r2, r2p, b2g = dconv3(after(r3, arrived[0]), t3b, s2)
    r2p = hand(r2p)
    r1, packed, b1s = None, [], []
    for first, count in NEAR:
        r1, part, b1g = dconv2(after(r2, late), t2b, s1, first, count, True, r1)
        packed.append(part)
        b1s.append(b1g)
    r1, b1g = dconv2(r2, t2b, s1, 0, FAR, False, r1)
    b1s.append(b1g)
    gots = [hand(after(packed[0], r2p))]
    g3 = wconv3(a2, after(r3, arrived[1]))
    g2 = wconv2(a1, after(r2, arrived[1]))
    g1 = wconv1(xt, after(r1, arrived[2]))
    small = pack(flag, b1s, shards, capacity, b2g, b3g, g1, g2, g3, db, hb, row_loss, owner_shard.T)
    t1b, t2b_online = band_frames(flag, k1, k1_got, k2, k2_got)
    far_chunk = hand(chunk[1])
    gots.append(hand(after(packed[1], arrived[-1], gots[0])))
    out, edge, outs = None, None, []
    for first, s1p in ((0, early), (EARLY, late)):
        out, edge = dframes(flag, r1, (r2p, s1p, t2b_online), t1b, rows, first, s1p.shape[0], edge, out)
        outs.append(edge)
    for (first, count), got in zip(NEAR, gots):
        out, edge = dframes(flag, r1, (got,), t1b, rows, first, count, edge, out)
        outs.append(edge)
    small = after(small, gots[0])
    bit, n = 1, -2
    while bit < shards:
        if 0 <= n < 3:
            small = after(small, outs[n])
        small = add(small, swap(small, bit))
        bit, n = 2 * bit, n + 1
    far_small = hand(small)
    mine = jnp.where(online, chunk[0], far_chunk)
    cur, other = gather_chunks(mine, me, gots[1])
    if shards != 16:
        cur, other = (unmix(v, me // 2).reshape(8, 512, 128) for v in (cur, other))
    dense_out, head_out = unchunk(flag, cur, other)
    o = split(flag, small, far_small, shards, capacity)
    return (
        o[0].reshape(4, 8, 4, 32),
        o[1].reshape(16),
        o[2].reshape(2, 4, 32, 64),
        o[3].reshape(32),
        o[4].reshape(3, 3, 32, 64).transpose(0, 1, 3, 2),
        o[5].reshape(32),
        dense_out,
        o[6].reshape(256),
        head_out.T,
        o[7].reshape(459),
        out.transpose(3, 2, 0, 1),
        o[8].transpose(1, 2, 0),
    )


def solution(mesh):
    return jax.shard_map(
        local,
        mesh=mesh,
        in_specs=(
            P("pair", "batch", None, None, None),
            P("pair", None, None, None, None),
            P("pair", None),
            P("pair", None, None, None, None),
            P("pair", None),
            P("pair", None, None, None, None),
            P("pair", None),
            P("pair", None, None),
            P("pair", None),
            P("pair", None, None),
            P("pair", None),
            P("batch"),
            P("batch"),
            P("batch"),
            P("batch", None),
            P("batch", None),
            P("batch", None),
        ),
        out_specs=(
            P("pair", None, None, None),
            P("pair"),
            P("pair", None, None, None),
            P("pair"),
            P(None, None, None, "pair"),
            P("pair"),
            P(None, "pair"),
            P("pair"),
            P("pair", None),
            P("pair"),
            P("batch", "pair", None, None),
            P("batch", None, "pair"),
        ),
        check_vma=False,
    )
```

```python
import functools

import jax
import jax.numpy as jnp
from jax import lax
from jax.experimental import pallas as pl
from jax.experimental.pallas import tpu as pltpu
from jax.sharding import PartitionSpec as P

ACT = 18
ATOMS = 51
LOGITS = ACT * ATOMS
LOSS_SCALE = 256
LANES = 256
BF = jnp.bfloat16
F32 = jnp.float32
VMEM_BIG = 60 << 20
FAR = 6
EARLY = 4
NEAR = ((6, 2), (8, 2))


def cost(us):
    return pl.CostEstimate(flops=int(us * 0.4e9), bytes_accessed=0, transcendentals=0)


def call(kernel, out, ins, outs, us, grid=None, scratch=()):
    return pl.pallas_call(
        kernel,
        out_shape=out,
        grid=() if grid is None else grid,
        in_specs=ins,
        out_specs=outs,
        scratch_shapes=list(scratch),
        compiler_params=pltpu.CompilerParams(vmem_limit_bytes=VMEM_BIG),
        cost_estimate=cost(us),
    )


def whole(shape):
    return pl.BlockSpec(shape, lambda *_: (0,) * len(shape))


def sds(shape, dtype):
    return jax.ShapeDtypeStruct(shape, dtype)


def dot(left, right):
    return jnp.dot(left, right, preferred_element_type=F32)


def dot_nt(left, right):
    return lax.dot_general(left, right, (((1,), (1,)), ((), ())), preferred_element_type=F32)


def act_slope(half):
    tan = jnp.tanh(half)
    up = 1.0 + tan
    act = half * up
    return act, up + act * (1.0 - tan)


def second_bands(k2n, w2b):
    for e in range(2):
        for t in range(2):
            u = 2 * t + e
            for j in range(6):
                lo = max(0, 2 * j - 2)
                hi = min(10, 2 * j + 2)
                v0 = lo - (2 * j - 2)
                w2b[320 * e + 32 * lo : 320 * e + 32 * hi, 384 * t + 64 * j : 384 * t + 64 * j + 64] = k2n[
                    128 * u + 32 * v0 : 128 * u + 32 * (v0 + hi - lo), :
                ]


def bands_kernel(k1, b1, k2, b2, k3, b3, t1, t2, t3, t3b, t2b, b2c, send, w1, w2, w3, w3b, w2b):
    for ref in (w1, w2, w3, w3b, w2b):
        ref[...] = jnp.zeros_like(ref)

    def turned(kernel, bias):
        flat = kernel[...].astype(F32)
        flat = flat.reshape(-1, flat.shape[-1])
        bias = jnp.broadcast_to(bias[...].astype(F32), (8, flat.shape[1]))
        return flat, flat.T, bias.T[:, :1]

    _, k1t, b1c = turned(k1, b1)
    send[:512, :] = k2[...].reshape(512, 64)
    send[512:, :32] = k1[:, :, 2:, :].astype(F32).reshape(128, 32).astype(BF)
    send[512:, 32:] = jnp.zeros((128, 32), BF)
    k2n, k2t, b2t = turned(k2, b2)
    k3n, k3t, b3c = turned(k3, b3)
    for jj in range(10):
        for dy in range(8):
            w1[32 * jj : 32 * jj + 32, 176 * dy + 16 * jj : 176 * dy + 16 * jj + 32] = k1t[:, 32 * dy : 32 * dy + 32]
        w1[32 * jj : 32 * jj + 32, 1408:1409] = b1c
    for jj in range(3):
        for u in range(4):
            w2[64 * jj : 64 * jj + 64, 256 * u + 64 * jj : 256 * u + 64 * jj + 128] = k2t[:, 128 * u : 128 * u + 128]
        b2c[64 * jj : 64 * jj + 64, :] = 0.5 * b2t
    for j in range(7):
        for u in range(3):
            w3[64 * j : 64 * j + 64, 576 * u + 64 * j : 576 * u + 64 * j + 192] = k3t[:, 192 * u : 192 * u + 192]
            w3b[64 * j : 64 * j + 192, 448 * (2 - u) + 64 * j : 448 * (2 - u) + 64 * j + 64] = k3n[192 * u : 192 * u + 192, :]
        w3[64 * j : 64 * j + 64, 1728:1729] = b3c
    second_bands(k2n, w2b)
    t1[...] = (0.5 * w1[...]).astype(BF)
    t2[...] = (0.5 * w2[...]).astype(BF)
    t3[...] = (0.5 * w3[...]).astype(BF)
    t3b[...] = (0.5 * w3b[...]).astype(BF)
    t2b[...] = (0.5 * w2b[...]).astype(BF)


def bands(*ins):
    shapes = ((320, 1424), (192, 1024), (448, 1744), (576, 1344), (640, 768))
    return call(
        bands_kernel,
        tuple(sds(s, BF) for s in shapes) + (sds((192, 1), F32), sds((640, 64), BF)),
        [whole(a.shape) for a in ins],
        [whole(s) for s in shapes] + [whole((192, 1)), whole((640, 64))],
        scratch=[pltpu.VMEM(s, F32) for s in shapes],
        us=5,
    )(*ins)


def band_frames_kernel(flag_ref, k1, k2, got, t1b, t2b, w1b, w2b):
    own = flag_ref[0] == 1
    w1b[...] = jnp.zeros_like(w1b)
    w2b[...] = jnp.zeros_like(w2b)
    half = jnp.where(own, k1[:, :, :2, :].astype(F32).reshape(128, 32), got[512:, :32].astype(F32)).reshape(8, 16, 32)
    for dy in range(8):
        t, row = divmod(dy, 4)
        for j in range(8):
            lo = max(0, 4 * j - 4)
            hi = min(28, 4 * j + 4)
            d0 = lo - (4 * j - 4)
            w1b[56 * row + 2 * lo : 56 * row + 2 * hi, 256 * t + 32 * j : 256 * t + 32 * j + 32] = half[
                dy, 2 * d0 : 2 * (d0 + hi - lo), :
            ]
    second_bands(jnp.where(own, k2[...].astype(F32).reshape(512, 64), got[:512, :].astype(F32)), w2b)
    t1b[...] = w1b[...].astype(BF)
    t2b[...] = (0.5 * w2b[...]).astype(BF)


def band_frames(flag, *ins):
    shapes = ((224, 512), (640, 768))
    return call(
        band_frames_kernel,
        tuple(sds(s, BF) for s in shapes),
        [pl.BlockSpec(memory_space=pltpu.SMEM)] + [whole(a.shape) for a in ins],
        [whole(s) for s in shapes],
        scratch=[pltpu.VMEM(s, F32) for s in shapes],
        us=3,
    )(flag, *ins)


def pack_rows(part, n):
    lane = lax.broadcasted_iota(jnp.int32, (n // 4, 128), 1)
    tail = [part[n // 4 * k : n // 4 * (k + 1), 128:] for k in range(4)]
    packed = [jnp.where(lane < 96, tail[k], pltpu.roll(tail[3], 96 - 32 * k, 1)) for k in range(3)]
    return jnp.concatenate([part[:, :128]] + packed, axis=0)


def unpack_rows(packed, n):
    lane = lax.broadcasted_iota(jnp.int32, (n // 4, 128), 1)
    tail = [packed[n + n // 4 * k : n + n // 4 * (k + 1)] for k in range(3)]
    last = pltpu.roll(tail[0], 32, 1)
    last = jnp.where(lane < 32, last, jnp.where(lane < 64, pltpu.roll(tail[1], 64, 1), pltpu.roll(tail[2], 96, 1)))
    return jnp.concatenate([packed[:n], jnp.concatenate(tail + [last], axis=0)], axis=1)


def conv1_kernel(rows, start, packs, first_ref, xa_ref, xb_ref, t1_ref, ones_ref, *rest):
    cells = rest[-1]
    a_ref, s_ref, xt_ref, p_ref = rest[-5:-1] if start else rest[-6:-2]
    m = pl.program_id(0) + start

    def relay(ref, slot):
        for dy in range(4):
            cells[slot, dy, :, :rows] = ref[dy].reshape(336, rows)

    @pl.when(m == start)
    def _():
        cells[...] = jnp.zeros_like(cells)
        relay(first_ref, 0)
        if not start:
            rest[-2][...] = cells[0]

    relay(xa_ref, 1)
    relay(xb_ref, 2)
    slopes = []
    for e in range(2):
        parts_of = lambda window, e=e: [cells[e + t, dy, window, :] for t in range(2) for dy in range(4)]
        row = []
        for g in range(2):
            half = dot(t1_ref[...], jnp.concatenate(parts_of(pl.ds(160 * g, 176)) + [ones_ref[...]], axis=0))
            act, slope = act_slope(half)
            a_ref[e, 320 * g : 320 * g + 320, :] = act.astype(BF)
            s_ref[e, 320 * g : 320 * g + 320, :] = slope.astype(BF)
            row.append(slope)
        slopes.append(row)
    if not start:
        for e in range(2):
            p_ref[0, e] = pack_rows(jnp.concatenate(slopes[e], axis=0), 640).astype(BF)
    for dy in range(4):
        xt_ref[dy, :, :LANES] = cells[1, dy]
        xt_ref[dy, :, LANES:] = cells[2, dy]
        cells[0, dy] = cells[2, dy]
    if start:

        @pl.when(m < packs)
        def _():
            for e in range(2):
                p_ref[0, e] = pack_rows(s_ref[e].astype(F32), 640).astype(BF)


def conv1(xv, t1, ones, start, stop, before):
    rows = xv.shape[3]
    packs = min(stop, FAR)
    cell = lambda f: pl.BlockSpec((4, 84, 4, rows), lambda m: (f(m + start), 0, 0, 0))
    out = pl.BlockSpec((2, 640, LANES), lambda m: (0, 0, m + start))
    outs = [
        out,
        out,
        pl.BlockSpec((4, 336, 2 * LANES), lambda m: (0, 0, m + start)),
        pl.BlockSpec((1, 2, 1120, 128), lambda m: (jnp.minimum(m, packs - start - 1), 0, 0, 0)),
    ]
    shapes = [
        sds((2, 640, 10 * LANES), BF),
        sds((2, 640, 10 * LANES), BF),
        sds((4, 336, 20 * LANES), BF),
        sds((packs - start, 2, 1120, 128), BF),
    ]
    if not start:
        outs.append(whole((4, 336, LANES)))
        shapes.append(sds((4, 336, LANES), BF))
    return pl.pallas_call(
        functools.partial(conv1_kernel, rows, start, packs),
        out_shape=tuple(shapes),
        grid=(stop - start,),
        in_specs=[
            pl.BlockSpec((4, 84, 4, rows), lambda m: (2 * start, 0, 0, 0)),
            cell(lambda m: 2 * m + 1),
            cell(lambda m: 2 * m + 2),
            whole((320, 1424)),
            whole((16, LANES)),
        ]
        + [pl.BlockSpec(memory_space=pl.ANY)] * len(before),
        out_specs=outs,
        scratch_shapes=[pltpu.VMEM((3, 4, 336, LANES), BF)],
        input_output_aliases={5 + n: n for n in range(len(before))},
        compiler_params=pltpu.CompilerParams(vmem_limit_bytes=VMEM_BIG),
        cost_estimate=cost(0.2 * (stop - start)),
    )(xv, xv, xv, t1, ones, *before)


def conv23_kernel(r0_ref, r1_ref, t2_ref, b2_ref, t3_ref, ones_ref, a2_ref, s2_ref, a3_ref, s3_ref, keep):
    g = pl.program_id(0)

    def third():
        window = pl.ds(pl.multiple_of(576 * (g - 3), 64), 1728)
        half = dot(t3_ref[...], jnp.concatenate([keep[window, :], ones_ref[...]], axis=0))
        act, slope = act_slope(half)
        a3_ref[...] = act.astype(BF)
        s3_ref[...] = slope.astype(BF)

    def second():
        for n in range(3):
            window = pl.ds(192 * n, 256)
            parts = [r0_ref[0, window, :], r0_ref[1, window, :], r1_ref[0, window, :], r1_ref[1, window, :]]
            half = dot(t2_ref[...], jnp.concatenate(parts, axis=0)) + b2_ref[...]
            act, slope = act_slope(half)
            act = act.astype(BF)
            a2_ref[192 * n : 192 * n + 192, :] = act
            keep[pl.ds(pl.multiple_of(576 * g + 192 * n, 64), 192), :] = act
            s2_ref[192 * n : 192 * n + 192, :] = slope.astype(BF)

    @pl.when(g < 3)
    def _():
        second()

    @pl.when((g >= 3) & (g < 9))
    def _():
        third()
        second()

    @pl.when(g == 9)
    def _():
        third()


def conv23(a1, t2, b2, t3, ones):
    row = lambda t: pl.BlockSpec((2, 640, LANES), lambda g: (0, 0, jnp.minimum(g, 8) + t))
    out2 = pl.BlockSpec((576, LANES), lambda g: (0, jnp.minimum(g, 8)))
    out3 = pl.BlockSpec((448, LANES), lambda g: (jnp.maximum(g - 3, 0), 0))
    return call(
        conv23_kernel,
        (sds((576, 9 * LANES), BF), sds((576, 9 * LANES), BF), sds((3136, LANES), BF), sds((3136, LANES), BF)),
        [row(0), row(1), whole((192, 1024)), whole((192, 1)), whole((448, 1744)), whole((16, LANES))],
        [out2, out2, out3, out3],
        us=2,
        grid=(10,),
        scratch=[pltpu.VMEM((9 * 576, LANES), BF)],
    )(a1, a1, t2, b2, t3, ones)


def head_kernel(rows, pd_ref, bd_ref, wh_ref, bh_ref, sel_ref, act_ref, slope_ref, lp_ref, cho_ref, lg_ref):
    bd = jnp.broadcast_to(bd_ref[...].astype(F32), (8, 512)).T[:, :1]
    bh = jnp.broadcast_to(bh_ref[...].astype(F32), (8, LOGITS)).T[:, :1]
    act, slope = act_slope((pd_ref[...] + bd) * 0.5)
    act_ref[...] = act.astype(BF)
    slope_ref[...] = slope.astype(BF)
    lg_ref[...] = dot(wh_ref[...], act_ref[...]) + bh
    sel = sel_ref[...]
    pick = jnp.zeros((ATOMS, rows), F32)
    for a in range(ACT):
        pick = jnp.where(sel == a, lg_ref[ATOMS * a : ATOMS * a + ATOMS, :rows], pick)
    shifted = pick - jnp.max(pick, axis=0, keepdims=True)
    grown = jnp.exp(shifted)
    total = jnp.sum(grown, axis=0, keepdims=True)
    cho_ref[...] = (grown / total).astype(BF)
    lp_ref[...] = shifted - jnp.log(total)


def head(pd, bd, wht, bh, sel):
    rows = sel.shape[1]
    ins = (pd, bd, wht, bh, sel)
    outs = (((512, LANES), BF), ((512, LANES), BF), ((ATOMS, rows), F32), ((ATOMS, rows), BF))
    return call(
        functools.partial(head_kernel, rows),
        tuple(sds(*o) for o in outs),
        [whole(a.shape) for a in ins],
        [whole(o[0]) for o in outs],
        scratch=[pltpu.VMEM((LOGITS, LANES), F32)],
        us=0.5,
    )(*ins)


def loss_kernel(rows, cho_ref, done_ref, low_ref, frac_ref, lp_ref, taken_ref, loss_ref, rh_ref, hb_ref, d_ref):
    atoms = lax.broadcasted_iota(jnp.int32, (ATOMS, rows), 0)
    done = done_ref[...].astype(F32)
    mass = (1.0 - done) * cho_ref[...].astype(F32) + done * (atoms == 0).astype(F32)
    frac = frac_ref[...]
    stay = mass * (1.0 - frac)
    move = mass * frac
    low = low_ref[...]
    proj = jnp.zeros((ATOMS, rows), F32)
    for i in range(ATOMS):
        gap = atoms - low[i : i + 1, :]
        proj = proj + jnp.where(gap == 0, stay[i : i + 1, :], jnp.where(gap == 1, move[i : i + 1, :], 0.0))
    lp = lp_ref[...]
    loss_ref[...] = -jnp.sum(proj * lp, axis=0, keepdims=True)
    diff = (jnp.sum(proj, axis=0, keepdims=True) * jnp.exp(lp) - proj) * LOSS_SCALE
    taken = taken_ref[...]
    for a in range(ACT):
        d_ref[ATOMS * a : ATOMS * a + ATOMS, :] = jnp.where(taken == a, diff, 0.0)
    rh_ref[...] = jnp.zeros_like(rh_ref)
    rh_ref[:, :rows] = d_ref[...].astype(BF)
    hb_ref[...] = jnp.sum(d_ref[...], axis=1, keepdims=True) * (1.0 / LOSS_SCALE)


def loss(cho, done, low, frac, lp, taken):
    rows = taken.shape[1]
    ins = (cho, done, low, frac, lp, taken)
    outs = (((1, rows), F32), ((LOGITS, LANES), BF), ((LOGITS, 1), F32))
    return call(
        functools.partial(loss_kernel, rows),
        tuple(sds(*o) for o in outs),
        [whole(a.shape) for a in ins],
        [whole(o[0]) for o in outs],
        scratch=[pltpu.VMEM((LOGITS, rows), F32)],
        us=0.5,
    )(*ins)


def dthird_kernel(w_ref, rd_ref, s3_ref, t_ref, s2_ref, r3_ref, b3_ref, r2_ref, p_ref, b2_ref, keep):
    g = pl.program_id(0)

    def third():
        diff = dot(w_ref[...], rd_ref[...]) * (0.5 * s3_ref[...].astype(F32))
        part = diff.astype(BF)
        r3_ref[...] = part
        keep[pl.ds(pl.multiple_of(448 * (g + 2), 64), 448), :] = part
        b3_ref[...] += jnp.sum(diff.reshape(7, 64, LANES), axis=0)

    def second():
        window = pl.ds(pl.multiple_of(448 * (g - 1), 64), 1344)
        diff = dot(t_ref[...], keep[window, :]) * s2_ref[...].astype(F32)
        r2_ref[...] = diff.astype(BF)
        b2_ref[...] += jnp.sum(diff.reshape(9, 64, LANES), axis=0)
        return diff

    def pack(diff):
        p_ref[0] = pack_rows(diff, 576).astype(BF)

    @pl.when(g == 0)
    def _():
        b3_ref[...] = jnp.zeros_like(b3_ref)
        b2_ref[...] = jnp.zeros_like(b2_ref)
        keep[:896, :] = jnp.zeros((896, LANES), BF)
        keep[4032:, :] = jnp.zeros((896, LANES), BF)
        third()

    @pl.when((g >= 1) & (g < 7))
    def _():
        pack(second())
        third()

    @pl.when((g >= 7) & (g <= FAR))
    def _():
        pack(second())

    @pl.when(g > FAR)
    def _():
        second()


def dthird(wd, rd, s3, t3b, s2):
    block3 = pl.BlockSpec((448, LANES), lambda g: (jnp.minimum(g, 6), 0))
    block2 = pl.BlockSpec((576, LANES), lambda g: (0, jnp.maximum(g - 1, 0)))
    packed = pl.BlockSpec((1, 1008, 128), lambda g: (jnp.clip(g - 1, 0, FAR - 1), 0, 0))
    return call(
        dthird_kernel,
        (
            sds((3136, LANES), BF),
            sds((64, LANES), F32),
            sds((576, 9 * LANES), BF),
            sds((FAR, 1008, 128), BF),
            sds((64, LANES), F32),
        ),
        [
            pl.BlockSpec((448, 512), lambda g: (jnp.minimum(g, 6), 0)),
            whole((512, LANES)),
            block3,
            whole((576, 1344)),
            block2,
        ],
        [block3, whole((64, LANES)), block2, packed, whole((64, LANES))],
        us=1.5,
        grid=(10,),
        scratch=[pltpu.VMEM((4928, LANES), BF)],
    )(wd, rd, s3, t3b, s2)


def first_diffs(t, cur, prev):
    none = jnp.zeros((64, LANES), BF)
    halves = []
    for h in range(2):
        if h == 0:
            parts = [none, cur[:320], none, prev[:320]]
        else:
            parts = [cur[256:], none, prev[256:], none]
        halves.append(dot(t, jnp.concatenate(parts, axis=0)))
    return [jnp.concatenate([half[320 * e : 320 * e + 320] for half in halves], axis=0) for e in range(2)]


def dconv2_kernel(first, packs, cur_ref, prev_ref, t_ref, s_ref, *rest):
    dense = [(ref, n) for ref, (_, size) in zip(rest[-3:-1], NEAR) for n in range(size)] if packs else []
    r_ref, b_ref = rest[-4 if packs else -2], rest[-1]
    q = pl.program_id(0)
    m = 2 * q + first
    zero = jnp.zeros((576, LANES), BF)

    @pl.when(pl.program_id(0) == 0)
    def _():
        b_ref[...] = jnp.zeros_like(b_ref)

    r2 = [
        jnp.where(m > 0, prev_ref[...], zero),
        cur_ref[:, :LANES],
        jnp.where(m < 8, cur_ref[:, LANES:], zero),
    ]
    total = b_ref[...]
    for k in range(2):
        lanes = slice(LANES * k, LANES * (k + 1))
        for e, part in enumerate(first_diffs(t_ref[...], r2[k + 1], r2[k])):
            part = part * s_ref[e, :, lanes].astype(F32)
            r_ref[e, :, lanes] = part.astype(BF)
            if packs:
                value = pack_rows(part, 640).astype(BF)
                for step in range(packs):

                    @pl.when(q == step)
                    def _(step=step, k=k, e=e, value=value):
                        ref, n = dense[2 * step + k]
                        ref[n, e] = value

            total = total + jnp.sum(part.reshape(20, 32, LANES), axis=0)
    b_ref[...] = total


def dconv2(r2, t2b, s1, first, count, dense, r1):
    packs = count // 2 if dense else 0
    block = pl.BlockSpec((2, 640, 2 * LANES), lambda q: (0, 0, q + first // 2))
    ins = [r2, r2, t2b, s1]
    in_specs = [
        pl.BlockSpec((576, 2 * LANES), lambda q: (0, q + first // 2)),
        pl.BlockSpec((576, LANES), lambda q: (0, jnp.maximum(2 * q + first - 1, 0))),
        whole((640, 768)),
        block,
    ]
    aliases = {}
    if r1 is not None:
        ins.append(r1)
        in_specs.append(pl.BlockSpec(memory_space=pl.ANY))
        aliases = {4: 0}
    parts = [(size, 2, 1120, 128) for _, size in NEAR] if packs else []
    shapes = [sds((2, 640, 10 * LANES), BF)] + [sds(p, BF) for p in parts] + [sds((32, LANES), F32)]
    outs = [block] + [whole(p) for p in parts] + [whole((32, LANES))]
    return pl.pallas_call(
        functools.partial(dconv2_kernel, first, packs),
        out_shape=tuple(shapes),
        grid=(count // 2,),
        in_specs=in_specs,
        out_specs=outs,
        input_output_aliases=aliases,
        compiler_params=pltpu.CompilerParams(vmem_limit_bytes=VMEM_BIG),
        cost_estimate=cost(2 * count),
    )(*ins)


def frame_rows(r0, r1, t1b, o_ref, at, rows):
    none = jnp.zeros((32, LANES), BF)
    for g in range(3):
        if g == 0:
            parts = [none, r0[:224], none, r1[:224]]
        elif g == 1:
            parts = [r0[192:448], r1[192:448]]
        else:
            parts = [r0[416:], none, r1[416:], none]
        out = dot(t1b, jnp.concatenate(parts, axis=0)).astype(BF)
        for dy in range(4):
            o_ref[at + dy, 28 * g : 28 * g + 28, :, :] = out[56 * dy : 56 * dy + 56, :rows].reshape(28, 2, rows)


def dframes_kernel(rows, first, last, far, flag_ref, own_ref, *rest):
    edge_ref, pair = rest[-2:]
    o_ref = rest[-3]
    own = flag_ref[0] == 1
    m = pl.program_id(0)
    t1b = rest[4] if far else rest[1]

    @pl.when(m == 0)
    def _():
        edge_ref[...] = jnp.zeros_like(edge_ref) if first == 0 else rest[5 if far else 2][...]

    @pl.when(own)
    def _():
        for e in range(2):
            pair[e] = own_ref[e]

    @pl.when(jnp.logical_not(own))
    def _():
        if far:
            cur = unpack_rows(rest[0][0].astype(F32), 576).astype(BF)
            prev = unpack_rows(rest[1][0].astype(F32), 576).astype(BF)
            prev = jnp.where(m + first > 0, prev, jnp.zeros_like(prev))
            for e, part in enumerate(first_diffs(rest[3][...], cur, prev)):
                pair[e] = (part * unpack_rows(rest[2][0, e].astype(F32), 640)).astype(BF)
        else:
            for e in range(2):
                pair[e] = unpack_rows(rest[0][0, e].astype(F32), 640).astype(BF)

    if last:
        inside = m < pl.num_programs(0) - 1
        for e in range(2):
            pair[e] = jnp.where(inside, pair[e], jnp.zeros((640, LANES), BF))
    frame_rows(pair[0], edge_ref[...], t1b[...], o_ref, 0, rows)
    if last:

        @pl.when(inside)
        def _():
            frame_rows(pair[1], pair[0], t1b[...], o_ref, 4, rows)

    else:
        frame_rows(pair[1], pair[0], t1b[...], o_ref, 4, rows)
    edge_ref[...] = pair[1]


def dframes(flag, own, got, t1b, rows, first, count, edge, out):
    far = len(got) > 1
    last = first + count == 10
    at = lambda m: jnp.minimum(m, count - 1)
    fixed = lambda shape: pl.BlockSpec(shape, lambda *_: (0,) * len(shape))
    ins = [flag, own]
    in_specs = [pl.BlockSpec((2, 640, LANES), lambda m, *_: (0, 0, at(m) + first))]
    if far:
        r2p, s1p, t2b = got
        ins += [r2p, r2p, s1p, t2b]
        in_specs += [
            pl.BlockSpec((1, 1008, 128), lambda m, *_: (m + first, 0, 0)),
            pl.BlockSpec((1, 1008, 128), lambda m, *_: (jnp.maximum(m + first - 1, 0), 0, 0)),
            pl.BlockSpec((1, 2, 1120, 128), lambda m, *_: (m, 0, 0, 0)),
            fixed((640, 768)),
        ]
    else:
        ins.append(got[0])
        in_specs.append(pl.BlockSpec((1, 2, 1120, 128), lambda m, *_: (at(m), 0, 0, 0)))
    ins.append(t1b)
    in_specs.append(fixed((224, 512)))
    aliases = {}
    if first:
        ins += [edge, out]
        in_specs += [fixed((640, LANES)), pl.BlockSpec(memory_space=pl.ANY)]
        aliases = {len(ins) - 1: 0}
    return pl.pallas_call(
        functools.partial(dframes_kernel, rows, first, last, far),
        out_shape=(sds((84, 84, 2, rows), BF), sds((640, LANES), BF)),
        grid_spec=pltpu.PrefetchScalarGridSpec(
            num_scalar_prefetch=1,
            grid=(count + 1 if last else count,),
            in_specs=in_specs,
            out_specs=[pl.BlockSpec((8, 84, 2, rows), lambda m, *_: (m + first, 0, 0, 0)), fixed((640, LANES))],
            scratch_shapes=[pltpu.VMEM((2, 640, LANES), BF)],
        ),
        input_output_aliases=aliases,
        compiler_params=pltpu.CompilerParams(vmem_limit_bytes=VMEM_BIG),
        cost_estimate=cost(0.03 * count),
    )(*ins)


def wdense_kernel(flag_ref, a_ref, rd_ref, rh_ref, h_ref, keep_ref, send_ref):
    core = flag_ref[1]
    grads = []
    for left, right in ((a_ref, rd_ref), (rh_ref, h_ref)):
        grads.append((dot_nt(left[...], right[...]) * (1.0 / LOSS_SCALE)).astype(BF))
    start = 0
    for grad in grads:
        size = grad.shape[0]
        for half in range(2):
            tile0 = grad[:, 256 * half : 256 * half + 128]
            tile1 = grad[:, 256 * half + 128 : 256 * half + 256]
            keep_ref[0, half, start : start + size, :] = jnp.where(core == 0, tile0, tile1)
            send_ref[0, half, start : start + size, :] = jnp.where(core == 0, tile1, tile0)
        start += size


def wdense(flag, a3, rd, rh, h):
    out = pl.BlockSpec((1, 2, 512, 128), lambda i, *_: (i, 0, 0, 0))
    return pl.pallas_call(
        wdense_kernel,
        out_shape=(sds((8, 2, 512, 128), BF), sds((8, 2, 512, 128), BF)),
        grid_spec=pltpu.PrefetchScalarGridSpec(
            num_scalar_prefetch=1,
            grid=(8,),
            in_specs=[
                pl.BlockSpec((392, LANES), lambda i, *_: (i, 0)),
                whole((512, LANES)),
                pl.BlockSpec((120, LANES), lambda i, *_: (i, 0)),
                whole((512, LANES)),
            ],
            out_specs=[out, out],
        ),
        compiler_params=pltpu.CompilerParams(vmem_limit_bytes=VMEM_BIG),
        cost_estimate=cost(1),
    )(flag, a3, rd, rh, h)


def wconv3_kernel(*refs):
    columns, (r_ref, g_ref, acc) = refs[:4], refs[4:]
    q = pl.program_id(0)

    @pl.when(q == 0)
    def _():
        acc[...] = jnp.zeros_like(acc)

    left = jnp.concatenate([ref[:, LANES * u : LANES * (u + 7)] for u in range(3) for ref in columns], axis=0)
    last = jnp.where(q < 3, r_ref[:, 64:, :], jnp.zeros((7, 64, LANES), BF))
    right = jnp.concatenate([jnp.concatenate([r_ref[i, :64], last[i]], axis=0) for i in range(7)], axis=1)
    acc[...] += dot_nt(left, right)

    @pl.when(q == 3)
    def _():
        for u in range(3):
            for v in range(3):
                at = 256 * u + 64 * v
                part = acc[at : at + 64, :64] + acc[at + 64 : at + 128, 64:]
                g_ref[:, 192 * u + 64 * v : 192 * u + 64 * v + 64] = part.T * (1.0 / LOSS_SCALE)


def wconv3(a2, r3):
    return call(
        wconv3_kernel,
        sds((64, 576), F32),
        [pl.BlockSpec((64, 9 * LANES), lambda q, k=k: (jnp.minimum(2 * q + k, 8), 0)) for k in range(4)]
        + [pl.BlockSpec((7, 128, LANES), lambda q: (0, q, 0))],
        whole((64, 576)),
        us=6,
        grid=(4,),
        scratch=[pltpu.VMEM((768, 128), F32)],
    )(a2, a2, a2, a2, r3.reshape(7, 448, LANES))


def wconv2_kernel(a0_ref, a1_ref, r_ref, g_ref, acc):
    q = pl.program_id(0)

    @pl.when(q == 0)
    def _():
        acc[...] = jnp.zeros_like(acc)

    left = jnp.concatenate(
        [ref[e, :, LANES * t : LANES * (t + 9)] for t in range(2) for e in range(2) for ref in (a0_ref, a1_ref)],
        axis=0,
    )
    last = jnp.where(q < 4, r_ref[64:, :], jnp.zeros((64, 9 * LANES), BF))
    acc[...] += dot_nt(left, jnp.concatenate([r_ref[:64, :], last], axis=0))

    @pl.when(q == 4)
    def _():
        for u in range(4):
            at = 192 * u
            g_ref[128 * u : 128 * u + 128, :] = (acc[at : at + 128, :64] + acc[at + 64 : at + 192, 64:]) * (
                1.0 / LOSS_SCALE
            )


def wconv2(a1, r2):
    return call(
        wconv2_kernel,
        sds((512, 64), F32),
        [
            pl.BlockSpec((2, 128, 10 * LANES), lambda q: (0, q, 0)),
            pl.BlockSpec((2, 64, 10 * LANES), lambda q: (0, jnp.minimum(2 * q + 2, 9), 0)),
            pl.BlockSpec((128, 9 * LANES), lambda q: (q, 0)),
        ],
        whole((512, 64)),
        us=8,
        grid=(5,),
        scratch=[pltpu.VMEM((768, 128), F32)],
    )(a1, a1, r2)


def wconv1_kernel(x_ref, x0_ref, r_ref, g_ref, acc, before):
    step = pl.program_id(0)

    @pl.when(step == 0)
    def _():
        acc[...] = jnp.zeros_like(acc)
        before[...] = x0_ref[...]

    def column(dy, rows, c):
        if c:
            return x_ref[dy, rows, LANES * (c - 1) : LANES * c]
        return before[dy, rows, :]

    total = acc[...]
    for g in range(5):
        rows = slice(64 * g, 64 * g + 80)
        left = jnp.concatenate(
            [
                jnp.concatenate([column(dy, rows, ii + t) for ii in range(4)], axis=1)
                for t in range(2)
                for dy in range(4)
            ],
            axis=0,
        )
        right = jnp.concatenate(
            [r_ref[ii % 2, 128 * g : 128 * g + 128, LANES * (ii // 2) : LANES * (ii // 2 + 1)] for ii in range(4)],
            axis=1,
        )
        total = total + dot_nt(left, right)
    acc[...] = total
    before[...] = x_ref[:, :, 3 * LANES :]

    @pl.when(step == 4)
    def _():
        for dy in range(8):
            part = jnp.zeros((32, 32), F32)
            for jj in range(4):
                part = part + acc[80 * dy + 16 * jj : 80 * dy + 16 * jj + 32, 32 * jj : 32 * jj + 32]
            g_ref[32 * dy : 32 * dy + 32, :] = part * (1.0 / LOSS_SCALE)


def wconv1(xt, x0, r1):
    return call(
        wconv1_kernel,
        sds((256, 32), F32),
        [
            pl.BlockSpec((4, 336, 4 * LANES), lambda s: (0, 0, s)),
            whole((4, 336, LANES)),
            pl.BlockSpec((2, 640, 2 * LANES), lambda s: (0, 0, s)),
        ],
        whole((256, 32)),
        us=14,
        grid=(5,),
        scratch=[pltpu.VMEM((640, 128), F32), pltpu.VMEM((4, 336, LANES), BF)],
    )(xt, x0, r1)


SMALL_ROWS = 704


def lanes_of(shards):
    return max(1, 128 // shards)


def slot_rows(capacity):
    return (capacity + 7) // 8 * 8


def pack_kernel(shards, capacity, flag_ref, *refs):
    b1_refs, (b2_ref, b3_ref, g1_ref, g2_ref, g3_ref, db_ref, hb_ref, loss_ref, owner_ref, p_ref, w) = refs[:-11], refs[-11:]
    scale = 1.0 / LOSS_SCALE
    w[...] = jnp.zeros_like(w)
    for k in range(4):
        w[64 * k : 64 * k + 64, :] = g3_ref[:, 128 * k : 128 * k + 128]
    w[256:320, :64] = g3_ref[:, 512:]
    w[320:576, :64] = g2_ref[:256, :]
    w[320:576, 64:] = g2_ref[256:, :]
    w[576:704, :32] = g1_ref[:128, :]
    w[576:704, 32:64] = g1_ref[128:, :]
    total = b1_refs[0][...]
    for ref in b1_refs[1:]:
        total = total + ref[...]
    for column, value in ((64, total), (65, b2_ref[...]), (66, b3_ref[...])):
        w[576 : 576 + value.shape[0], column : column + 1] = jnp.sum(value, axis=1, keepdims=True) * scale
    for k in range(4):
        w[576:704, 67 + k : 68 + k] = db_ref[128 * k : 128 * k + 128, :] * scale
    for half in range(2):
        for k in range(4):
            start = 459 * half + 128 * k
            size = min(128, 459 * (half + 1) - start)
            w[576 : 576 + size, 71 + 4 * half + k : 72 + 4 * half + k] = hb_ref[start : start + size, :]

    owner = owner_ref[...]
    rows = owner.shape[1]
    owner_f = owner.astype(F32)
    down = jnp.broadcast_to(owner_f, (8, rows)).T[:, :1]
    same = (down == owner_f) & (
        lax.broadcasted_iota(jnp.int32, (rows, rows), 0) < lax.broadcasted_iota(jnp.int32, (rows, rows), 1)
    )
    slot = jnp.sum(same.astype(F32), axis=0, keepdims=True)
    group, height = lanes_of(shards), slot_rows(capacity)
    place = lax.broadcasted_iota(jnp.int32, (height, rows), 0).astype(F32)
    spread = jnp.where(place == slot, loss_ref[...], 0.0).astype(BF)
    lane = lax.broadcasted_iota(jnp.int32, (128, rows), 0)
    here = shards * lax.rem(owner, group) + flag_ref[2]
    for g in range(shards // group):
        hot = ((lane == here) & (owner // group == g)).astype(BF)
        w[SMALL_ROWS + height * g : SMALL_ROWS + height * g + height, :] = dot_nt(spread, hot)
    p_ref[...] = w[...].astype(BF)


def pack(flag, b1s, shards, capacity, *ins):
    total = SMALL_ROWS + shards // lanes_of(shards) * slot_rows(capacity)
    ins = tuple(b1s) + ins
    return call(
        functools.partial(pack_kernel, shards, capacity),
        sds((total, 128), BF),
        [pl.BlockSpec(memory_space=pltpu.SMEM)] + [whole(a.shape) for a in ins],
        whole((total, 128)),
        scratch=[pltpu.VMEM((total, 128), F32)],
        us=0.1,
    )(flag, *ins)


def split_kernel(shards, capacity, flag_ref, own_ref, got_ref, k1, b1, k2, b2, k3, b3, db, hb, prio, w):
    own = flag_ref[0] == 1
    w[...] = jnp.where(own, own_ref[...].astype(F32), got_ref[...].astype(F32))

    def pick(low, high):
        return jnp.where(own, low, high)

    k1[...] = pick(w[576:704, :32], w[576:704, 32:64])
    k2[...] = pick(w[320:576, :64], w[320:576, 64:])
    for n in range(9):
        rows = slice(64 * (n // 2), 64 * (n // 2) + 64)
        part = w[rows, 64 * (n % 2) : 64 * (n % 2) + 64]
        k3[n] = pick(part[:32], part[32:])
    columns = w[576:704, :].T
    b1[...] = pick(columns[64:65, :16], columns[64:65, 16:32])
    for ref, at in ((b2, 65), (b3, 66)):
        ref[...] = pick(columns[at : at + 1, :32], columns[at : at + 1, 32:64])
    for k in range(2):
        db[:, 128 * k : 128 * k + 128] = pick(columns[67 + k : 68 + k], columns[69 + k : 70 + k])
    for k in range(4):
        size = min(128, 459 - 128 * k)
        hb[:, 128 * k : 128 * k + size] = pick(columns[71 + k : 72 + k, :size], columns[75 + k : 76 + k, :size])
    group, height = lanes_of(shards), slot_rows(capacity)
    me = flag_ref[2]
    block = w[pl.ds(pl.multiple_of(SMALL_ROWS + height * (me // group), 8), height), :]
    if group > 1:
        block = pltpu.roll(block, lax.rem(128 - shards * lax.rem(me, group), 128), 1)
    half = capacity // 2
    prio[:, 0, :] = pick(block[:half, :shards], block[half : 2 * half, :shards])


def split(flag, own, got, shards, capacity):
    shapes = (
        (128, 32),
        (1, 16),
        (256, 64),
        (1, 32),
        (9, 32, 64),
        (1, 32),
        (1, 256),
        (1, 459),
        (capacity // 2, 1, shards),
    )
    return call(
        functools.partial(split_kernel, shards, capacity),
        tuple(sds(s, F32) for s in shapes),
        [pl.BlockSpec(memory_space=pltpu.SMEM), whole(own.shape), whole(got.shape)],
        [whole(s) for s in shapes],
        scratch=[pltpu.VMEM(own.shape, F32)],
        us=2,
    )(flag, own, got)


def unchunk_kernel(flag_ref, cur_ref, other_ref, d_ref, h_ref):
    core, code = flag_ref[1], flag_ref[3]
    for k in range(2):
        block = (2 * pl.program_id(0) + k) ^ code
        cur, other = cur_ref[block].astype(F32), other_ref[block].astype(F32)
        for lane, tile in enumerate((jnp.where(core == 0, cur, other), jnp.where(core == 0, other, cur))):
            d_ref[392 * k : 392 * k + 392, 128 * lane : 128 * lane + 128] = tile[:392]
            h_ref[120 * k : 120 * k + 120, 128 * lane : 128 * lane + 128] = tile[392:]


def unchunk(flag, cur, other):
    return call(
        unchunk_kernel,
        (sds((3136, 256), F32), sds((LOGITS, 256), F32)),
        [pl.BlockSpec(memory_space=pltpu.SMEM), whole(cur.shape), whole(other.shape)],
        [pl.BlockSpec((784, 256), lambda i: (i, 0)), pl.BlockSpec((240, 256), lambda i: (i, 0))],
        us=4,
        grid=(4,),
    )(flag, cur, other)


def after(value, *others):
    return lax.optimization_barrier((value,) + others)[0]


def hand(value):
    return lax.ppermute(value, "pair", [(0, 1)])


def swap(value, bit):
    devices = lax.axis_size("batch")
    return lax.ppermute(value, "batch", [(i, i ^ bit) for i in range(devices)])


def add(left, right):
    return (left.astype(F32) + right.astype(F32)).astype(BF)


def split_blocks(cur):
    devices = lax.axis_size("batch")
    spread = devices // 16
    if spread > 1:
        cur = cur.reshape(8, 2, spread, 512 // spread, 128).transpose(0, 2, 1, 3, 4)
        cur = cur.reshape(devices // 2, 2, 512 // spread, 128)
    return cur


def halve(cur, me, bit):
    mine = (me // bit) % 2
    pairs = cur.reshape((cur.shape[0] // 2, 2) + cur.shape[1:])
    send = lax.dynamic_index_in_dim(pairs, 1 - mine, axis=1, keepdims=False)
    keep = lax.dynamic_index_in_dim(pairs, mine, axis=1, keepdims=False)
    return keep, swap(send, bit)


def unmix(blocks, code):
    bit = 1
    while bit < blocks.shape[0]:
        pairs = blocks.reshape((-1, 2, bit) + blocks.shape[1:])
        blocks = jnp.where((code // bit) % 2 == 1, pairs[:, ::-1], pairs).reshape(blocks.shape)
        bit *= 2
    return blocks


def join(cur, other):
    return jnp.stack([cur, other], axis=1).reshape((2 * cur.shape[0],) + cur.shape[1:])


def local(
    frames,
    kernel_first,
    bias_first,
    kernel_second,
    bias_second,
    kernel_third,
    bias_third,
    dense_weight,
    dense_bias,
    head_weight,
    head_bias,
    taken_actions,
    greedy_actions,
    done_flags,
    bin_lower,
    bin_fraction,
    owner_shard,
):
    online = lax.axis_index("pair") == 0
    me = lax.axis_index("batch")
    shards = lax.axis_size("batch")
    rows = frames.shape[1]
    capacity = 2 * ((rows + shards - 1) // shards)
    block = me // 2 if shards == 16 else me * 0
    flag = jnp.stack([online.astype(jnp.int32), me % 2, me, block]).astype(jnp.int32)
    xv = frames[0].transpose(2, 3, 1, 0)
    k1, k2, k3 = kernel_first[0], kernel_second[0], kernel_third[0]
    ones = jnp.zeros((16, LANES), BF).at[0].set(1)
    t1, t2, t3, t3b, t2b, b2, kernels = bands(k1, bias_first, k2, bias_second, k3, bias_third)

    kernels = hand(kernels)
    a1, s1, xt, early, x0 = conv1(xv, t1, ones, 0, EARLY, ())
    early = hand(after(early, kernels))
    a1, s1, xt, late = conv1(xv, t1, ones, EARLY, 10, (a1, s1, xt))
    late = hand(late)
    a2, s2, a3, s3 = conv23(a1, t2, b2, t3, ones)
    wd = dense_weight[0]
    wht = head_weight[0].T
    pd = lax.dot_general(wd, a3, (((0,), (0,)), ((), ())), preferred_element_type=F32)
    taken = taken_actions[None, :]
    sel = jnp.where(online, taken, greedy_actions[None, :])
    h, sd, lp, cho = head(pd, dense_bias, wht, head_bias, sel)
    cho = lax.ppermute(cho, "pair", [(1, 0)])
    row_loss, rh, hb = loss(cho, done_flags[None, :], bin_lower.T, bin_fraction.T, lp, taken)

    diff_dense = lax.dot_general(wht, rh, (((0,), (0,)), ((), ())), preferred_element_type=F32)
    diff_dense = diff_dense * (0.5 * sd.astype(F32))
    rd = diff_dense.astype(BF)
    db = jnp.sum(diff_dense, axis=1, keepdims=True)

    keep, send = wdense(flag, a3, after(rd, early), rh, h)
    cur = split_blocks(add(keep, swap(send, 1)))
    keep, got = halve(cur, me, 2)

    r3, b3g, r2, r2p, b2g = dthird(wd, rd, s3, t3b, s2)
    r2p = hand(r2p)
    r1, near0, near1, b1g = dconv2(r2, t2b, s1, FAR, 10 - FAR, True, None)
    cur = add(after(keep, b1g), got)
    keep, far = halve(cur, me, 4)
    r1, b1g_far = dconv2(after(r2, got, late), t2b, s1, 0, FAR, False, r1)
    b1s = [b1g, b1g_far]
    g3 = wconv3(a2, after(r3, b1g_far))
    bit = 4
    while 2 * bit < shards:
        cur = add(after(keep, g3) if bit == 4 else keep, far)
        bit *= 2
        keep, far = halve(cur, me, bit)
    g1 = wconv1(xt, x0, after(r1, g3))
    chunk = add(after(keep, g1), far)[0]
    far_chunk = hand(chunk[1])
    gots = [hand(after(near0, far))]
    gots.append(hand(after(near1, gots[0])))
    t1b, t2b_online = band_frames(after(flag, g1), k1, k2, kernels)
    mine = jnp.where(online, chunk[0], far_chunk)
    g2 = wconv2(a1, after(r2, mine, t1b))

    parts = [early, late] + gots
    firsts = [0, EARLY] + [first for first, _ in NEAR]
    out, edge = None, None

    def frames_step(n, *waits):
        extra = (r2p, parts[n], t2b_online) if n < 2 else (parts[n],)
        return dframes(flag, after(r1, *waits), extra, t1b, rows, firsts[n], parts[n].shape[0], edge, out)

    bit = shards // 2
    cur = mine[None]
    part = swap(cur, bit)
    small = pack(after(flag, part, r2p), b1s, shards, capacity, b2g, b3g, g1, g2, g3, db, hb, row_loss, owner_shard.T)
    cur = join(cur, part)
    part = swap(cur, bit // 2)
    small = add(small, swap(small, 1))
    got = swap(small, 2)
    out, edge = frames_step(0, cur, small)
    cur = join(after(cur, edge), part)
    small = add(after(small, edge), got)
    part_y, got_z = swap(cur, bit // 4), swap(small, 4)
    out, edge = frames_step(1, cur, small, gots[0])
    small = add(after(small, edge), got_z)
    got = swap(small, 8)
    out, edge = frames_step(2, small)
    cur = join(after(cur, edge), part_y)
    small = add(after(small, edge), got)
    lower = 16
    while lower < shards:
        small = add(small, swap(small, lower))
        cur = join(cur, swap(cur, 2 * bit // lower))
        lower *= 2
    other = swap(cur, 1)
    far_small = hand(after(small, gots[1]))
    out, edge = frames_step(3, cur, small)
    if shards != 16:
        cur, other = (unmix(v, me // 2).reshape(8, 512, 128) for v in (cur, other))
    dense_out, head_out = unchunk(flag, cur, other)
    o = split(flag, small, far_small, shards, capacity)
    return (
        o[0].reshape(4, 8, 4, 32),
        o[1].reshape(16),
        o[2].reshape(2, 4, 32, 64),
        o[3].reshape(32),
        o[4].reshape(3, 3, 32, 64).transpose(0, 1, 3, 2),
        o[5].reshape(32),
        dense_out,
        o[6].reshape(256),
        head_out.T,
        o[7].reshape(459),
        out.transpose(3, 2, 0, 1),
        o[8].transpose(1, 2, 0),
    )


def solution(mesh):
    return jax.shard_map(
        local,
        mesh=mesh,
        in_specs=(
            P("pair", "batch", None, None, None),
            P("pair", None, None, None, None),
            P("pair", None),
            P("pair", None, None, None, None),
            P("pair", None),
            P("pair", None, None, None, None),
            P("pair", None),
            P("pair", None, None),
            P("pair", None),
            P("pair", None, None),
            P("pair", None),
            P("batch"),
            P("batch"),
            P("batch"),
            P("batch", None),
            P("batch", None),
            P("batch", None),
        ),
        out_specs=(
            P("pair", None, None, None),
            P("pair"),
            P("pair", None, None, None),
            P("pair"),
            P(None, None, None, "pair"),
            P("pair"),
            P(None, "pair"),
            P("pair"),
            P("pair", None),
            P("pair"),
            P("batch", "pair", None, None),
            P("batch", None, "pair"),
        ),
        check_vma=False,
    )
```

```python
import functools

import jax
import jax.numpy as jnp
from jax import lax
from jax.experimental import pallas as pl
from jax.experimental.pallas import tpu as pltpu
from jax.sharding import PartitionSpec as P

ACT = 18
ATOMS = 51
LOGITS = ACT * ATOMS
LOSS_SCALE = 256
LANES = 256
BF = jnp.bfloat16
F32 = jnp.float32
VMEM_BIG = 24 << 20
FAR = 6
EARLY = 3
ALONE = 1
NEAR = ((6, 4),)


def cost(us):
    return pl.CostEstimate(flops=int(us * 0.4e9), bytes_accessed=0, transcendentals=0)


def call(kernel, out, ins, outs, us, grid=None, scratch=()):
    return pl.pallas_call(
        kernel,
        out_shape=out,
        grid=() if grid is None else grid,
        in_specs=ins,
        out_specs=outs,
        scratch_shapes=list(scratch),
        compiler_params=pltpu.CompilerParams(vmem_limit_bytes=VMEM_BIG),
        cost_estimate=cost(us),
    )


def whole(shape):
    return pl.BlockSpec(shape, lambda *_: (0,) * len(shape))


def hbm(value):
    return pltpu.with_memory_space_constraint(value, pltpu.HBM)


def sds(shape, dtype):
    return jax.ShapeDtypeStruct(shape, dtype)


def dot(left, right):
    return jnp.dot(left, right, preferred_element_type=F32)


def dot_nt(left, right):
    return lax.dot_general(left, right, (((1,), (1,)), ((), ())), preferred_element_type=F32)


def act_slope(half):
    tan = jnp.tanh(half)
    up = 1.0 + tan
    act = half * up
    return act, up + act * (1.0 - tan)


def second_bands(k2n, w2b):
    for e in range(2):
        for t in range(2):
            u = 2 * t + e
            for j in range(6):
                lo = max(0, 2 * j - 2)
                hi = min(10, 2 * j + 2)
                v0 = lo - (2 * j - 2)
                w2b[320 * e + 32 * lo : 320 * e + 32 * hi, 384 * t + 64 * j : 384 * t + 64 * j + 64] = k2n[
                    128 * u + 32 * v0 : 128 * u + 32 * (v0 + hi - lo), :
                ]


def turned(kernel, bias=None):
    flat = kernel[...].astype(F32)
    flat = flat.reshape(-1, flat.shape[-1])
    if bias is not None:
        bias = jnp.broadcast_to(bias[...].astype(F32), (8, flat.shape[1])).T[:, :1]
    return flat, flat.T, bias


def bands_kernel(k1, b1, k2, b2, k3, b3, t1, t2, t3, b2c, send, w1, w2, w3):
    for ref in (w1, w2, w3):
        ref[...] = jnp.zeros_like(ref)
    _, k1t, b1c = turned(k1, b1)
    k2n, k2t, b2t = turned(k2, b2)
    _, k3t, b3c = turned(k3, b3)
    send[:512, :] = k2n.astype(BF)
    send[512:, :32] = k1[:, :, 2:, :].astype(F32).reshape(128, 32).astype(BF)
    send[512:, 32:] = jnp.zeros((128, 32), BF)
    for jj in range(10):
        for dy in range(8):
            w1[32 * jj : 32 * jj + 32, 176 * dy + 16 * jj : 176 * dy + 16 * jj + 32] = k1t[:, 32 * dy : 32 * dy + 32]
        w1[32 * jj : 32 * jj + 32, 1408:1409] = b1c
    for jj in range(3):
        for u in range(4):
            w2[64 * jj : 64 * jj + 64, 256 * u + 64 * jj : 256 * u + 64 * jj + 128] = k2t[:, 128 * u : 128 * u + 128]
        b2c[64 * jj : 64 * jj + 64, :] = 0.5 * b2t
    for j in range(7):
        for u in range(3):
            w3[64 * j : 64 * j + 64, 576 * u + 64 * j : 576 * u + 64 * j + 192] = k3t[:, 192 * u : 192 * u + 192]
        w3[64 * j : 64 * j + 64, 1728:1729] = b3c
    t1[...] = (0.5 * w1[...]).astype(BF)
    t2[...] = (0.5 * w2[...]).astype(BF)
    t3[...] = (0.5 * w3[...]).astype(BF)


def bands(*ins):
    shapes = ((320, 1424), (192, 1024), (448, 1744))
    return call(
        bands_kernel,
        (sds(shapes[0], BF), pltpu.HBM(shapes[1], BF), pltpu.HBM(shapes[2], BF), sds((192, 1), F32), pltpu.HBM((640, 64), BF)),
        [whole(a.shape) for a in ins],
        [whole(s) for s in shapes] + [whole((192, 1)), whole((640, 64))],
        us=3,
        scratch=[pltpu.VMEM(s, F32) for s in shapes],
    )(*[hbm(v) for v in ins])


def bands_back_kernel(flag_ref, k1, k2, k3, got, t3b, t2b, t2o, t1b, w3b, w2b, w1b):
    own = flag_ref[0] == 1
    for ref in (w3b, w2b, w1b):
        ref[...] = jnp.zeros_like(ref)
    k3n, k2n = turned(k3)[0], turned(k2)[0]
    for j in range(7):
        for u in range(3):
            w3b[64 * j : 64 * j + 192, 448 * (2 - u) + 64 * j : 448 * (2 - u) + 64 * j + 64] = k3n[192 * u : 192 * u + 192, :]
    t3b[...] = (0.5 * w3b[...]).astype(BF)
    second_bands(k2n, w2b)
    t2b[...] = (0.5 * w2b[...]).astype(BF)
    second_bands(jnp.where(own, k2n, got[:512, :].astype(F32)), w2b)
    t2o[...] = (0.5 * w2b[...]).astype(BF)
    half = jnp.where(own, k1[:, :, :2, :].astype(F32).reshape(128, 32), got[512:, :32].astype(F32)).reshape(8, 16, 32)
    for dy in range(8):
        t, row = divmod(dy, 4)
        for j in range(8):
            lo = max(0, 4 * j - 4)
            hi = min(28, 4 * j + 4)
            d0 = lo - (4 * j - 4)
            w1b[56 * row + 2 * lo : 56 * row + 2 * hi, 256 * t + 32 * j : 256 * t + 32 * j + 32] = half[
                dy, 2 * d0 : 2 * (d0 + hi - lo), :
            ]
    t1b[...] = w1b[...].astype(BF)


def bands_back(flag, *ins):
    shapes = ((576, 1344), (640, 768), (640, 768), (224, 512))
    return call(
        bands_back_kernel,
        tuple(pltpu.HBM(s, BF) for s in shapes),
        [pl.BlockSpec(memory_space=pltpu.SMEM)] + [whole(a.shape) for a in ins],
        [whole(s) for s in shapes],
        us=4,
        scratch=[pltpu.VMEM(s, F32) for s in (shapes[0], shapes[1], shapes[3])],
    )(flag, *[hbm(v) for v in ins])


def pack_rows(part, n):
    lane = lax.broadcasted_iota(jnp.int32, (n // 4, 128), 1)
    tail = [part[n // 4 * k : n // 4 * (k + 1), 128:] for k in range(4)]
    packed = [jnp.where(lane < 96, tail[k], pltpu.roll(tail[3], 96 - 32 * k, 1)) for k in range(3)]
    return jnp.concatenate([part[:, :128]] + packed, axis=0)


def unpack_rows(packed, n):
    lane = lax.broadcasted_iota(jnp.int32, (n // 4, 128), 1)
    tail = [packed[n + n // 4 * k : n + n // 4 * (k + 1)] for k in range(3)]
    last = pltpu.roll(tail[0], 32, 1)
    last = jnp.where(lane < 32, last, jnp.where(lane < 64, pltpu.roll(tail[1], 64, 1), pltpu.roll(tail[2], 96, 1)))
    return jnp.concatenate([packed[:n], jnp.concatenate(tail + [last], axis=0)], axis=1)


def conv1_kernel(rows, start, packs, first_ref, xa_ref, xb_ref, t1_ref, ones_ref, *rest):
    cells = rest[-1]
    a_ref, s_ref, xt_ref, p_ref = rest[-5:-1] if start else rest[-6:-2]
    m = pl.program_id(0) + start

    def relay(ref, slot):
        for dy in range(4):
            cells[slot, dy, :, :rows] = ref[dy].reshape(336, rows)

    @pl.when(m == start)
    def _():
        cells[...] = jnp.zeros_like(cells)
        relay(first_ref, 0)
        if not start:
            rest[-2][...] = cells[0]

    relay(xa_ref, 1)
    relay(xb_ref, 2)
    slopes = []
    for e in range(2):
        parts_of = lambda window, e=e: [cells[e + t, dy, window, :] for t in range(2) for dy in range(4)]
        row = []
        for g in range(2):
            half = dot(t1_ref[...], jnp.concatenate(parts_of(pl.ds(160 * g, 176)) + [ones_ref[...]], axis=0))
            act, slope = act_slope(half)
            a_ref[e, 320 * g : 320 * g + 320, :] = act.astype(BF)
            s_ref[e, 320 * g : 320 * g + 320, :] = slope.astype(BF)
            row.append(slope)
        slopes.append(row)
    if not start:
        for e in range(2):
            p_ref[0, e] = pack_rows(jnp.concatenate(slopes[e], axis=0), 640).astype(BF)
    for dy in range(4):
        xt_ref[dy, :, :LANES] = cells[1, dy]
        xt_ref[dy, :, LANES:] = cells[2, dy]
        cells[0, dy] = cells[2, dy]
    if start:

        @pl.when(m < packs)
        def _():
            for e in range(2):
                p_ref[0, e] = pack_rows(s_ref[e].astype(F32), 640).astype(BF)


def conv1(xv, t1, ones, start, stop, before):
    rows = xv.shape[3]
    packs = min(stop, FAR)
    cell = lambda f: pl.BlockSpec((4, 84, 4, rows), lambda m: (f(m + start), 0, 0, 0))
    out = pl.BlockSpec((2, 640, LANES), lambda m: (0, 0, m + start))
    outs = [
        out,
        out,
        pl.BlockSpec((4, 336, 2 * LANES), lambda m: (0, 0, m + start)),
        pl.BlockSpec((1, 2, 1120, 128), lambda m: (jnp.minimum(m, packs - start - 1), 0, 0, 0)),
    ]
    shapes = [
        pltpu.HBM((2, 640, 10 * LANES), BF),
        pltpu.HBM((2, 640, 10 * LANES), BF),
        pltpu.HBM((4, 336, 20 * LANES), BF),
        pltpu.HBM((packs - start, 2, 1120, 128), BF),
    ]
    if not start:
        outs.append(whole((4, 336, LANES)))
        shapes.append(pltpu.HBM((4, 336, LANES), BF))
    return pl.pallas_call(
        functools.partial(conv1_kernel, rows, start, packs),
        out_shape=tuple(shapes),
        grid=(stop - start,),
        in_specs=[
            pl.BlockSpec((4, 84, 4, rows), lambda m: (2 * start, 0, 0, 0)),
            cell(lambda m: 2 * m + 1),
            cell(lambda m: 2 * m + 2),
            whole((320, 1424)),
            whole((16, LANES)),
        ]
        + [pl.BlockSpec(memory_space=pl.ANY)] * len(before),
        out_specs=outs,
        scratch_shapes=[pltpu.VMEM((3, 4, 336, LANES), BF)],
        input_output_aliases={5 + n: n for n in range(len(before))},
        compiler_params=pltpu.CompilerParams(vmem_limit_bytes=VMEM_BIG),
        cost_estimate=cost(0.02 * (stop - start)),
    )(hbm(xv), hbm(xv), hbm(xv), t1, ones, *[hbm(v) for v in before])


def conv23_kernel(r0_ref, r1_ref, t2_ref, b2_ref, t3_ref, ones_ref, a2_ref, s2_ref, a3_ref, s3_ref, keep):
    g = pl.program_id(0)

    def third():
        window = pl.ds(pl.multiple_of(576 * (g - 3), 64), 1728)
        half = dot(t3_ref[...], jnp.concatenate([keep[window, :], ones_ref[...]], axis=0))
        act, slope = act_slope(half)
        a3_ref[...] = act.astype(BF)
        s3_ref[...] = slope.astype(BF)

    def second():
        for n in range(3):
            window = pl.ds(192 * n, 256)
            parts = [r0_ref[0, window, :], r0_ref[1, window, :], r1_ref[0, window, :], r1_ref[1, window, :]]
            half = dot(t2_ref[...], jnp.concatenate(parts, axis=0)) + b2_ref[...]
            act, slope = act_slope(half)
            act = act.astype(BF)
            a2_ref[192 * n : 192 * n + 192, :] = act
            keep[pl.ds(pl.multiple_of(576 * g + 192 * n, 64), 192), :] = act
            s2_ref[192 * n : 192 * n + 192, :] = slope.astype(BF)

    @pl.when(g < 3)
    def _():
        second()

    @pl.when((g >= 3) & (g < 9))
    def _():
        third()
        second()

    @pl.when(g == 9)
    def _():
        third()


def conv23(a1, t2, b2, t3, ones):
    row = lambda t: pl.BlockSpec((2, 640, LANES), lambda g: (0, 0, jnp.minimum(g, 8) + t))
    out2 = pl.BlockSpec((576, LANES), lambda g: (0, jnp.minimum(g, 8)))
    out3 = pl.BlockSpec((448, LANES), lambda g: (jnp.maximum(g - 3, 0), 0))
    return call(
        conv23_kernel,
        (pltpu.HBM((576, 9 * LANES), BF), pltpu.HBM((576, 9 * LANES), BF), sds((3136, LANES), BF), pltpu.HBM((3136, LANES), BF)),
        [row(0), row(1), whole((192, 1024)), whole((192, 1)), whole((448, 1744)), whole((16, LANES))],
        [out2, out2, out3, out3],
        us=14,
        grid=(10,),
        scratch=[pltpu.VMEM((9 * 576, LANES), BF)],
    )(hbm(a1), hbm(a1), hbm(t2), b2, hbm(t3), ones)


def head_kernel(rows, pd_ref, bd_ref, wh_ref, bh_ref, sel_ref, act_ref, slope_ref, lp_ref, cho_ref, lg_ref):
    bd = jnp.broadcast_to(bd_ref[...].astype(F32), (8, 512)).T[:, :1]
    bh = jnp.broadcast_to(bh_ref[...].astype(F32), (8, LOGITS)).T[:, :1]
    act, slope = act_slope((pd_ref[...] + bd) * 0.5)
    act_ref[...] = act.astype(BF)
    slope_ref[...] = slope.astype(BF)
    lg_ref[...] = dot(wh_ref[...], act_ref[...]) + bh
    sel = sel_ref[...]
    pick = jnp.zeros((ATOMS, rows), F32)
    for a in range(ACT):
        pick = jnp.where(sel == a, lg_ref[ATOMS * a : ATOMS * a + ATOMS, :rows], pick)
    shifted = pick - jnp.max(pick, axis=0, keepdims=True)
    grown = jnp.exp(shifted)
    total = jnp.sum(grown, axis=0, keepdims=True)
    cho_ref[...] = (grown / total).astype(BF)
    lp_ref[...] = shifted - jnp.log(total)


def head(pd, bd, wht, bh, sel):
    rows = sel.shape[1]
    ins = (pd, bd, wht, bh, sel)
    outs = (((512, LANES), BF), ((512, LANES), BF), ((ATOMS, rows), F32), ((ATOMS, rows), BF))
    return call(
        functools.partial(head_kernel, rows),
        tuple(sds(*o) for o in outs),
        [whole(a.shape) for a in ins],
        [whole(o[0]) for o in outs],
        scratch=[pltpu.VMEM((LOGITS, LANES), F32)],
        us=3,
    )(*ins)


def loss_kernel(rows, cho_ref, done_ref, low_ref, frac_ref, lp_ref, taken_ref, loss_ref, rh_ref, hb_ref, d_ref):
    atoms = lax.broadcasted_iota(jnp.int32, (ATOMS, rows), 0)
    done = done_ref[...].astype(F32)
    mass = (1.0 - done) * cho_ref[...].astype(F32) + done * (atoms == 0).astype(F32)
    frac = frac_ref[...]
    stay = mass * (1.0 - frac)
    move = mass * frac
    low = low_ref[...]
    proj = jnp.zeros((ATOMS, rows), F32)
    for i in range(ATOMS):
        gap = atoms - low[i : i + 1, :]
        proj = proj + jnp.where(gap == 0, stay[i : i + 1, :], jnp.where(gap == 1, move[i : i + 1, :], 0.0))
    lp = lp_ref[...]
    loss_ref[...] = -jnp.sum(proj * lp, axis=0, keepdims=True)
    diff = (jnp.sum(proj, axis=0, keepdims=True) * jnp.exp(lp) - proj) * LOSS_SCALE
    taken = taken_ref[...]
    for a in range(ACT):
        d_ref[ATOMS * a : ATOMS * a + ATOMS, :] = jnp.where(taken == a, diff, 0.0)
    rh_ref[...] = jnp.zeros_like(rh_ref)
    rh_ref[:, :rows] = d_ref[...].astype(BF)
    hb_ref[...] = jnp.sum(d_ref[...], axis=1, keepdims=True) * (1.0 / LOSS_SCALE)


def loss(cho, done, low, frac, lp, taken):
    rows = taken.shape[1]
    ins = (cho, done, low, frac, lp, taken)
    outs = (((1, rows), F32), ((LOGITS, LANES), BF), ((LOGITS, 1), F32))
    return call(
        functools.partial(loss_kernel, rows),
        tuple(sds(*o) for o in outs),
        [whole(a.shape) for a in ins],
        [whole(o[0]) for o in outs],
        scratch=[pltpu.VMEM((LOGITS, rows), F32)],
        us=3,
    )(*ins)


def dthird_kernel(w_ref, rd_ref, s3_ref, t_ref, s2_ref, r3_ref, b3_ref, r2_ref, p_ref, b2_ref, keep):
    g = pl.program_id(0)

    def third():
        diff = dot(w_ref[...], rd_ref[...]) * (0.5 * s3_ref[...].astype(F32))
        part = diff.astype(BF)
        r3_ref[...] = part
        keep[pl.ds(pl.multiple_of(448 * (g + 2), 64), 448), :] = part
        b3_ref[...] += jnp.sum(diff.reshape(7, 64, LANES), axis=0)

    def second():
        window = pl.ds(pl.multiple_of(448 * (g - 1), 64), 1344)
        diff = dot(t_ref[...], keep[window, :]) * s2_ref[...].astype(F32)
        r2_ref[...] = diff.astype(BF)
        b2_ref[...] += jnp.sum(diff.reshape(9, 64, LANES), axis=0)
        return diff

    def pack(diff):
        p_ref[0] = pack_rows(diff, 576).astype(BF)

    @pl.when(g == 0)
    def _():
        b3_ref[...] = jnp.zeros_like(b3_ref)
        b2_ref[...] = jnp.zeros_like(b2_ref)
        keep[:896, :] = jnp.zeros((896, LANES), BF)
        keep[4032:, :] = jnp.zeros((896, LANES), BF)
        third()

    @pl.when((g >= 1) & (g < 7))
    def _():
        pack(second())
        third()

    @pl.when((g >= 7) & (g <= FAR))
    def _():
        pack(second())

    @pl.when(g > FAR)
    def _():
        second()


def dthird(wd, rd, s3, t3b, s2):
    block3 = pl.BlockSpec((448, LANES), lambda g: (jnp.minimum(g, 6), 0))
    block2 = pl.BlockSpec((576, LANES), lambda g: (0, jnp.maximum(g - 1, 0)))
    packed = pl.BlockSpec((1, 1008, 128), lambda g: (jnp.clip(g - 1, 0, FAR - 1), 0, 0))
    return call(
        dthird_kernel,
        (
            sds((3136, LANES), BF),
            sds((64, LANES), F32),
            sds((576, 9 * LANES), BF),
            pltpu.HBM((FAR, 1008, 128), BF),
            sds((64, LANES), F32),
        ),
        [
            pl.BlockSpec((448, 512), lambda g: (jnp.minimum(g, 6), 0)),
            whole((512, LANES)),
            block3,
            whole((576, 1344)),
            block2,
        ],
        [block3, whole((64, LANES)), block2, packed, whole((64, LANES))],
        us=12,
        grid=(10,),
        scratch=[pltpu.VMEM((4928, LANES), BF)],
    )(hbm(wd), rd, hbm(s3), hbm(t3b), hbm(s2))


def first_diffs(t, cur, prev):
    none = jnp.zeros((64, LANES), BF)
    halves = []
    for h in range(2):
        if h == 0:
            parts = [none, cur[:320], none, prev[:320]]
        else:
            parts = [cur[256:], none, prev[256:], none]
        halves.append(dot(t, jnp.concatenate(parts, axis=0)))
    return [jnp.concatenate([half[320 * e : 320 * e + 320] for half in halves], axis=0) for e in range(2)]


def dconv2_kernel(first, packs, cur_ref, prev_ref, t_ref, s_ref, *rest):
    r_ref, b_ref = rest[-4 if packs else -2], rest[-1]
    q = pl.program_id(0)
    m = 2 * q + first
    zero = jnp.zeros((576, LANES), BF)

    @pl.when(pl.program_id(0) == 0)
    def _():
        b_ref[...] = jnp.zeros_like(b_ref)

    r2 = [
        jnp.where(m > 0, prev_ref[...], zero),
        cur_ref[:, :LANES],
        jnp.where(m < 8, cur_ref[:, LANES:], zero),
    ]
    total = b_ref[...]
    for k in range(2):
        lanes = slice(LANES * k, LANES * (k + 1))
        for e, part in enumerate(first_diffs(t_ref[...], r2[k + 1], r2[k])):
            part = part * s_ref[e, :, lanes].astype(F32)
            r_ref[e, :, lanes] = part.astype(BF)
            if packs:
                value = pack_rows(part, 640).astype(BF)
                for step in range(2):

                    @pl.when(q == step)
                    def _(at=2 * step + k, e=e, value=value):
                        if at < ALONE:
                            rest[-3][at, e] = value
                        else:
                            rest[-2][at - ALONE, e] = value

            total = total + jnp.sum(part.reshape(20, 32, LANES), axis=0)
    b_ref[...] = total


def dconv2(r2, t2b, s1, first, count, packs, r1):
    block = pl.BlockSpec((2, 640, 2 * LANES), lambda q: (0, 0, q + first // 2))
    ins = [r2, r2, hbm(t2b), hbm(s1)]
    in_specs = [
        pl.BlockSpec((576, 2 * LANES), lambda q: (0, q + first // 2)),
        pl.BlockSpec((576, LANES), lambda q: (0, jnp.maximum(2 * q + first - 1, 0))),
        whole((640, 768)),
        block,
    ]
    aliases = {}
    if r1 is not None:
        ins.append(hbm(r1))
        in_specs.append(pl.BlockSpec(memory_space=pl.ANY))
        aliases = {4: 0}
    parts = [(ALONE, 2, 1120, 128), (count - ALONE, 2, 1120, 128)] if packs else []
    shapes = [pltpu.HBM((2, 640, 10 * LANES), BF)] + [pltpu.HBM(p, BF) for p in parts] + [sds((32, LANES), F32)]
    outs = [block] + [whole(p) for p in parts] + [whole((32, LANES))]
    return pl.pallas_call(
        functools.partial(dconv2_kernel, first, packs),
        out_shape=tuple(shapes),
        grid=(count // 2,),
        in_specs=in_specs,
        out_specs=outs,
        input_output_aliases=aliases,
        compiler_params=pltpu.CompilerParams(vmem_limit_bytes=VMEM_BIG),
        cost_estimate=cost(1.5 * count),
    )(*ins)


def frame_rows(r0, r1, t1b, o_ref, at, rows):
    none = jnp.zeros((32, LANES), BF)
    for g in range(3):
        if g == 0:
            parts = [none, r0[:224], none, r1[:224]]
        elif g == 1:
            parts = [r0[192:448], r1[192:448]]
        else:
            parts = [r0[416:], none, r1[416:], none]
        out = dot(t1b, jnp.concatenate(parts, axis=0)).astype(BF)
        for dy in range(4):
            o_ref[at + dy, 28 * g : 28 * g + 28, :, :] = out[56 * dy : 56 * dy + 56, :rows].reshape(28, 2, rows)


def dframes_kernel(rows, first, last, far, flag_ref, own_ref, before_ref, *rest):
    o_ref, edge_ref = rest[-2:]
    own = flag_ref[0] == 1
    q = pl.program_id(0)
    final = q == pl.num_programs(0) - 1
    t1b = rest[5] if far else rest[2]

    @pl.when(q == 0)
    def _():
        edge_ref[...] = jnp.zeros_like(edge_ref) if first == 0 else rest[6 if far else 3][...]

    def emit(four, before):
        for n, row in enumerate(four):
            frame_rows(row, before, t1b[...], o_ref, 4 * n, rows)
            before = row

    def own_rows():
        before = before_ref[0]
        if first == 0:
            before = jnp.where(q > 0, before, jnp.zeros_like(before))
        emit([own_ref[e, :, LANES * k : LANES * (k + 1)] for k in range(2) for e in range(2)], before)

    def other_rows():
        four = []
        for k in range(2):
            if far:
                cur = unpack_rows(rest[0][k].astype(F32), 576).astype(BF)
                if k == 0:
                    prev = unpack_rows(rest[1][0].astype(F32), 576).astype(BF)
                    if first == 0:
                        prev = jnp.where(q > 0, prev, jnp.zeros_like(prev))
                for e, part in enumerate(first_diffs(rest[4][...], cur, prev)):
                    m = 2 * q + k
                    soon = rest[2][jnp.minimum(m, EARLY - 1), e]
                    slope = jnp.where(m < EARLY, soon, rest[3][jnp.maximum(m - EARLY, 0), e]).astype(F32)
                    four.append((part * unpack_rows(slope, 640)).astype(BF))
                prev = cur
            else:
                for e in range(2):
                    early_part = rest[0][k, e] if k < ALONE else rest[1][k - ALONE, e]
                    part = jnp.where(q == 0, early_part, rest[1][2 + k - ALONE, e]).astype(F32)
                    four.append(unpack_rows(part, 640).astype(BF))
        emit(four, edge_ref[...])
        edge_ref[...] = four[3]

    more = jnp.logical_not(final) if last else True
    pl.when(own & more)(own_rows)
    pl.when(jnp.logical_not(own) & more)(other_rows)
    if last:

        @pl.when(final)
        def _():
            frame_rows(jnp.zeros((640, LANES), BF), jnp.where(own, before_ref[0], edge_ref[...]), t1b[...], o_ref, 0, rows)


def dframes(flag, own, got, t1b, rows, first, count, edge, out):
    far = len(got) > 2
    last = first + count == 10
    steps = count // 2
    at = lambda q: jnp.minimum(q, steps - 1)
    fixed = lambda shape: pl.BlockSpec(shape, lambda *_: (0,) * len(shape))
    ins = [flag, hbm(own), hbm(own)]
    in_specs = [
        pl.BlockSpec((2, 640, 2 * LANES), lambda q, *_: (0, 0, at(q) + first // 2)),
        pl.BlockSpec((1, 640, LANES), lambda q, *_: (1, 0, jnp.maximum(2 * q + first - 1, 0))),
    ]
    if far:
        r2p, early, late, t2b = got
        ins += [hbm(v) for v in (r2p, r2p, early, late, t2b)]
        in_specs += [
            pl.BlockSpec((2, 1008, 128), lambda q, *_: (q + first // 2, 0, 0)),
            pl.BlockSpec((1, 1008, 128), lambda q, *_: (jnp.maximum(2 * q + first - 1, 0), 0, 0)),
            fixed(early.shape),
            fixed(late.shape),
            fixed((640, 768)),
        ]
    else:
        ins += [hbm(v) for v in got]
        in_specs += [fixed(v.shape) for v in got]
    ins.append(hbm(t1b))
    in_specs.append(fixed((224, 512)))
    aliases = {}
    if first:
        ins += [edge, hbm(out)]
        in_specs += [fixed((640, LANES)), pl.BlockSpec(memory_space=pl.ANY)]
        aliases = {len(ins) - 1: 0}
    return pl.pallas_call(
        functools.partial(dframes_kernel, rows, first, last, far),
        out_shape=(pltpu.HBM((84, 84, 2, rows), BF), sds((640, LANES), BF)),
        grid_spec=pltpu.PrefetchScalarGridSpec(
            num_scalar_prefetch=1,
            grid=(steps + 1 if last else steps,),
            in_specs=in_specs,
            out_specs=[pl.BlockSpec((16, 84, 2, rows), lambda q, *_: (q + first // 2, 0, 0, 0)), fixed((640, LANES))],
        ),
        input_output_aliases=aliases,
        compiler_params=pltpu.CompilerParams(vmem_limit_bytes=VMEM_BIG),
        cost_estimate=cost(1.5 * count),
    )(*ins)


def wdense_kernel(flag_ref, a_ref, rd_ref, rh_ref, h_ref, keep_ref, send_ref):
    core = flag_ref[1]
    grads = []
    for left, right in ((a_ref, rd_ref), (rh_ref, h_ref)):
        grads.append((dot_nt(left[...], right[...]) * (1.0 / LOSS_SCALE)).astype(BF))
    start = 0
    for grad in grads:
        size = grad.shape[0]
        for half in range(2):
            tile0 = grad[:, 256 * half : 256 * half + 128]
            tile1 = grad[:, 256 * half + 128 : 256 * half + 256]
            keep_ref[0, half, start : start + size, :] = jnp.where(core == 0, tile0, tile1)
            send_ref[0, half, start : start + size, :] = jnp.where(core == 0, tile1, tile0)
        start += size


def wdense(flag, a3, rd, rh, h):
    out = pl.BlockSpec((1, 2, 512, 128), lambda i, *_: (i, 0, 0, 0))
    return pl.pallas_call(
        wdense_kernel,
        out_shape=(sds((8, 2, 512, 128), BF), sds((8, 2, 512, 128), BF)),
        grid_spec=pltpu.PrefetchScalarGridSpec(
            num_scalar_prefetch=1,
            grid=(8,),
            in_specs=[
                pl.BlockSpec((392, LANES), lambda i, *_: (i, 0)),
                whole((512, LANES)),
                pl.BlockSpec((120, LANES), lambda i, *_: (i, 0)),
                whole((512, LANES)),
            ],
            out_specs=[out, out],
        ),
        compiler_params=pltpu.CompilerParams(vmem_limit_bytes=VMEM_BIG),
        cost_estimate=cost(8),
    )(flag, a3, rd, rh, h)


def wconv3_kernel(*refs):
    columns, (r_ref, g_ref, acc) = refs[:4], refs[4:]
    q = pl.program_id(0)

    @pl.when(q == 0)
    def _():
        acc[...] = jnp.zeros_like(acc)

    left = jnp.concatenate([ref[:, LANES * u : LANES * (u + 7)] for u in range(3) for ref in columns], axis=0)
    last = jnp.where(q < 3, r_ref[:, 64:, :], jnp.zeros((7, 64, LANES), BF))
    right = jnp.concatenate([jnp.concatenate([r_ref[i, :64], last[i]], axis=0) for i in range(7)], axis=1)
    acc[...] += dot_nt(left, right)

    @pl.when(q == 3)
    def _():
        for u in range(3):
            for v in range(3):
                at = 256 * u + 64 * v
                part = acc[at : at + 64, :64] + acc[at + 64 : at + 128, 64:]
                g_ref[:, 192 * u + 64 * v : 192 * u + 64 * v + 64] = part.T * (1.0 / LOSS_SCALE)


def wconv3(a2, r3):
    return call(
        wconv3_kernel,
        sds((64, 576), F32),
        [pl.BlockSpec((64, 9 * LANES), lambda q, k=k: (jnp.minimum(2 * q + k, 8), 0)) for k in range(4)]
        + [pl.BlockSpec((7, 128, LANES), lambda q: (0, q, 0))],
        whole((64, 576)),
        us=7,
        grid=(4,),
        scratch=[pltpu.VMEM((768, 128), F32)],
    )(hbm(a2), hbm(a2), hbm(a2), hbm(a2), r3.reshape(7, 448, LANES))


def wconv2_kernel(a0_ref, a1_ref, r_ref, g_ref, acc):
    q = pl.program_id(0)

    @pl.when(q == 0)
    def _():
        acc[...] = jnp.zeros_like(acc)

    left = jnp.concatenate(
        [ref[e, :, LANES * t : LANES * (t + 9)] for t in range(2) for e in range(2) for ref in (a0_ref, a1_ref)],
        axis=0,
    )
    last = jnp.where(q < 4, r_ref[64:, :], jnp.zeros((64, 9 * LANES), BF))
    acc[...] += dot_nt(left, jnp.concatenate([r_ref[:64, :], last], axis=0))

    @pl.when(q == 4)
    def _():
        for u in range(4):
            at = 192 * u
            g_ref[128 * u : 128 * u + 128, :] = (acc[at : at + 128, :64] + acc[at + 64 : at + 192, 64:]) * (
                1.0 / LOSS_SCALE
            )


def wconv2(a1, r2):
    return call(
        wconv2_kernel,
        sds((512, 64), F32),
        [
            pl.BlockSpec((2, 128, 10 * LANES), lambda q: (0, q, 0)),
            pl.BlockSpec((2, 64, 10 * LANES), lambda q: (0, jnp.minimum(2 * q + 2, 9), 0)),
            pl.BlockSpec((128, 9 * LANES), lambda q: (q, 0)),
        ],
        whole((512, 64)),
        us=9,
        grid=(5,),
        scratch=[pltpu.VMEM((768, 128), F32)],
    )(hbm(a1), hbm(a1), r2)


def wconv1_kernel(x_ref, x0_ref, r_ref, g_ref, acc, before):
    step = pl.program_id(0)

    @pl.when(step == 0)
    def _():
        acc[...] = jnp.zeros_like(acc)
        before[...] = x0_ref[...]

    def column(dy, rows, c):
        if c:
            return x_ref[dy, rows, LANES * (c - 1) : LANES * c]
        return before[dy, rows, :]

    total = acc[...]
    for g in range(5):
        rows = slice(64 * g, 64 * g + 80)
        left = jnp.concatenate(
            [
                jnp.concatenate([column(dy, rows, ii + t) for ii in range(4)], axis=1)
                for t in range(2)
                for dy in range(4)
            ],
            axis=0,
        )
        right = jnp.concatenate(
            [r_ref[ii % 2, 128 * g : 128 * g + 128, LANES * (ii // 2) : LANES * (ii // 2 + 1)] for ii in range(4)],
            axis=1,
        )
        total = total + dot_nt(left, right)
    acc[...] = total
    before[...] = x_ref[:, :, 3 * LANES :]

    @pl.when(step == 4)
    def _():
        for dy in range(8):
            part = jnp.zeros((32, 32), F32)
            for jj in range(4):
                part = part + acc[80 * dy + 16 * jj : 80 * dy + 16 * jj + 32, 32 * jj : 32 * jj + 32]
            g_ref[32 * dy : 32 * dy + 32, :] = part * (1.0 / LOSS_SCALE)


def wconv1(xt, x0, r1):
    return call(
        wconv1_kernel,
        sds((256, 32), F32),
        [
            pl.BlockSpec((4, 336, 4 * LANES), lambda s: (0, 0, s)),
            whole((4, 336, LANES)),
            pl.BlockSpec((2, 640, 2 * LANES), lambda s: (0, 0, s)),
        ],
        whole((256, 32)),
        us=13,
        grid=(5,),
        scratch=[pltpu.VMEM((640, 128), F32), pltpu.VMEM((4, 336, LANES), BF)],
    )(hbm(xt), hbm(x0), hbm(r1))


SMALL_ROWS = 704


def lanes_of(shards):
    return max(1, 128 // shards)


def slot_rows(capacity):
    return (capacity + 7) // 8 * 8


def pack_kernel(shards, capacity, flag_ref, *refs):
    b1_refs, (b2_ref, b3_ref, g1_ref, g2_ref, g3_ref, db_ref, hb_ref, loss_ref, owner_ref, p_ref, w) = refs[:-11], refs[-11:]
    scale = 1.0 / LOSS_SCALE
    w[...] = jnp.zeros_like(w)
    for k in range(4):
        w[64 * k : 64 * k + 64, :] = g3_ref[:, 128 * k : 128 * k + 128]
    w[256:320, :64] = g3_ref[:, 512:]
    w[320:576, :64] = g2_ref[:256, :]
    w[320:576, 64:] = g2_ref[256:, :]
    w[576:704, :32] = g1_ref[:128, :]
    w[576:704, 32:64] = g1_ref[128:, :]
    total = b1_refs[0][...]
    for ref in b1_refs[1:]:
        total = total + ref[...]
    for column, value in ((64, total), (65, b2_ref[...]), (66, b3_ref[...])):
        w[576 : 576 + value.shape[0], column : column + 1] = jnp.sum(value, axis=1, keepdims=True) * scale
    for k in range(4):
        w[576:704, 67 + k : 68 + k] = db_ref[128 * k : 128 * k + 128, :] * scale
    for half in range(2):
        for k in range(4):
            start = 459 * half + 128 * k
            size = min(128, 459 * (half + 1) - start)
            w[576 : 576 + size, 71 + 4 * half + k : 72 + 4 * half + k] = hb_ref[start : start + size, :]

    owner = owner_ref[...]
    rows = owner.shape[1]
    owner_f = owner.astype(F32)
    down = jnp.broadcast_to(owner_f, (8, rows)).T[:, :1]
    same = (down == owner_f) & (
        lax.broadcasted_iota(jnp.int32, (rows, rows), 0) < lax.broadcasted_iota(jnp.int32, (rows, rows), 1)
    )
    slot = jnp.sum(same.astype(F32), axis=0, keepdims=True)
    group, height = lanes_of(shards), slot_rows(capacity)
    place = lax.broadcasted_iota(jnp.int32, (height, rows), 0).astype(F32)
    spread = jnp.where(place == slot, loss_ref[...], 0.0).astype(BF)
    lane = lax.broadcasted_iota(jnp.int32, (128, rows), 0)
    here = shards * lax.rem(owner, group) + flag_ref[2]
    for g in range(shards // group):
        hot = ((lane == here) & (owner // group == g)).astype(BF)
        w[SMALL_ROWS + height * g : SMALL_ROWS + height * g + height, :] = dot_nt(spread, hot)
    p_ref[...] = w[...].astype(BF)


def pack(flag, b1s, shards, capacity, *ins):
    total = SMALL_ROWS + shards // lanes_of(shards) * slot_rows(capacity)
    ins = tuple(b1s) + ins
    return call(
        functools.partial(pack_kernel, shards, capacity),
        sds((total, 128), BF),
        [pl.BlockSpec(memory_space=pltpu.SMEM)] + [whole(a.shape) for a in ins],
        whole((total, 128)),
        scratch=[pltpu.VMEM((total, 128), F32)],
        us=3,
    )(flag, *ins)


def split_kernel(shards, capacity, flag_ref, own_ref, got_ref, k1, b1, k2, b2, k3, b3, db, hb, prio, w):
    own = flag_ref[0] == 1
    w[...] = jnp.where(own, own_ref[...].astype(F32), got_ref[...].astype(F32))

    def pick(low, high):
        return jnp.where(own, low, high)

    k1[...] = pick(w[576:704, :32], w[576:704, 32:64])
    k2[...] = pick(w[320:576, :64], w[320:576, 64:])
    for n in range(9):
        rows = slice(64 * (n // 2), 64 * (n // 2) + 64)
        part = w[rows, 64 * (n % 2) : 64 * (n % 2) + 64]
        k3[n] = pick(part[:32], part[32:])
    columns = w[576:704, :].T
    b1[...] = pick(columns[64:65, :16], columns[64:65, 16:32])
    for ref, at in ((b2, 65), (b3, 66)):
        ref[...] = pick(columns[at : at + 1, :32], columns[at : at + 1, 32:64])
    for k in range(2):
        db[:, 128 * k : 128 * k + 128] = pick(columns[67 + k : 68 + k], columns[69 + k : 70 + k])
    for k in range(4):
        size = min(128, 459 - 128 * k)
        hb[:, 128 * k : 128 * k + size] = pick(columns[71 + k : 72 + k, :size], columns[75 + k : 76 + k, :size])
    group, height = lanes_of(shards), slot_rows(capacity)
    me = flag_ref[2]
    block = w[pl.ds(pl.multiple_of(SMALL_ROWS + height * (me // group), 8), height), :]
    if group > 1:
        block = pltpu.roll(block, lax.rem(128 - shards * lax.rem(me, group), 128), 1)
    half = capacity // 2
    prio[:, 0, :] = pick(block[:half, :shards], block[half : 2 * half, :shards])


def split(flag, own, got, shards, capacity):
    shapes = (
        (128, 32),
        (1, 16),
        (256, 64),
        (1, 32),
        (9, 32, 64),
        (1, 32),
        (1, 256),
        (1, 459),
        (capacity // 2, 1, shards),
    )
    return call(
        functools.partial(split_kernel, shards, capacity),
        tuple(sds(s, F32) for s in shapes),
        [pl.BlockSpec(memory_space=pltpu.SMEM), whole(own.shape), whole(got.shape)],
        [whole(s) for s in shapes],
        scratch=[pltpu.VMEM(own.shape, F32)],
        us=2,
    )(flag, own, got)


def unchunk_kernel(flag_ref, cur_ref, other_ref, d_ref, h_ref):
    core, code = flag_ref[1], flag_ref[3]
    for k in range(2):
        block = (2 * pl.program_id(0) + k) ^ code
        cur, other = cur_ref[block].astype(F32), other_ref[block].astype(F32)
        for lane, tile in enumerate((jnp.where(core == 0, cur, other), jnp.where(core == 0, other, cur))):
            d_ref[392 * k : 392 * k + 392, 128 * lane : 128 * lane + 128] = tile[:392]
            h_ref[120 * k : 120 * k + 120, 128 * lane : 128 * lane + 128] = tile[392:]


def unchunk(flag, cur, other):
    return call(
        unchunk_kernel,
        (sds((3136, 256), F32), sds((LOGITS, 256), F32)),
        [pl.BlockSpec(memory_space=pltpu.SMEM), whole(cur.shape), whole(other.shape)],
        [pl.BlockSpec((784, 256), lambda i: (i, 0)), pl.BlockSpec((240, 256), lambda i: (i, 0))],
        us=4,
        grid=(4,),
    )(flag, cur, other)


def after(value, *others):
    return lax.optimization_barrier((value,) + others)[0]


def hand(value):
    return lax.ppermute(value, "pair", [(0, 1)])


def swap(value, bit):
    devices = lax.axis_size("batch")
    return lax.ppermute(value, "batch", [(i, i ^ bit) for i in range(devices)])


def add(left, right):
    return (left.astype(F32) + right.astype(F32)).astype(BF)


def split_blocks(cur):
    devices = lax.axis_size("batch")
    spread = devices // 16
    if spread > 1:
        cur = cur.reshape(8, 2, spread, 512 // spread, 128).transpose(0, 2, 1, 3, 4)
        cur = cur.reshape(devices // 2, 2, 512 // spread, 128)
    return cur


def halve(cur, me, bit):
    mine = (me // bit) % 2
    pairs = cur.reshape((cur.shape[0] // 2, 2) + cur.shape[1:])
    send = lax.dynamic_index_in_dim(pairs, 1 - mine, axis=1, keepdims=False)
    keep = lax.dynamic_index_in_dim(pairs, mine, axis=1, keepdims=False)
    return keep, swap(send, bit)


def unmix(blocks, code):
    bit = 1
    while bit < blocks.shape[0]:
        pairs = blocks.reshape((-1, 2, bit) + blocks.shape[1:])
        blocks = jnp.where((code // bit) % 2 == 1, pairs[:, ::-1], pairs).reshape(blocks.shape)
        bit *= 2
    return blocks


def join(cur, other):
    return jnp.stack([cur, other], axis=1).reshape((2 * cur.shape[0],) + cur.shape[1:])


def local(
    frames,
    kernel_first,
    bias_first,
    kernel_second,
    bias_second,
    kernel_third,
    bias_third,
    dense_weight,
    dense_bias,
    head_weight,
    head_bias,
    taken_actions,
    greedy_actions,
    done_flags,
    bin_lower,
    bin_fraction,
    owner_shard,
):
    online = lax.axis_index("pair") == 0
    me = lax.axis_index("batch")
    shards = lax.axis_size("batch")
    rows = frames.shape[1]
    capacity = 2 * ((rows + shards - 1) // shards)
    block = me // 2 if shards == 16 else me * 0
    flag = jnp.stack([online.astype(jnp.int32), me % 2, me, block]).astype(jnp.int32)
    xv = frames[0].transpose(2, 3, 1, 0)
    k1, k2, k3 = kernel_first[0], kernel_second[0], kernel_third[0]
    ones = jnp.zeros((16, LANES), BF).at[0].set(1)
    t1, t2, t3, b2, kernels = bands(k1, bias_first, k2, bias_second, k3, bias_third)

    kernels = hand(kernels)
    a1, s1, xt, early, x0 = conv1(xv, t1, ones, 0, EARLY, ())
    early = hand(after(early, kernels))
    a1, s1, xt, late = conv1(xv, t1, ones, EARLY, 10, (a1, s1, xt))
    late = hand(late)
    a2, s2, a3, s3 = conv23(a1, t2, b2, t3, ones)
    wd = dense_weight[0]
    wht = head_weight[0].T
    pd = lax.dot_general(wd, a3, (((0,), (0,)), ((), ())), preferred_element_type=F32)
    taken = taken_actions[None, :]
    sel = jnp.where(online, taken, greedy_actions[None, :])
    h, sd, lp, cho = head(pd, dense_bias, wht, head_bias, sel)
    cho = lax.ppermute(cho, "pair", [(1, 0)])
    t3b, t2b, t2b_online, t1b = bands_back(after(flag, lp), k1, k2, k3, kernels)
    row_loss, rh, hb = loss(after(cho, t1b), done_flags[None, :], bin_lower.T, bin_fraction.T, lp, taken)

    diff_dense = lax.dot_general(wht, rh, (((0,), (0,)), ((), ())), preferred_element_type=F32)
    diff_dense = diff_dense * (0.5 * sd.astype(F32))
    rd = diff_dense.astype(BF)
    db = jnp.sum(diff_dense, axis=1, keepdims=True)

    keep, send = wdense(flag, a3, after(rd, early), rh, h)
    cur = split_blocks(add(keep, swap(send, 1)))
    keep, got = halve(cur, me, 2)

    r3, b3g, r2, r2p, b2g = dthird(wd, rd, s3, t3b, s2)
    r2p = hand(r2p)
    r1, near0, near1, b1g = dconv2(r2, t2b, s1, FAR, 10 - FAR, True, None)
    cur = add(after(keep, b1g), got)
    keep, far = halve(cur, me, 4)
    r1, b1g_far = dconv2(after(r2, got, late), t2b, s1, 0, FAR, False, r1)
    b1s = [b1g, b1g_far]
    g3 = wconv3(a2, after(r3, b1g_far))
    bit = 4
    while 2 * bit < shards:
        cur = add(after(keep, g3) if bit == 4 else keep, far)
        bit *= 2
        keep, far = halve(cur, me, bit)
    g1 = wconv1(xt, x0, after(r1, g3))
    chunk = add(after(keep, g1), far)[0]
    far_chunk = hand(chunk[1])
    near0 = hand(after(near0, far))
    near1 = hand(after(near1, far))
    mine = jnp.where(online, chunk[0], far_chunk)
    g2 = wconv2(a1, after(r2, chunk))

    cur = mine[None]
    part = swap(cur, bit)
    small = pack(after(flag, part, r2p), b1s, shards, capacity, b2g, b3g, g1, g2, g3, db, hb, row_loss, owner_shard.T)
    small = add(small, swap(small, 1))
    got = swap(small, 2)
    cur = join(cur, part)
    part = swap(cur, bit // 2)
    out, edge = dframes(flag, after(r1, small, cur, near0), (r2p, early, late, t2b_online), t1b, rows, 0, FAR, None, None)
    cur = join(after(cur, edge), part)
    small = add(after(small, edge), got)
    part, got = swap(cur, bit // 4), swap(small, 4)
    small = add(small, got)
    got = swap(small, 8)
    small = add(after(small, near1), got)
    cur = join(after(cur, got), part)
    lower = 16
    while lower < shards:
        small = add(small, swap(small, lower))
        cur = join(cur, swap(cur, 2 * bit // lower))
        lower *= 2
    other = swap(cur, 1)
    far_small = hand(small)
    out, edge = dframes(flag, after(r1, cur, small), [near0, near1], t1b, rows, FAR, 10 - FAR, edge, out)
    if shards != 16:
        cur, other = (unmix(v, me // 2).reshape(8, 512, 128) for v in (cur, other))
    dense_out, head_out = unchunk(flag, cur, other)
    o = split(flag, small, far_small, shards, capacity)
    return (
        o[0].reshape(4, 8, 4, 32),
        o[1].reshape(16),
        o[2].reshape(2, 4, 32, 64),
        o[3].reshape(32),
        o[4].reshape(3, 3, 32, 64).transpose(0, 1, 3, 2),
        o[5].reshape(32),
        dense_out,
        o[6].reshape(256),
        head_out.T,
        o[7].reshape(459),
        out.transpose(3, 2, 0, 1),
        o[8].transpose(1, 2, 0),
    )


def solution(mesh):
    return jax.shard_map(
        local,
        mesh=mesh,
        in_specs=(
            P("pair", "batch", None, None, None),
            P("pair", None, None, None, None),
            P("pair", None),
            P("pair", None, None, None, None),
            P("pair", None),
            P("pair", None, None, None, None),
            P("pair", None),
            P("pair", None, None),
            P("pair", None),
            P("pair", None, None),
            P("pair", None),
            P("batch"),
            P("batch"),
            P("batch"),
            P("batch", None),
            P("batch", None),
            P("batch", None),
        ),
        out_specs=(
            P("pair", None, None, None),
            P("pair"),
            P("pair", None, None, None),
            P("pair"),
            P(None, None, None, "pair"),
            P("pair"),
            P(None, "pair"),
            P("pair"),
            P("pair", None),
            P("pair"),
            P("batch", "pair", None, None),
            P("batch", None, "pair"),
        ),
        check_vma=False,
    )
```

```python
import functools

import jax
import jax.numpy as jnp
from jax import lax
from jax.experimental import pallas as pl
from jax.experimental.pallas import tpu as pltpu
from jax.sharding import PartitionSpec as P

ACT = 18
ATOMS = 51
LOGITS = ACT * ATOMS
LOSS_SCALE = 256
LANES = 256
BF = jnp.bfloat16
F32 = jnp.float32
VMEM_BIG = 24 << 20
FAR = 6
EARLY = 3
ALONE = 1
NEAR = ((6, 4),)


def cost(us):
    return pl.CostEstimate(flops=int(us * 0.4e9), bytes_accessed=0, transcendentals=0)


def call(kernel, out, ins, outs, us, grid=None, scratch=()):
    return pl.pallas_call(
        kernel,
        out_shape=out,
        grid=() if grid is None else grid,
        in_specs=ins,
        out_specs=outs,
        scratch_shapes=list(scratch),
        compiler_params=pltpu.CompilerParams(vmem_limit_bytes=VMEM_BIG),
        cost_estimate=cost(us),
    )


def whole(shape):
    return pl.BlockSpec(shape, lambda *_: (0,) * len(shape))


def hbm(value):
    return pltpu.with_memory_space_constraint(value, pltpu.HBM)


def sds(shape, dtype):
    return jax.ShapeDtypeStruct(shape, dtype)


def dot(left, right):
    return jnp.dot(left, right, preferred_element_type=F32)


def dot_nt(left, right):
    return lax.dot_general(left, right, (((1,), (1,)), ((), ())), preferred_element_type=F32)


def act_slope(half):
    tan = jnp.tanh(half)
    up = 1.0 + tan
    act = half * up
    return act, up + act * (1.0 - tan)


def second_bands(k2n, w2b):
    for e in range(2):
        for t in range(2):
            u = 2 * t + e
            for j in range(6):
                lo = max(0, 2 * j - 2)
                hi = min(10, 2 * j + 2)
                v0 = lo - (2 * j - 2)
                w2b[320 * e + 32 * lo : 320 * e + 32 * hi, 384 * t + 64 * j : 384 * t + 64 * j + 64] = k2n[
                    128 * u + 32 * v0 : 128 * u + 32 * (v0 + hi - lo), :
                ]


def turned(kernel, bias=None):
    flat = kernel[...].astype(F32)
    flat = flat.reshape(-1, flat.shape[-1])
    if bias is not None:
        bias = jnp.broadcast_to(bias[...].astype(F32), (8, flat.shape[1])).T[:, :1]
    return flat, flat.T, bias


def bands_kernel(k1, b1, k2, b2, k3, b3, t1, t2, t3, b2c, send, w1, w2, w3):
    for ref in (w1, w2, w3):
        ref[...] = jnp.zeros_like(ref)
    _, k1t, b1c = turned(k1, b1)
    k2n, k2t, b2t = turned(k2, b2)
    _, k3t, b3c = turned(k3, b3)
    send[:512, :] = k2n.astype(BF)
    send[512:, :32] = k1[:, :, 2:, :].astype(F32).reshape(128, 32).astype(BF)
    send[512:, 32:] = jnp.zeros((128, 32), BF)
    for jj in range(10):
        for dy in range(8):
            w1[32 * jj : 32 * jj + 32, 176 * dy + 16 * jj : 176 * dy + 16 * jj + 32] = k1t[:, 32 * dy : 32 * dy + 32]
        w1[32 * jj : 32 * jj + 32, 1408:1409] = b1c
    for jj in range(3):
        for u in range(4):
            w2[64 * jj : 64 * jj + 64, 256 * u + 64 * jj : 256 * u + 64 * jj + 128] = k2t[:, 128 * u : 128 * u + 128]
        b2c[64 * jj : 64 * jj + 64, :] = 0.5 * b2t
    for j in range(7):
        for u in range(3):
            w3[64 * j : 64 * j + 64, 576 * u + 64 * j : 576 * u + 64 * j + 192] = k3t[:, 192 * u : 192 * u + 192]
        w3[64 * j : 64 * j + 64, 1728:1729] = b3c
    t1[...] = (0.5 * w1[...]).astype(BF)
    t2[...] = (0.5 * w2[...]).astype(BF)
    t3[...] = (0.5 * w3[...]).astype(BF)


def bands(*ins):
    shapes = ((320, 1424), (192, 1024), (448, 1744))
    return call(
        bands_kernel,
        (sds(shapes[0], BF), pltpu.HBM(shapes[1], BF), pltpu.HBM(shapes[2], BF), sds((192, 1), F32), pltpu.HBM((640, 64), BF)),
        [whole(a.shape) for a in ins],
        [whole(s) for s in shapes] + [whole((192, 1)), whole((640, 64))],
        us=3,
        scratch=[pltpu.VMEM(s, F32) for s in shapes],
    )(*[hbm(v) for v in ins])


def bands_back_kernel(flag_ref, k1, k2, k3, got, t3b, t2b, t2o, t1b, w3b, w2b, w1b):
    own = flag_ref[0] == 1
    for ref in (w3b, w2b, w1b):
        ref[...] = jnp.zeros_like(ref)
    k3n, k2n = turned(k3)[0], turned(k2)[0]
    for j in range(7):
        for u in range(3):
            w3b[64 * j : 64 * j + 192, 448 * (2 - u) + 64 * j : 448 * (2 - u) + 64 * j + 64] = k3n[192 * u : 192 * u + 192, :]
    t3b[...] = (0.5 * w3b[...]).astype(BF)
    second_bands(k2n, w2b)
    t2b[...] = (0.5 * w2b[...]).astype(BF)
    second_bands(jnp.where(own, k2n, got[:512, :].astype(F32)), w2b)
    t2o[...] = (0.5 * w2b[...]).astype(BF)
    half = jnp.where(own, k1[:, :, :2, :].astype(F32).reshape(128, 32), got[512:, :32].astype(F32)).reshape(8, 16, 32)
    for dy in range(8):
        t, row = divmod(dy, 4)
        for j in range(8):
            lo = max(0, 4 * j - 4)
            hi = min(28, 4 * j + 4)
            d0 = lo - (4 * j - 4)
            w1b[56 * row + 2 * lo : 56 * row + 2 * hi, 256 * t + 32 * j : 256 * t + 32 * j + 32] = half[
                dy, 2 * d0 : 2 * (d0 + hi - lo), :
            ]
    t1b[...] = w1b[...].astype(BF)


def bands_back(flag, *ins):
    shapes = ((576, 1344), (640, 768), (640, 768), (224, 512))
    return call(
        bands_back_kernel,
        tuple(pltpu.HBM(s, BF) for s in shapes),
        [pl.BlockSpec(memory_space=pltpu.SMEM)] + [whole(a.shape) for a in ins],
        [whole(s) for s in shapes],
        us=4,
        scratch=[pltpu.VMEM(s, F32) for s in (shapes[0], shapes[1], shapes[3])],
    )(flag, *[hbm(v) for v in ins])


def pack_rows(part, n):
    lane = lax.broadcasted_iota(jnp.int32, (n // 4, 128), 1)
    tail = [part[n // 4 * k : n // 4 * (k + 1), 128:] for k in range(4)]
    packed = [jnp.where(lane < 96, tail[k], pltpu.roll(tail[3], 96 - 32 * k, 1)) for k in range(3)]
    return jnp.concatenate([part[:, :128]] + packed, axis=0)


def unpack_rows(packed, n):
    lane = lax.broadcasted_iota(jnp.int32, (n // 4, 128), 1)
    tail = [packed[n + n // 4 * k : n + n // 4 * (k + 1)] for k in range(3)]
    last = pltpu.roll(tail[0], 32, 1)
    last = jnp.where(lane < 32, last, jnp.where(lane < 64, pltpu.roll(tail[1], 64, 1), pltpu.roll(tail[2], 96, 1)))
    return jnp.concatenate([packed[:n], jnp.concatenate(tail + [last], axis=0)], axis=1)


def conv1_kernel(rows, start, packs, first_ref, xa_ref, xb_ref, t1_ref, ones_ref, *rest):
    cells = rest[-1]
    a_ref, s_ref, xt_ref, p_ref = rest[-5:-1] if start else rest[-6:-2]
    m = pl.program_id(0) + start

    def relay(ref, slot):
        for dy in range(4):
            cells[slot, dy, :, :rows] = ref[dy].reshape(336, rows)

    @pl.when(m == start)
    def _():
        cells[...] = jnp.zeros_like(cells)
        relay(first_ref, 0)
        if not start:
            rest[-2][...] = cells[0]

    relay(xa_ref, 1)
    relay(xb_ref, 2)
    slopes = []
    for e in range(2):
        parts_of = lambda window, e=e: [cells[e + t, dy, window, :] for t in range(2) for dy in range(4)]
        row = []
        for g in range(2):
            half = dot(t1_ref[...], jnp.concatenate(parts_of(pl.ds(160 * g, 176)) + [ones_ref[...]], axis=0))
            act, slope = act_slope(half)
            a_ref[e, 320 * g : 320 * g + 320, :] = act.astype(BF)
            s_ref[e, 320 * g : 320 * g + 320, :] = slope.astype(BF)
            row.append(slope)
        slopes.append(row)
    if not start:
        for e in range(2):
            p_ref[0, e] = pack_rows(jnp.concatenate(slopes[e], axis=0), 640).astype(BF)
    for dy in range(4):
        xt_ref[dy, :, :LANES] = cells[1, dy]
        xt_ref[dy, :, LANES:] = cells[2, dy]
        cells[0, dy] = cells[2, dy]
    if start:

        @pl.when(m < packs)
        def _():
            for e in range(2):
                p_ref[0, e] = pack_rows(s_ref[e].astype(F32), 640).astype(BF)


def conv1(xv, t1, ones, start, stop, before):
    rows = xv.shape[3]
    packs = min(stop, FAR)
    cell = lambda f: pl.BlockSpec((4, 84, 4, rows), lambda m: (f(m + start), 0, 0, 0))
    out = pl.BlockSpec((2, 640, LANES), lambda m: (0, 0, m + start))
    outs = [
        out,
        out,
        pl.BlockSpec((4, 336, 2 * LANES), lambda m: (0, 0, m + start)),
        pl.BlockSpec((1, 2, 1120, 128), lambda m: (jnp.minimum(m, packs - start - 1), 0, 0, 0)),
    ]
    shapes = [
        pltpu.HBM((2, 640, 10 * LANES), BF),
        pltpu.HBM((2, 640, 10 * LANES), BF),
        pltpu.HBM((4, 336, 20 * LANES), BF),
        pltpu.HBM((packs - start, 2, 1120, 128), BF),
    ]
    if not start:
        outs.append(whole((4, 336, LANES)))
        shapes.append(pltpu.HBM((4, 336, LANES), BF))
    return pl.pallas_call(
        functools.partial(conv1_kernel, rows, start, packs),
        out_shape=tuple(shapes),
        grid=(stop - start,),
        in_specs=[
            pl.BlockSpec((4, 84, 4, rows), lambda m: (2 * start, 0, 0, 0)),
            cell(lambda m: 2 * m + 1),
            cell(lambda m: 2 * m + 2),
            whole((320, 1424)),
            whole((16, LANES)),
        ]
        + [pl.BlockSpec(memory_space=pl.ANY)] * len(before),
        out_specs=outs,
        scratch_shapes=[pltpu.VMEM((3, 4, 336, LANES), BF)],
        input_output_aliases={5 + n: n for n in range(len(before))},
        compiler_params=pltpu.CompilerParams(vmem_limit_bytes=VMEM_BIG),
        cost_estimate=cost(0.02 * (stop - start)),
    )(hbm(xv), hbm(xv), hbm(xv), t1, ones, *[hbm(v) for v in before])


def conv23_kernel(r0_ref, r1_ref, t2_ref, b2_ref, t3_ref, ones_ref, a2_ref, s2_ref, a3_ref, s3_ref, keep):
    g = pl.program_id(0)

    def third():
        window = pl.ds(pl.multiple_of(576 * (g - 3), 64), 1728)
        half = dot(t3_ref[...], jnp.concatenate([keep[window, :], ones_ref[...]], axis=0))
        act, slope = act_slope(half)
        a3_ref[...] = act.astype(BF)
        s3_ref[...] = slope.astype(BF)

    def second():
        for n in range(3):
            window = pl.ds(192 * n, 256)
            parts = [r0_ref[0, window, :], r0_ref[1, window, :], r1_ref[0, window, :], r1_ref[1, window, :]]
            half = dot(t2_ref[...], jnp.concatenate(parts, axis=0)) + b2_ref[...]
            act, slope = act_slope(half)
            act = act.astype(BF)
            a2_ref[192 * n : 192 * n + 192, :] = act
            keep[pl.ds(pl.multiple_of(576 * g + 192 * n, 64), 192), :] = act
            s2_ref[192 * n : 192 * n + 192, :] = slope.astype(BF)

    @pl.when(g < 3)
    def _():
        second()

    @pl.when((g >= 3) & (g < 9))
    def _():
        third()
        second()

    @pl.when(g == 9)
    def _():
        third()


def conv23(a1, t2, b2, t3, ones):
    row = lambda t: pl.BlockSpec((2, 640, LANES), lambda g: (0, 0, jnp.minimum(g, 8) + t))
    out2 = pl.BlockSpec((576, LANES), lambda g: (0, jnp.minimum(g, 8)))
    out3 = pl.BlockSpec((448, LANES), lambda g: (jnp.maximum(g - 3, 0), 0))
    return call(
        conv23_kernel,
        (pltpu.HBM((576, 9 * LANES), BF), pltpu.HBM((576, 9 * LANES), BF), sds((3136, LANES), BF), pltpu.HBM((3136, LANES), BF)),
        [row(0), row(1), whole((192, 1024)), whole((192, 1)), whole((448, 1744)), whole((16, LANES))],
        [out2, out2, out3, out3],
        us=14,
        grid=(10,),
        scratch=[pltpu.VMEM((9 * 576, LANES), BF)],
    )(hbm(a1), hbm(a1), hbm(t2), b2, hbm(t3), ones)


def head_kernel(rows, pd_ref, bd_ref, wh_ref, bh_ref, sel_ref, act_ref, slope_ref, lp_ref, cho_ref, lg_ref):
    bd = jnp.broadcast_to(bd_ref[...].astype(F32), (8, 512)).T[:, :1]
    bh = jnp.broadcast_to(bh_ref[...].astype(F32), (8, LOGITS)).T[:, :1]
    act, slope = act_slope((pd_ref[...] + bd) * 0.5)
    act_ref[...] = act.astype(BF)
    slope_ref[...] = slope.astype(BF)
    lg_ref[...] = dot(wh_ref[...], act_ref[...]) + bh
    sel = sel_ref[...]
    pick = jnp.zeros((ATOMS, rows), F32)
    for a in range(ACT):
        pick = jnp.where(sel == a, lg_ref[ATOMS * a : ATOMS * a + ATOMS, :rows], pick)
    shifted = pick - jnp.max(pick, axis=0, keepdims=True)
    grown = jnp.exp(shifted)
    total = jnp.sum(grown, axis=0, keepdims=True)
    cho_ref[...] = (grown / total).astype(BF)
    lp_ref[...] = shifted - jnp.log(total)


def head(pd, bd, wht, bh, sel):
    rows = sel.shape[1]
    ins = (pd, bd, wht, bh, sel)
    outs = (((512, LANES), BF), ((512, LANES), BF), ((ATOMS, rows), F32), ((ATOMS, rows), BF))
    return call(
        functools.partial(head_kernel, rows),
        tuple(sds(*o) for o in outs),
        [whole(a.shape) for a in ins],
        [whole(o[0]) for o in outs],
        scratch=[pltpu.VMEM((LOGITS, LANES), F32)],
        us=3,
    )(*ins)


def loss_kernel(rows, cho_ref, done_ref, low_ref, frac_ref, lp_ref, taken_ref, loss_ref, rh_ref, hb_ref, d_ref):
    atoms = lax.broadcasted_iota(jnp.int32, (ATOMS, rows), 0)
    done = done_ref[...].astype(F32)
    mass = (1.0 - done) * cho_ref[...].astype(F32) + done * (atoms == 0).astype(F32)
    frac = frac_ref[...]
    stay = mass * (1.0 - frac)
    move = mass * frac
    low = low_ref[...]
    proj = jnp.zeros((ATOMS, rows), F32)
    for i in range(ATOMS):
        gap = atoms - low[i : i + 1, :]
        proj = proj + jnp.where(gap == 0, stay[i : i + 1, :], jnp.where(gap == 1, move[i : i + 1, :], 0.0))
    lp = lp_ref[...]
    loss_ref[...] = -jnp.sum(proj * lp, axis=0, keepdims=True)
    diff = (jnp.sum(proj, axis=0, keepdims=True) * jnp.exp(lp) - proj) * LOSS_SCALE
    taken = taken_ref[...]
    for a in range(ACT):
        d_ref[ATOMS * a : ATOMS * a + ATOMS, :] = jnp.where(taken == a, diff, 0.0)
    rh_ref[...] = jnp.zeros_like(rh_ref)
    rh_ref[:, :rows] = d_ref[...].astype(BF)
    hb_ref[...] = jnp.sum(d_ref[...], axis=1, keepdims=True) * (1.0 / LOSS_SCALE)


def loss(cho, done, low, frac, lp, taken):
    rows = taken.shape[1]
    ins = (cho, done, low, frac, lp, taken)
    outs = (((1, rows), F32), ((LOGITS, LANES), BF), ((LOGITS, 1), F32))
    return call(
        functools.partial(loss_kernel, rows),
        tuple(sds(*o) for o in outs),
        [whole(a.shape) for a in ins],
        [whole(o[0]) for o in outs],
        scratch=[pltpu.VMEM((LOGITS, rows), F32)],
        us=3,
    )(*ins)


def dthird_kernel(w_ref, rd_ref, s3_ref, t_ref, s2_ref, r3_ref, b3_ref, r2_ref, p_ref, b2_ref, keep):
    g = pl.program_id(0)

    def third():
        diff = dot(w_ref[...], rd_ref[...]) * (0.5 * s3_ref[...].astype(F32))
        part = diff.astype(BF)
        r3_ref[...] = part
        keep[pl.ds(pl.multiple_of(448 * (g + 2), 64), 448), :] = part
        b3_ref[...] += jnp.sum(diff.reshape(7, 64, LANES), axis=0)

    def second():
        window = pl.ds(pl.multiple_of(448 * (g - 1), 64), 1344)
        diff = dot(t_ref[...], keep[window, :]) * s2_ref[...].astype(F32)
        r2_ref[...] = diff.astype(BF)
        b2_ref[...] += jnp.sum(diff.reshape(9, 64, LANES), axis=0)
        return diff

    def pack(diff):
        p_ref[0] = pack_rows(diff, 576).astype(BF)

    @pl.when(g == 0)
    def _():
        b3_ref[...] = jnp.zeros_like(b3_ref)
        b2_ref[...] = jnp.zeros_like(b2_ref)
        keep[:896, :] = jnp.zeros((896, LANES), BF)
        keep[4032:, :] = jnp.zeros((896, LANES), BF)
        third()

    @pl.when((g >= 1) & (g < 7))
    def _():
        pack(second())
        third()

    @pl.when((g >= 7) & (g <= FAR))
    def _():
        pack(second())

    @pl.when(g > FAR)
    def _():
        second()


def dthird(wd, rd, s3, t3b, s2):
    block3 = pl.BlockSpec((448, LANES), lambda g: (jnp.minimum(g, 6), 0))
    block2 = pl.BlockSpec((576, LANES), lambda g: (0, jnp.maximum(g - 1, 0)))
    packed = pl.BlockSpec((1, 1008, 128), lambda g: (jnp.clip(g - 1, 0, FAR - 1), 0, 0))
    return call(
        dthird_kernel,
        (
            sds((3136, LANES), BF),
            sds((64, LANES), F32),
            sds((576, 9 * LANES), BF),
            pltpu.HBM((FAR, 1008, 128), BF),
            sds((64, LANES), F32),
        ),
        [
            pl.BlockSpec((448, 512), lambda g: (jnp.minimum(g, 6), 0)),
            whole((512, LANES)),
            block3,
            whole((576, 1344)),
            block2,
        ],
        [block3, whole((64, LANES)), block2, packed, whole((64, LANES))],
        us=12,
        grid=(10,),
        scratch=[pltpu.VMEM((4928, LANES), BF)],
    )(hbm(wd), rd, hbm(s3), hbm(t3b), hbm(s2))


def first_diffs(t, cur, prev):
    none = jnp.zeros((64, LANES), BF)
    halves = []
    for h in range(2):
        if h == 0:
            parts = [none, cur[:320], none, prev[:320]]
        else:
            parts = [cur[256:], none, prev[256:], none]
        halves.append(dot(t, jnp.concatenate(parts, axis=0)))
    return [jnp.concatenate([half[320 * e : 320 * e + 320] for half in halves], axis=0) for e in range(2)]


def dconv2_kernel(first, packs, cur_ref, prev_ref, t_ref, s_ref, *rest):
    r_ref, b_ref = rest[-4 if packs else -2], rest[-1]
    q = pl.program_id(0)
    m = 2 * q + first
    zero = jnp.zeros((576, LANES), BF)

    @pl.when(pl.program_id(0) == 0)
    def _():
        b_ref[...] = jnp.zeros_like(b_ref)

    r2 = [
        jnp.where(m > 0, prev_ref[...], zero),
        cur_ref[:, :LANES],
        jnp.where(m < 8, cur_ref[:, LANES:], zero),
    ]
    total = b_ref[...]
    for k in range(2):
        lanes = slice(LANES * k, LANES * (k + 1))
        for e, part in enumerate(first_diffs(t_ref[...], r2[k + 1], r2[k])):
            part = part * s_ref[e, :, lanes].astype(F32)
            r_ref[e, :, lanes] = part.astype(BF)
            if packs:
                value = pack_rows(part, 640).astype(BF)
                for step in range(2):

                    @pl.when(q == step)
                    def _(at=2 * step + k, e=e, value=value):
                        if at < ALONE:
                            rest[-3][at, e] = value
                        else:
                            rest[-2][at - ALONE, e] = value

            total = total + jnp.sum(part.reshape(20, 32, LANES), axis=0)
    b_ref[...] = total


def dconv2(r2, t2b, s1, first, count, packs, r1):
    block = pl.BlockSpec((2, 640, 2 * LANES), lambda q: (0, 0, q + first // 2))
    ins = [r2, r2, hbm(t2b), hbm(s1)]
    in_specs = [
        pl.BlockSpec((576, 2 * LANES), lambda q: (0, q + first // 2)),
        pl.BlockSpec((576, LANES), lambda q: (0, jnp.maximum(2 * q + first - 1, 0))),
        whole((640, 768)),
        block,
    ]
    aliases = {}
    if r1 is not None:
        ins.append(hbm(r1))
        in_specs.append(pl.BlockSpec(memory_space=pl.ANY))
        aliases = {4: 0}
    parts = [(ALONE, 2, 1120, 128), (count - ALONE, 2, 1120, 128)] if packs else []
    shapes = [pltpu.HBM((2, 640, 10 * LANES), BF)] + [pltpu.HBM(p, BF) for p in parts] + [sds((32, LANES), F32)]
    outs = [block] + [whole(p) for p in parts] + [whole((32, LANES))]
    return pl.pallas_call(
        functools.partial(dconv2_kernel, first, packs),
        out_shape=tuple(shapes),
        grid=(count // 2,),
        in_specs=in_specs,
        out_specs=outs,
        input_output_aliases=aliases,
        compiler_params=pltpu.CompilerParams(vmem_limit_bytes=VMEM_BIG),
        cost_estimate=cost(1.5 * count),
    )(*ins)


def frame_rows(r0, r1, t1b, o_ref, at, rows):
    none = jnp.zeros((32, LANES), BF)
    for g in range(3):
        if g == 0:
            parts = [none, r0[:224], none, r1[:224]]
        elif g == 1:
            parts = [r0[192:448], r1[192:448]]
        else:
            parts = [r0[416:], none, r1[416:], none]
        out = dot(t1b, jnp.concatenate(parts, axis=0)).astype(BF)
        for dy in range(4):
            o_ref[at + dy, 28 * g : 28 * g + 28, :, :] = out[56 * dy : 56 * dy + 56, :rows].reshape(28, 2, rows)


def dframes_kernel(rows, first, last, far, flag_ref, own_ref, before_ref, *rest):
    o_ref, edge_ref = rest[-2:]
    own = flag_ref[0] == 1
    q = pl.program_id(0)
    final = q == pl.num_programs(0) - 1
    t1b = rest[5] if far else rest[2]

    @pl.when(q == 0)
    def _():
        edge_ref[...] = jnp.zeros_like(edge_ref) if first == 0 else rest[6 if far else 3][...]

    def emit(four, before):
        for n, row in enumerate(four):
            frame_rows(row, before, t1b[...], o_ref, 4 * n, rows)
            before = row

    def own_rows():
        before = before_ref[0]
        if first == 0:
            before = jnp.where(q > 0, before, jnp.zeros_like(before))
        emit([own_ref[e, :, LANES * k : LANES * (k + 1)] for k in range(2) for e in range(2)], before)

    def other_rows():
        four = []
        for k in range(2):
            if far:
                cur = unpack_rows(rest[0][k].astype(F32), 576).astype(BF)
                if k == 0:
                    prev = unpack_rows(rest[1][0].astype(F32), 576).astype(BF)
                    if first == 0:
                        prev = jnp.where(q > 0, prev, jnp.zeros_like(prev))
                for e, part in enumerate(first_diffs(rest[4][...], cur, prev)):
                    m = 2 * q + k
                    soon = rest[2][jnp.minimum(m, EARLY - 1), e]
                    slope = jnp.where(m < EARLY, soon, rest[3][jnp.maximum(m - EARLY, 0), e]).astype(F32)
                    four.append((part * unpack_rows(slope, 640)).astype(BF))
                prev = cur
            else:
                for e in range(2):
                    early_part = rest[0][k, e] if k < ALONE else rest[1][k - ALONE, e]
                    part = jnp.where(q == 0, early_part, rest[1][2 + k - ALONE, e]).astype(F32)
                    four.append(unpack_rows(part, 640).astype(BF))
        emit(four, edge_ref[...])
        edge_ref[...] = four[3]

    more = jnp.logical_not(final) if last else True
    pl.when(own & more)(own_rows)
    pl.when(jnp.logical_not(own) & more)(other_rows)
    if last:

        @pl.when(final)
        def _():
            frame_rows(jnp.zeros((640, LANES), BF), jnp.where(own, before_ref[0], edge_ref[...]), t1b[...], o_ref, 0, rows)


def dframes(flag, own, got, t1b, rows, first, count, edge, out):
    far = len(got) > 2
    last = first + count == 10
    steps = count // 2
    at = lambda q: jnp.minimum(q, steps - 1)
    fixed = lambda shape: pl.BlockSpec(shape, lambda *_: (0,) * len(shape))
    ins = [flag, hbm(own), hbm(own)]
    in_specs = [
        pl.BlockSpec((2, 640, 2 * LANES), lambda q, *_: (0, 0, at(q) + first // 2)),
        pl.BlockSpec((1, 640, LANES), lambda q, *_: (1, 0, jnp.maximum(2 * q + first - 1, 0))),
    ]
    if far:
        r2p, early, late, t2b = got
        ins += [hbm(v) for v in (r2p, r2p, early, late, t2b)]
        in_specs += [
            pl.BlockSpec((2, 1008, 128), lambda q, *_: (q + first // 2, 0, 0)),
            pl.BlockSpec((1, 1008, 128), lambda q, *_: (jnp.maximum(2 * q + first - 1, 0), 0, 0)),
            fixed(early.shape),
            fixed(late.shape),
            fixed((640, 768)),
        ]
    else:
        ins += got
        in_specs += [fixed(v.shape) for v in got]
    ins.append(t1b)
    in_specs.append(fixed((224, 512)))
    aliases = {}
    if first:
        ins += [edge, hbm(out)]
        in_specs += [fixed((640, LANES)), pl.BlockSpec(memory_space=pl.ANY)]
        aliases = {len(ins) - 1: 0}
    return pl.pallas_call(
        functools.partial(dframes_kernel, rows, first, last, far),
        out_shape=(pltpu.HBM((84, 84, 2, rows), BF), sds((640, LANES), BF)),
        grid_spec=pltpu.PrefetchScalarGridSpec(
            num_scalar_prefetch=1,
            grid=(steps + 1 if last else steps,),
            in_specs=in_specs,
            out_specs=[pl.BlockSpec((16, 84, 2, rows), lambda q, *_: (q + first // 2, 0, 0, 0)), fixed((640, LANES))],
        ),
        input_output_aliases=aliases,
        compiler_params=pltpu.CompilerParams(vmem_limit_bytes=VMEM_BIG),
        cost_estimate=cost(1.5 * count),
    )(*ins)


def wdense_kernel(flag_ref, a_ref, rd_ref, rh_ref, h_ref, keep_ref, send_ref):
    core = flag_ref[1]
    grads = []
    for left, right in ((a_ref, rd_ref), (rh_ref, h_ref)):
        grads.append((dot_nt(left[...], right[...]) * (1.0 / LOSS_SCALE)).astype(BF))
    start = 0
    for grad in grads:
        size = grad.shape[0]
        for half in range(2):
            tile0 = grad[:, 256 * half : 256 * half + 128]
            tile1 = grad[:, 256 * half + 128 : 256 * half + 256]
            keep_ref[0, half, start : start + size, :] = jnp.where(core == 0, tile0, tile1)
            send_ref[0, half, start : start + size, :] = jnp.where(core == 0, tile1, tile0)
        start += size


def wdense(flag, a3, rd, rh, h):
    out = pl.BlockSpec((1, 2, 512, 128), lambda i, *_: (i, 0, 0, 0))
    return pl.pallas_call(
        wdense_kernel,
        out_shape=(sds((8, 2, 512, 128), BF), sds((8, 2, 512, 128), BF)),
        grid_spec=pltpu.PrefetchScalarGridSpec(
            num_scalar_prefetch=1,
            grid=(8,),
            in_specs=[
                pl.BlockSpec((392, LANES), lambda i, *_: (i, 0)),
                whole((512, LANES)),
                pl.BlockSpec((120, LANES), lambda i, *_: (i, 0)),
                whole((512, LANES)),
            ],
            out_specs=[out, out],
        ),
        compiler_params=pltpu.CompilerParams(vmem_limit_bytes=VMEM_BIG),
        cost_estimate=cost(8),
    )(flag, a3, rd, rh, h)


def wconv3_kernel(*refs):
    columns, (r_ref, g_ref, acc) = refs[:4], refs[4:]
    q = pl.program_id(0)

    @pl.when(q == 0)
    def _():
        acc[...] = jnp.zeros_like(acc)

    left = jnp.concatenate([ref[:, LANES * u : LANES * (u + 7)] for u in range(3) for ref in columns], axis=0)
    last = jnp.where(q < 3, r_ref[:, 64:, :], jnp.zeros((7, 64, LANES), BF))
    right = jnp.concatenate([jnp.concatenate([r_ref[i, :64], last[i]], axis=0) for i in range(7)], axis=1)
    acc[...] += dot_nt(left, right)

    @pl.when(q == 3)
    def _():
        for u in range(3):
            for v in range(3):
                at = 256 * u + 64 * v
                part = acc[at : at + 64, :64] + acc[at + 64 : at + 128, 64:]
                g_ref[:, 192 * u + 64 * v : 192 * u + 64 * v + 64] = part.T * (1.0 / LOSS_SCALE)


def wconv3(a2, r3):
    return call(
        wconv3_kernel,
        sds((64, 576), F32),
        [pl.BlockSpec((64, 9 * LANES), lambda q, k=k: (jnp.minimum(2 * q + k, 8), 0)) for k in range(4)]
        + [pl.BlockSpec((7, 128, LANES), lambda q: (0, q, 0))],
        whole((64, 576)),
        us=7,
        grid=(4,),
        scratch=[pltpu.VMEM((768, 128), F32)],
    )(a2, a2, a2, a2, r3.reshape(7, 448, LANES))


def wconv2_kernel(a0_ref, a1_ref, r_ref, g_ref, acc):
    q = pl.program_id(0)

    @pl.when(q == 0)
    def _():
        acc[...] = jnp.zeros_like(acc)

    left = jnp.concatenate(
        [ref[e, :, LANES * t : LANES * (t + 9)] for t in range(2) for e in range(2) for ref in (a0_ref, a1_ref)],
        axis=0,
    )
    last = jnp.where(q < 4, r_ref[64:, :], jnp.zeros((64, 9 * LANES), BF))
    acc[...] += dot_nt(left, jnp.concatenate([r_ref[:64, :], last], axis=0))

    @pl.when(q == 4)
    def _():
        for u in range(4):
            at = 192 * u
            g_ref[128 * u : 128 * u + 128, :] = (acc[at : at + 128, :64] + acc[at + 64 : at + 192, 64:]) * (
                1.0 / LOSS_SCALE
            )


def wconv2(a1, r2):
    return call(
        wconv2_kernel,
        sds((512, 64), F32),
        [
            pl.BlockSpec((2, 128, 10 * LANES), lambda q: (0, q, 0)),
            pl.BlockSpec((2, 64, 10 * LANES), lambda q: (0, jnp.minimum(2 * q + 2, 9), 0)),
            pl.BlockSpec((128, 9 * LANES), lambda q: (q, 0)),
        ],
        whole((512, 64)),
        us=9,
        grid=(5,),
        scratch=[pltpu.VMEM((768, 128), F32)],
    )(hbm(a1), hbm(a1), r2)


def wconv1_kernel(x_ref, x0_ref, r_ref, g_ref, acc, before):
    step = pl.program_id(0)

    @pl.when(step == 0)
    def _():
        acc[...] = jnp.zeros_like(acc)
        before[...] = x0_ref[...]

    def column(dy, rows, c):
        if c:
            return x_ref[dy, rows, LANES * (c - 1) : LANES * c]
        return before[dy, rows, :]

    total = acc[...]
    for g in range(5):
        rows = slice(64 * g, 64 * g + 80)
        left = jnp.concatenate(
            [
                jnp.concatenate([column(dy, rows, ii + t) for ii in range(4)], axis=1)
                for t in range(2)
                for dy in range(4)
            ],
            axis=0,
        )
        right = jnp.concatenate(
            [r_ref[ii % 2, 128 * g : 128 * g + 128, LANES * (ii // 2) : LANES * (ii // 2 + 1)] for ii in range(4)],
            axis=1,
        )
        total = total + dot_nt(left, right)
    acc[...] = total
    before[...] = x_ref[:, :, 3 * LANES :]

    @pl.when(step == 4)
    def _():
        for dy in range(8):
            part = jnp.zeros((32, 32), F32)
            for jj in range(4):
                part = part + acc[80 * dy + 16 * jj : 80 * dy + 16 * jj + 32, 32 * jj : 32 * jj + 32]
            g_ref[32 * dy : 32 * dy + 32, :] = part * (1.0 / LOSS_SCALE)


def wconv1(xt, x0, r1):
    return call(
        wconv1_kernel,
        sds((256, 32), F32),
        [
            pl.BlockSpec((4, 336, 4 * LANES), lambda s: (0, 0, s)),
            whole((4, 336, LANES)),
            pl.BlockSpec((2, 640, 2 * LANES), lambda s: (0, 0, s)),
        ],
        whole((256, 32)),
        us=13,
        grid=(5,),
        scratch=[pltpu.VMEM((640, 128), F32), pltpu.VMEM((4, 336, LANES), BF)],
    )(hbm(xt), hbm(x0), hbm(r1))


SMALL_ROWS = 704


def lanes_of(shards):
    return max(1, 128 // shards)


def slot_rows(capacity):
    return (capacity + 7) // 8 * 8


def pack_kernel(shards, capacity, flag_ref, *refs):
    b1_refs, (b2_ref, b3_ref, g1_ref, g2_ref, g3_ref, db_ref, hb_ref, loss_ref, owner_ref, p_ref, w) = refs[:-11], refs[-11:]
    scale = 1.0 / LOSS_SCALE
    w[...] = jnp.zeros_like(w)
    for k in range(4):
        w[64 * k : 64 * k + 64, :] = g3_ref[:, 128 * k : 128 * k + 128]
    w[256:320, :64] = g3_ref[:, 512:]
    w[320:576, :64] = g2_ref[:256, :]
    w[320:576, 64:] = g2_ref[256:, :]
    w[576:704, :32] = g1_ref[:128, :]
    w[576:704, 32:64] = g1_ref[128:, :]
    total = b1_refs[0][...]
    for ref in b1_refs[1:]:
        total = total + ref[...]
    for column, value in ((64, total), (65, b2_ref[...]), (66, b3_ref[...])):
        w[576 : 576 + value.shape[0], column : column + 1] = jnp.sum(value, axis=1, keepdims=True) * scale
    for k in range(4):
        w[576:704, 67 + k : 68 + k] = db_ref[128 * k : 128 * k + 128, :] * scale
    for half in range(2):
        for k in range(4):
            start = 459 * half + 128 * k
            size = min(128, 459 * (half + 1) - start)
            w[576 : 576 + size, 71 + 4 * half + k : 72 + 4 * half + k] = hb_ref[start : start + size, :]

    owner = owner_ref[...]
    rows = owner.shape[1]
    owner_f = owner.astype(F32)
    down = jnp.broadcast_to(owner_f, (8, rows)).T[:, :1]
    same = (down == owner_f) & (
        lax.broadcasted_iota(jnp.int32, (rows, rows), 0) < lax.broadcasted_iota(jnp.int32, (rows, rows), 1)
    )
    slot = jnp.sum(same.astype(F32), axis=0, keepdims=True)
    group, height = lanes_of(shards), slot_rows(capacity)
    place = lax.broadcasted_iota(jnp.int32, (height, rows), 0).astype(F32)
    spread = jnp.where(place == slot, loss_ref[...], 0.0).astype(BF)
    lane = lax.broadcasted_iota(jnp.int32, (128, rows), 0)
    here = shards * lax.rem(owner, group) + flag_ref[2]
    for g in range(shards // group):
        hot = ((lane == here) & (owner // group == g)).astype(BF)
        w[SMALL_ROWS + height * g : SMALL_ROWS + height * g + height, :] = dot_nt(spread, hot)
    p_ref[...] = w[...].astype(BF)


def pack(flag, b1s, shards, capacity, *ins):
    total = SMALL_ROWS + shards // lanes_of(shards) * slot_rows(capacity)
    ins = tuple(b1s) + ins
    return call(
        functools.partial(pack_kernel, shards, capacity),
        sds((total, 128), BF),
        [pl.BlockSpec(memory_space=pltpu.SMEM)] + [whole(a.shape) for a in ins],
        whole((total, 128)),
        scratch=[pltpu.VMEM((total, 128), F32)],
        us=3,
    )(flag, *ins)


def split_kernel(shards, capacity, flag_ref, own_ref, got_ref, k1, b1, k2, b2, k3, b3, db, hb, prio, w):
    own = flag_ref[0] == 1
    w[...] = jnp.where(own, own_ref[...].astype(F32), got_ref[...].astype(F32))

    def pick(low, high):
        return jnp.where(own, low, high)

    k1[...] = pick(w[576:704, :32], w[576:704, 32:64])
    k2[...] = pick(w[320:576, :64], w[320:576, 64:])
    for n in range(9):
        rows = slice(64 * (n // 2), 64 * (n // 2) + 64)
        part = w[rows, 64 * (n % 2) : 64 * (n % 2) + 64]
        k3[n] = pick(part[:32], part[32:])
    columns = w[576:704, :].T
    b1[...] = pick(columns[64:65, :16], columns[64:65, 16:32])
    for ref, at in ((b2, 65), (b3, 66)):
        ref[...] = pick(columns[at : at + 1, :32], columns[at : at + 1, 32:64])
    for k in range(2):
        db[:, 128 * k : 128 * k + 128] = pick(columns[67 + k : 68 + k], columns[69 + k : 70 + k])
    for k in range(4):
        size = min(128, 459 - 128 * k)
        hb[:, 128 * k : 128 * k + size] = pick(columns[71 + k : 72 + k, :size], columns[75 + k : 76 + k, :size])
    group, height = lanes_of(shards), slot_rows(capacity)
    me = flag_ref[2]
    block = w[pl.ds(pl.multiple_of(SMALL_ROWS + height * (me // group), 8), height), :]
    if group > 1:
        block = pltpu.roll(block, lax.rem(128 - shards * lax.rem(me, group), 128), 1)
    half = capacity // 2
    prio[:, 0, :] = pick(block[:half, :shards], block[half : 2 * half, :shards])


def split(flag, own, got, shards, capacity):
    shapes = (
        (128, 32),
        (1, 16),
        (256, 64),
        (1, 32),
        (9, 32, 64),
        (1, 32),
        (1, 256),
        (1, 459),
        (capacity // 2, 1, shards),
    )
    return call(
        functools.partial(split_kernel, shards, capacity),
        tuple(sds(s, F32) for s in shapes),
        [pl.BlockSpec(memory_space=pltpu.SMEM), whole(own.shape), whole(got.shape)],
        [whole(s) for s in shapes],
        scratch=[pltpu.VMEM(own.shape, F32)],
        us=2,
    )(flag, own, got)


def unchunk_kernel(flag_ref, cur_ref, other_ref, d_ref, h_ref):
    core, code = flag_ref[1], flag_ref[3]
    for k in range(2):
        block = (2 * pl.program_id(0) + k) ^ code
        cur, other = cur_ref[block].astype(F32), other_ref[block].astype(F32)
        for lane, tile in enumerate((jnp.where(core == 0, cur, other), jnp.where(core == 0, other, cur))):
            d_ref[392 * k : 392 * k + 392, 128 * lane : 128 * lane + 128] = tile[:392]
            h_ref[120 * k : 120 * k + 120, 128 * lane : 128 * lane + 128] = tile[392:]


def unchunk(flag, cur, other):
    return call(
        unchunk_kernel,
        (sds((3136, 256), F32), sds((LOGITS, 256), F32)),
        [pl.BlockSpec(memory_space=pltpu.SMEM), whole(cur.shape), whole(other.shape)],
        [pl.BlockSpec((784, 256), lambda i: (i, 0)), pl.BlockSpec((240, 256), lambda i: (i, 0))],
        us=4,
        grid=(4,),
    )(flag, cur, other)


def after(value, *others):
    return lax.optimization_barrier((value,) + others)[0]


def hand(value):
    return lax.ppermute(value, "pair", [(0, 1)])


def swap(value, bit):
    devices = lax.axis_size("batch")
    return lax.ppermute(value, "batch", [(i, i ^ bit) for i in range(devices)])


def add(left, right):
    return (left.astype(F32) + right.astype(F32)).astype(BF)


def split_blocks(cur):
    devices = lax.axis_size("batch")
    spread = devices // 16
    if spread > 1:
        cur = cur.reshape(8, 2, spread, 512 // spread, 128).transpose(0, 2, 1, 3, 4)
        cur = cur.reshape(devices // 2, 2, 512 // spread, 128)
    return cur


def halve(cur, me, bit):
    mine = (me // bit) % 2
    pairs = cur.reshape((cur.shape[0] // 2, 2) + cur.shape[1:])
    send = lax.dynamic_index_in_dim(pairs, 1 - mine, axis=1, keepdims=False)
    keep = lax.dynamic_index_in_dim(pairs, mine, axis=1, keepdims=False)
    return keep, swap(send, bit)


def unmix(blocks, code):
    bit = 1
    while bit < blocks.shape[0]:
        pairs = blocks.reshape((-1, 2, bit) + blocks.shape[1:])
        blocks = jnp.where((code // bit) % 2 == 1, pairs[:, ::-1], pairs).reshape(blocks.shape)
        bit *= 2
    return blocks


def join(cur, other):
    return jnp.stack([cur, other], axis=1).reshape((2 * cur.shape[0],) + cur.shape[1:])


def local(
    frames,
    kernel_first,
    bias_first,
    kernel_second,
    bias_second,
    kernel_third,
    bias_third,
    dense_weight,
    dense_bias,
    head_weight,
    head_bias,
    taken_actions,
    greedy_actions,
    done_flags,
    bin_lower,
    bin_fraction,
    owner_shard,
):
    online = lax.axis_index("pair") == 0
    me = lax.axis_index("batch")
    shards = lax.axis_size("batch")
    rows = frames.shape[1]
    capacity = 2 * ((rows + shards - 1) // shards)
    block = me // 2 if shards == 16 else me * 0
    flag = jnp.stack([online.astype(jnp.int32), me % 2, me, block]).astype(jnp.int32)
    xv = frames[0].transpose(2, 3, 1, 0)
    k1, k2, k3 = kernel_first[0], kernel_second[0], kernel_third[0]
    ones = jnp.zeros((16, LANES), BF).at[0].set(1)
    t1, t2, t3, b2, kernels = bands(k1, bias_first, k2, bias_second, k3, bias_third)

    kernels = hand(kernels)
    a1, s1, xt, early, x0 = conv1(xv, t1, ones, 0, EARLY, ())
    early = hand(after(early, kernels))
    a1, s1, xt, late = conv1(xv, t1, ones, EARLY, 10, (a1, s1, xt))
    late = hand(late)
    a2, s2, a3, s3 = conv23(a1, t2, b2, t3, ones)
    wd = dense_weight[0]
    wht = head_weight[0].T
    pd = lax.dot_general(wd, a3, (((0,), (0,)), ((), ())), preferred_element_type=F32)
    taken = taken_actions[None, :]
    sel = jnp.where(online, taken, greedy_actions[None, :])
    h, sd, lp, cho = head(pd, dense_bias, wht, head_bias, sel)
    cho = lax.ppermute(cho, "pair", [(1, 0)])
    t3b, t2b, t2b_online, t1b = bands_back(after(flag, lp), k1, k2, k3, kernels)
    row_loss, rh, hb = loss(after(cho, t1b), done_flags[None, :], bin_lower.T, bin_fraction.T, lp, taken)

    diff_dense = lax.dot_general(wht, rh, (((0,), (0,)), ((), ())), preferred_element_type=F32)
    diff_dense = diff_dense * (0.5 * sd.astype(F32))
    rd = diff_dense.astype(BF)
    db = jnp.sum(diff_dense, axis=1, keepdims=True)

    keep, send = wdense(flag, a3, after(rd, early), rh, h)
    cur = split_blocks(add(keep, swap(send, 1)))
    keep, got = halve(cur, me, 2)

    r3, b3g, r2, r2p, b2g = dthird(wd, rd, s3, t3b, s2)
    r2p = hand(r2p)
    r1, near0, near1, b1g = dconv2(r2, t2b, s1, FAR, 10 - FAR, True, None)
    cur = add(after(keep, b1g), got)
    keep, far = halve(cur, me, 4)
    r1, b1g_far = dconv2(after(r2, got, late), t2b, s1, 0, FAR, False, r1)
    b1s = [b1g, b1g_far]
    g3 = wconv3(a2, after(r3, b1g_far))
    bit = 4
    while 2 * bit < shards:
        cur = add(after(keep, g3) if bit == 4 else keep, far)
        bit *= 2
        keep, far = halve(cur, me, bit)
    g1 = wconv1(xt, x0, after(r1, g3))
    chunk = add(after(keep, g1), far)[0]
    far_chunk = hand(chunk[1])
    near0 = hand(after(near0, far))
    near1 = hand(after(near1, far))
    mine = jnp.where(online, chunk[0], far_chunk)
    g2 = wconv2(a1, after(r2, chunk))

    cur = mine[None]
    part = swap(cur, bit)
    small = pack(after(flag, part, r2p), b1s, shards, capacity, b2g, b3g, g1, g2, g3, db, hb, row_loss, owner_shard.T)
    small = add(small, swap(small, 1))
    got = swap(small, 2)
    cur = join(cur, part)
    part = swap(cur, bit // 2)
    out, edge = dframes(flag, after(r1, small, cur, near0), (r2p, early, late, t2b_online), t1b, rows, 0, FAR, None, None)
    cur = join(after(cur, edge), part)
    small = add(after(small, edge), got)
    part, got = swap(cur, bit // 4), swap(small, 4)
    small = add(small, got)
    got = swap(small, 8)
    small = add(after(small, near1), got)
    cur = join(after(cur, got), part)
    lower = 16
    while lower < shards:
        small = add(small, swap(small, lower))
        cur = join(cur, swap(cur, 2 * bit // lower))
        lower *= 2
    other = swap(cur, 1)
    far_small = hand(small)
    out, edge = dframes(flag, after(r1, cur, small), [near0, near1], t1b, rows, FAR, 10 - FAR, edge, out)
    if shards != 16:
        cur, other = (unmix(v, me // 2).reshape(8, 512, 128) for v in (cur, other))
    dense_out, head_out = unchunk(flag, cur, other)
    o = split(flag, small, far_small, shards, capacity)
    return (
        o[0].reshape(4, 8, 4, 32),
        o[1].reshape(16),
        o[2].reshape(2, 4, 32, 64),
        o[3].reshape(32),
        o[4].reshape(3, 3, 32, 64).transpose(0, 1, 3, 2),
        o[5].reshape(32),
        dense_out,
        o[6].reshape(256),
        head_out.T,
        o[7].reshape(459),
        out.transpose(3, 2, 0, 1),
        o[8].transpose(1, 2, 0),
    )


def solution(mesh):
    return jax.shard_map(
        local,
        mesh=mesh,
        in_specs=(
            P("pair", "batch", None, None, None),
            P("pair", None, None, None, None),
            P("pair", None),
            P("pair", None, None, None, None),
            P("pair", None),
            P("pair", None, None, None, None),
            P("pair", None),
            P("pair", None, None),
            P("pair", None),
            P("pair", None, None),
            P("pair", None),
            P("batch"),
            P("batch"),
            P("batch"),
            P("batch", None),
            P("batch", None),
            P("batch", None),
        ),
        out_specs=(
            P("pair", None, None, None),
            P("pair"),
            P("pair", None, None, None),
            P("pair"),
            P(None, None, None, "pair"),
            P("pair"),
            P(None, "pair"),
            P("pair"),
            P("pair", None),
            P("pair"),
            P("batch", "pair", None, None),
            P("batch", None, "pair"),
        ),
        check_vma=False,
    )
```

```python
import functools

import jax
import jax.numpy as jnp
from jax import lax
from jax.experimental import pallas as pl
from jax.experimental.pallas import tpu as pltpu
from jax.sharding import PartitionSpec as P

ACT = 18
ATOMS = 51
LOGITS = ACT * ATOMS
LOSS_SCALE = 256
LANES = 256
BF = jnp.bfloat16
F32 = jnp.float32
VMEM_BIG = 24 << 20
FAR = 6
EARLY = 3
ALONE = 1
NEAR = ((6, 4),)


def cost(us):
    return pl.CostEstimate(flops=int(us * 0.4e9), bytes_accessed=0, transcendentals=0)


def call(kernel, out, ins, outs, us, grid=None, scratch=()):
    return pl.pallas_call(
        kernel,
        out_shape=out,
        grid=() if grid is None else grid,
        in_specs=ins,
        out_specs=outs,
        scratch_shapes=list(scratch),
        compiler_params=pltpu.CompilerParams(vmem_limit_bytes=VMEM_BIG),
        cost_estimate=cost(us),
    )


def whole(shape):
    return pl.BlockSpec(shape, lambda *_: (0,) * len(shape))


def hbm(value):
    return pltpu.with_memory_space_constraint(value, pltpu.HBM)


def sds(shape, dtype):
    return jax.ShapeDtypeStruct(shape, dtype)


def dot(left, right):
    return jnp.dot(left, right, preferred_element_type=F32)


def dot_nt(left, right):
    return lax.dot_general(left, right, (((1,), (1,)), ((), ())), preferred_element_type=F32)


def act_slope(half):
    tan = jnp.tanh(half)
    up = 1.0 + tan
    act = half * up
    return act, up + act * (1.0 - tan)


def second_bands(k2n, w2b):
    for e in range(2):
        for t in range(2):
            u = 2 * t + e
            for j in range(6):
                lo = max(0, 2 * j - 2)
                hi = min(10, 2 * j + 2)
                v0 = lo - (2 * j - 2)
                w2b[320 * e + 32 * lo : 320 * e + 32 * hi, 384 * t + 64 * j : 384 * t + 64 * j + 64] = k2n[
                    128 * u + 32 * v0 : 128 * u + 32 * (v0 + hi - lo), :
                ]


def turned(kernel, bias=None):
    flat = kernel[...].astype(F32)
    flat = flat.reshape(-1, flat.shape[-1])
    if bias is not None:
        bias = jnp.broadcast_to(bias[...].astype(F32), (8, flat.shape[1])).T[:, :1]
    return flat, flat.T, bias


def bands_kernel(k1, b1, k2, b2, k3, b3, t1, t2, t3, b2c, send, w1, w2, w3):
    for ref in (w1, w2, w3):
        ref[...] = jnp.zeros_like(ref)
    _, k1t, b1c = turned(k1, b1)
    k2n, k2t, b2t = turned(k2, b2)
    _, k3t, b3c = turned(k3, b3)
    send[:512, :] = k2n.astype(BF)
    send[512:, :32] = k1[:, :, 2:, :].astype(F32).reshape(128, 32).astype(BF)
    send[512:, 32:] = jnp.zeros((128, 32), BF)
    for jj in range(10):
        for dy in range(8):
            w1[32 * jj : 32 * jj + 32, 176 * dy + 16 * jj : 176 * dy + 16 * jj + 32] = k1t[:, 32 * dy : 32 * dy + 32]
        w1[32 * jj : 32 * jj + 32, 1408:1409] = b1c
    for jj in range(3):
        for u in range(4):
            w2[64 * jj : 64 * jj + 64, 256 * u + 64 * jj : 256 * u + 64 * jj + 128] = k2t[:, 128 * u : 128 * u + 128]
        b2c[64 * jj : 64 * jj + 64, :] = 0.5 * b2t
    for j in range(7):
        for u in range(3):
            w3[64 * j : 64 * j + 64, 576 * u + 64 * j : 576 * u + 64 * j + 192] = k3t[:, 192 * u : 192 * u + 192]
        w3[64 * j : 64 * j + 64, 1728:1729] = b3c
    t1[...] = (0.5 * w1[...]).astype(BF)
    t2[...] = (0.5 * w2[...]).astype(BF)
    t3[...] = (0.5 * w3[...]).astype(BF)


def bands(*ins):
    shapes = ((320, 1424), (192, 1024), (448, 1744))
    return call(
        bands_kernel,
        (sds(shapes[0], BF), pltpu.HBM(shapes[1], BF), pltpu.HBM(shapes[2], BF), sds((192, 1), F32), pltpu.HBM((640, 64), BF)),
        [whole(a.shape) for a in ins],
        [whole(s) for s in shapes] + [whole((192, 1)), whole((640, 64))],
        us=3,
        scratch=[pltpu.VMEM(s, F32) for s in shapes],
    )(*[hbm(v) for v in ins])


def bands_back_kernel(flag_ref, k1, k2, k3, got, t3b, t2b, t2o, t1b, w3b, w2b, w1b):
    own = flag_ref[0] == 1
    for ref in (w3b, w2b, w1b):
        ref[...] = jnp.zeros_like(ref)
    k3n, k2n = turned(k3)[0], turned(k2)[0]
    for j in range(7):
        for u in range(3):
            w3b[64 * j : 64 * j + 192, 448 * (2 - u) + 64 * j : 448 * (2 - u) + 64 * j + 64] = k3n[192 * u : 192 * u + 192, :]
    t3b[...] = (0.5 * w3b[...]).astype(BF)
    second_bands(k2n, w2b)
    t2b[...] = (0.5 * w2b[...]).astype(BF)
    second_bands(jnp.where(own, k2n, got[:512, :].astype(F32)), w2b)
    t2o[...] = (0.5 * w2b[...]).astype(BF)
    half = jnp.where(own, k1[:, :, :2, :].astype(F32).reshape(128, 32), got[512:, :32].astype(F32)).reshape(8, 16, 32)
    for dy in range(8):
        t, row = divmod(dy, 4)
        for j in range(8):
            lo = max(0, 4 * j - 4)
            hi = min(28, 4 * j + 4)
            d0 = lo - (4 * j - 4)
            w1b[56 * row + 2 * lo : 56 * row + 2 * hi, 256 * t + 32 * j : 256 * t + 32 * j + 32] = half[
                dy, 2 * d0 : 2 * (d0 + hi - lo), :
            ]
    t1b[...] = w1b[...].astype(BF)


def bands_back(flag, *ins):
    shapes = ((576, 1344), (640, 768), (640, 768), (224, 512))
    return call(
        bands_back_kernel,
        tuple(pltpu.HBM(s, BF) for s in shapes),
        [pl.BlockSpec(memory_space=pltpu.SMEM)] + [whole(a.shape) for a in ins],
        [whole(s) for s in shapes],
        us=4,
        scratch=[pltpu.VMEM(s, F32) for s in (shapes[0], shapes[1], shapes[3])],
    )(flag, *[hbm(v) for v in ins])


def pack_rows(part, n):
    lane = lax.broadcasted_iota(jnp.int32, (n // 4, 128), 1)
    tail = [part[n // 4 * k : n // 4 * (k + 1), 128:] for k in range(4)]
    packed = [jnp.where(lane < 96, tail[k], pltpu.roll(tail[3], 96 - 32 * k, 1)) for k in range(3)]
    return jnp.concatenate([part[:, :128]] + packed, axis=0)


def unpack_rows(packed, n):
    lane = lax.broadcasted_iota(jnp.int32, (n // 4, 128), 1)
    tail = [packed[n + n // 4 * k : n + n // 4 * (k + 1)] for k in range(3)]
    last = pltpu.roll(tail[0], 32, 1)
    last = jnp.where(lane < 32, last, jnp.where(lane < 64, pltpu.roll(tail[1], 64, 1), pltpu.roll(tail[2], 96, 1)))
    return jnp.concatenate([packed[:n], jnp.concatenate(tail + [last], axis=0)], axis=1)


def conv1_kernel(rows, start, packs, first_ref, xa_ref, xb_ref, t1_ref, ones_ref, *rest):
    cells = rest[-1]
    a_ref, s_ref, xt_ref, p_ref = rest[-5:-1] if start else rest[-6:-2]
    m = pl.program_id(0) + start

    def relay(ref, slot):
        for dy in range(4):
            cells[slot, dy, :, :rows] = ref[dy].reshape(336, rows)

    @pl.when(m == start)
    def _():
        cells[...] = jnp.zeros_like(cells)
        relay(first_ref, 0)
        if not start:
            rest[-2][...] = cells[0]

    relay(xa_ref, 1)
    relay(xb_ref, 2)
    slopes = []
    for e in range(2):
        parts_of = lambda window, e=e: [cells[e + t, dy, window, :] for t in range(2) for dy in range(4)]
        row = []
        for g in range(2):
            half = dot(t1_ref[...], jnp.concatenate(parts_of(pl.ds(160 * g, 176)) + [ones_ref[...]], axis=0))
            act, slope = act_slope(half)
            a_ref[e, 320 * g : 320 * g + 320, :] = act.astype(BF)
            s_ref[e, 320 * g : 320 * g + 320, :] = slope.astype(BF)
            row.append(slope)
        slopes.append(row)
    if not start:
        for e in range(2):
            p_ref[0, e] = pack_rows(jnp.concatenate(slopes[e], axis=0), 640).astype(BF)
    for dy in range(4):
        xt_ref[dy, :, :LANES] = cells[1, dy]
        xt_ref[dy, :, LANES:] = cells[2, dy]
        cells[0, dy] = cells[2, dy]
    if start:

        @pl.when(m < packs)
        def _():
            for e in range(2):
                p_ref[0, e] = pack_rows(s_ref[e].astype(F32), 640).astype(BF)


def conv1(xv, t1, ones, start, stop, before):
    rows = xv.shape[3]
    packs = min(stop, FAR)
    cell = lambda f: pl.BlockSpec((4, 84, 4, rows), lambda m: (f(m + start), 0, 0, 0))
    out = pl.BlockSpec((2, 640, LANES), lambda m: (0, 0, m + start))
    outs = [
        out,
        out,
        pl.BlockSpec((4, 336, 2 * LANES), lambda m: (0, 0, m + start)),
        pl.BlockSpec((1, 2, 1120, 128), lambda m: (jnp.minimum(m, packs - start - 1), 0, 0, 0)),
    ]
    shapes = [
        pltpu.HBM((2, 640, 10 * LANES), BF),
        pltpu.HBM((2, 640, 10 * LANES), BF),
        pltpu.HBM((4, 336, 20 * LANES), BF),
        pltpu.HBM((packs - start, 2, 1120, 128), BF),
    ]
    if not start:
        outs.append(whole((4, 336, LANES)))
        shapes.append(pltpu.HBM((4, 336, LANES), BF))
    return pl.pallas_call(
        functools.partial(conv1_kernel, rows, start, packs),
        out_shape=tuple(shapes),
        grid=(stop - start,),
        in_specs=[
            pl.BlockSpec((4, 84, 4, rows), lambda m: (2 * start, 0, 0, 0)),
            cell(lambda m: 2 * m + 1),
            cell(lambda m: 2 * m + 2),
            whole((320, 1424)),
            whole((16, LANES)),
        ]
        + [pl.BlockSpec(memory_space=pl.ANY)] * len(before),
        out_specs=outs,
        scratch_shapes=[pltpu.VMEM((3, 4, 336, LANES), BF)],
        input_output_aliases={5 + n: n for n in range(len(before))},
        compiler_params=pltpu.CompilerParams(vmem_limit_bytes=VMEM_BIG),
        cost_estimate=cost(0.02 * (stop - start)),
    )(hbm(xv), hbm(xv), hbm(xv), t1, ones, *[hbm(v) for v in before])


def conv23_kernel(r0_ref, r1_ref, t2_ref, b2_ref, t3_ref, ones_ref, a2_ref, s2_ref, a3_ref, s3_ref, keep):
    g = pl.program_id(0)

    def third():
        window = pl.ds(pl.multiple_of(576 * (g - 3), 64), 1728)
        half = dot(t3_ref[...], jnp.concatenate([keep[window, :], ones_ref[...]], axis=0))
        act, slope = act_slope(half)
        a3_ref[...] = act.astype(BF)
        s3_ref[...] = slope.astype(BF)

    def second():
        for n in range(3):
            window = pl.ds(192 * n, 256)
            parts = [r0_ref[0, window, :], r0_ref[1, window, :], r1_ref[0, window, :], r1_ref[1, window, :]]
            half = dot(t2_ref[...], jnp.concatenate(parts, axis=0)) + b2_ref[...]
            act, slope = act_slope(half)
            act = act.astype(BF)
            a2_ref[192 * n : 192 * n + 192, :] = act
            keep[pl.ds(pl.multiple_of(576 * g + 192 * n, 64), 192), :] = act
            s2_ref[192 * n : 192 * n + 192, :] = slope.astype(BF)

    @pl.when(g < 3)
    def _():
        second()

    @pl.when((g >= 3) & (g < 9))
    def _():
        third()
        second()

    @pl.when(g == 9)
    def _():
        third()


def conv23(a1, t2, b2, t3, ones):
    row = lambda t: pl.BlockSpec((2, 640, LANES), lambda g: (0, 0, jnp.minimum(g, 8) + t))
    out2 = pl.BlockSpec((576, LANES), lambda g: (0, jnp.minimum(g, 8)))
    out3 = pl.BlockSpec((448, LANES), lambda g: (jnp.maximum(g - 3, 0), 0))
    return call(
        conv23_kernel,
        (pltpu.HBM((576, 9 * LANES), BF), pltpu.HBM((576, 9 * LANES), BF), sds((3136, LANES), BF), pltpu.HBM((3136, LANES), BF)),
        [row(0), row(1), whole((192, 1024)), whole((192, 1)), whole((448, 1744)), whole((16, LANES))],
        [out2, out2, out3, out3],
        us=14,
        grid=(10,),
        scratch=[pltpu.VMEM((9 * 576, LANES), BF)],
    )(hbm(a1), hbm(a1), hbm(t2), b2, hbm(t3), ones)


def head_kernel(rows, pd_ref, bd_ref, wh_ref, bh_ref, sel_ref, act_ref, slope_ref, lp_ref, cho_ref, lg_ref):
    bd = jnp.broadcast_to(bd_ref[...].astype(F32), (8, 512)).T[:, :1]
    bh = jnp.broadcast_to(bh_ref[...].astype(F32), (8, LOGITS)).T[:, :1]
    act, slope = act_slope((pd_ref[...] + bd) * 0.5)
    act_ref[...] = act.astype(BF)
    slope_ref[...] = slope.astype(BF)
    lg_ref[...] = dot(wh_ref[...], act_ref[...]) + bh
    sel = sel_ref[...]
    pick = jnp.zeros((ATOMS, rows), F32)
    for a in range(ACT):
        pick = jnp.where(sel == a, lg_ref[ATOMS * a : ATOMS * a + ATOMS, :rows], pick)
    shifted = pick - jnp.max(pick, axis=0, keepdims=True)
    grown = jnp.exp(shifted)
    total = jnp.sum(grown, axis=0, keepdims=True)
    cho_ref[...] = (grown / total).astype(BF)
    lp_ref[...] = shifted - jnp.log(total)


def head(pd, bd, wht, bh, sel):
    rows = sel.shape[1]
    ins = (pd, bd, wht, bh, sel)
    outs = (((512, LANES), BF), ((512, LANES), BF), ((ATOMS, rows), F32), ((ATOMS, rows), BF))
    return call(
        functools.partial(head_kernel, rows),
        tuple(sds(*o) for o in outs),
        [whole(a.shape) for a in ins],
        [whole(o[0]) for o in outs],
        scratch=[pltpu.VMEM((LOGITS, LANES), F32)],
        us=3,
    )(*ins)


def loss_kernel(rows, cho_ref, done_ref, low_ref, frac_ref, lp_ref, taken_ref, loss_ref, rh_ref, hb_ref, d_ref):
    atoms = lax.broadcasted_iota(jnp.int32, (ATOMS, rows), 0)
    done = done_ref[...].astype(F32)
    mass = (1.0 - done) * cho_ref[...].astype(F32) + done * (atoms == 0).astype(F32)
    frac = frac_ref[...]
    stay = mass * (1.0 - frac)
    move = mass * frac
    low = low_ref[...]
    proj = jnp.zeros((ATOMS, rows), F32)
    for i in range(ATOMS):
        gap = atoms - low[i : i + 1, :]
        proj = proj + jnp.where(gap == 0, stay[i : i + 1, :], jnp.where(gap == 1, move[i : i + 1, :], 0.0))
    lp = lp_ref[...]
    loss_ref[...] = -jnp.sum(proj * lp, axis=0, keepdims=True)
    diff = (jnp.sum(proj, axis=0, keepdims=True) * jnp.exp(lp) - proj) * LOSS_SCALE
    taken = taken_ref[...]
    for a in range(ACT):
        d_ref[ATOMS * a : ATOMS * a + ATOMS, :] = jnp.where(taken == a, diff, 0.0)
    rh_ref[...] = jnp.zeros_like(rh_ref)
    rh_ref[:, :rows] = d_ref[...].astype(BF)
    hb_ref[...] = jnp.sum(d_ref[...], axis=1, keepdims=True) * (1.0 / LOSS_SCALE)


def loss(cho, done, low, frac, lp, taken):
    rows = taken.shape[1]
    ins = (cho, done, low, frac, lp, taken)
    outs = (((1, rows), F32), ((LOGITS, LANES), BF), ((LOGITS, 1), F32))
    return call(
        functools.partial(loss_kernel, rows),
        tuple(sds(*o) for o in outs),
        [whole(a.shape) for a in ins],
        [whole(o[0]) for o in outs],
        scratch=[pltpu.VMEM((LOGITS, rows), F32)],
        us=3,
    )(*ins)


def dthird_kernel(w_ref, rd_ref, s3_ref, t_ref, s2_ref, r3_ref, b3_ref, r2_ref, p_ref, b2_ref, keep):
    g = pl.program_id(0)

    def third():
        diff = dot(w_ref[...], rd_ref[...]) * (0.5 * s3_ref[...].astype(F32))
        part = diff.astype(BF)
        r3_ref[...] = part
        keep[pl.ds(pl.multiple_of(448 * (g + 2), 64), 448), :] = part
        b3_ref[...] += jnp.sum(diff.reshape(7, 64, LANES), axis=0)

    def second():
        window = pl.ds(pl.multiple_of(448 * (g - 1), 64), 1344)
        diff = dot(t_ref[...], keep[window, :]) * s2_ref[...].astype(F32)
        r2_ref[...] = diff.astype(BF)
        b2_ref[...] += jnp.sum(diff.reshape(9, 64, LANES), axis=0)
        return diff

    def pack(diff):
        p_ref[0] = pack_rows(diff, 576).astype(BF)

    @pl.when(g == 0)
    def _():
        b3_ref[...] = jnp.zeros_like(b3_ref)
        b2_ref[...] = jnp.zeros_like(b2_ref)
        keep[:896, :] = jnp.zeros((896, LANES), BF)
        keep[4032:, :] = jnp.zeros((896, LANES), BF)
        third()

    @pl.when((g >= 1) & (g < 7))
    def _():
        pack(second())
        third()

    @pl.when((g >= 7) & (g <= FAR))
    def _():
        pack(second())

    @pl.when(g > FAR)
    def _():
        second()


def dthird(wd, rd, s3, t3b, s2):
    block3 = pl.BlockSpec((448, LANES), lambda g: (jnp.minimum(g, 6), 0))
    block2 = pl.BlockSpec((576, LANES), lambda g: (0, jnp.maximum(g - 1, 0)))
    packed = pl.BlockSpec((1, 1008, 128), lambda g: (jnp.clip(g - 1, 0, FAR - 1), 0, 0))
    return call(
        dthird_kernel,
        (
            sds((3136, LANES), BF),
            sds((64, LANES), F32),
            sds((576, 9 * LANES), BF),
            pltpu.HBM((FAR, 1008, 128), BF),
            sds((64, LANES), F32),
        ),
        [
            pl.BlockSpec((448, 512), lambda g: (jnp.minimum(g, 6), 0)),
            whole((512, LANES)),
            block3,
            whole((576, 1344)),
            block2,
        ],
        [block3, whole((64, LANES)), block2, packed, whole((64, LANES))],
        us=12,
        grid=(10,),
        scratch=[pltpu.VMEM((4928, LANES), BF)],
    )(hbm(wd), rd, hbm(s3), hbm(t3b), hbm(s2))


def first_diffs(t, cur, prev):
    none = jnp.zeros((64, LANES), BF)
    halves = []
    for h in range(2):
        if h == 0:
            parts = [none, cur[:320], none, prev[:320]]
        else:
            parts = [cur[256:], none, prev[256:], none]
        halves.append(dot(t, jnp.concatenate(parts, axis=0)))
    return [jnp.concatenate([half[320 * e : 320 * e + 320] for half in halves], axis=0) for e in range(2)]


def dconv2_kernel(first, packs, cur_ref, prev_ref, t_ref, s_ref, *rest):
    r_ref, b_ref = rest[-4 if packs else -2], rest[-1]
    q = pl.program_id(0)
    m = 2 * q + first
    zero = jnp.zeros((576, LANES), BF)

    @pl.when(pl.program_id(0) == 0)
    def _():
        b_ref[...] = jnp.zeros_like(b_ref)

    r2 = [
        jnp.where(m > 0, prev_ref[...], zero),
        cur_ref[:, :LANES],
        jnp.where(m < 8, cur_ref[:, LANES:], zero),
    ]
    total = b_ref[...]
    for k in range(2):
        lanes = slice(LANES * k, LANES * (k + 1))
        for e, part in enumerate(first_diffs(t_ref[...], r2[k + 1], r2[k])):
            part = part * s_ref[e, :, lanes].astype(F32)
            r_ref[e, :, lanes] = part.astype(BF)
            if packs:
                value = pack_rows(part, 640).astype(BF)
                for step in range(2):

                    @pl.when(q == step)
                    def _(at=2 * step + k, e=e, value=value):
                        if at < ALONE:
                            rest[-3][at, e] = value
                        else:
                            rest[-2][at - ALONE, e] = value

            total = total + jnp.sum(part.reshape(20, 32, LANES), axis=0)
    b_ref[...] = total


def dconv2(r2, t2b, s1, first, count, packs, r1):
    block = pl.BlockSpec((2, 640, 2 * LANES), lambda q: (0, 0, q + first // 2))
    ins = [r2, r2, hbm(t2b), hbm(s1)]
    in_specs = [
        pl.BlockSpec((576, 2 * LANES), lambda q: (0, q + first // 2)),
        pl.BlockSpec((576, LANES), lambda q: (0, jnp.maximum(2 * q + first - 1, 0))),
        whole((640, 768)),
        block,
    ]
    aliases = {}
    if r1 is not None:
        ins.append(hbm(r1))
        in_specs.append(pl.BlockSpec(memory_space=pl.ANY))
        aliases = {4: 0}
    parts = [(ALONE, 2, 1120, 128), (count - ALONE, 2, 1120, 128)] if packs else []
    shapes = [pltpu.HBM((2, 640, 10 * LANES), BF)] + [pltpu.HBM(p, BF) for p in parts] + [sds((32, LANES), F32)]
    outs = [block] + [whole(p) for p in parts] + [whole((32, LANES))]
    return pl.pallas_call(
        functools.partial(dconv2_kernel, first, packs),
        out_shape=tuple(shapes),
        grid=(count // 2,),
        in_specs=in_specs,
        out_specs=outs,
        input_output_aliases=aliases,
        compiler_params=pltpu.CompilerParams(vmem_limit_bytes=VMEM_BIG),
        cost_estimate=cost(1.5 * count),
    )(*ins)


def frame_rows(r0, r1, t1b, o_ref, at, rows):
    none = jnp.zeros((32, LANES), BF)
    for g in range(3):
        if g == 0:
            parts = [none, r0[:224], none, r1[:224]]
        elif g == 1:
            parts = [r0[192:448], r1[192:448]]
        else:
            parts = [r0[416:], none, r1[416:], none]
        out = dot(t1b, jnp.concatenate(parts, axis=0)).astype(BF)
        for dy in range(4):
            o_ref[at + dy, 28 * g : 28 * g + 28, :, :] = out[56 * dy : 56 * dy + 56, :rows].reshape(28, 2, rows)


def dframes_kernel(rows, first, last, far, flag_ref, own_ref, before_ref, *rest):
    o_ref, edge_ref = rest[-2:]
    own = flag_ref[0] == 1
    q = pl.program_id(0)
    final = q == pl.num_programs(0) - 1
    t1b = rest[5] if far else rest[2]

    @pl.when(q == 0)
    def _():
        edge_ref[...] = jnp.zeros_like(edge_ref) if first == 0 else rest[6 if far else 3][...]

    def emit(four, before):
        for n, row in enumerate(four):
            frame_rows(row, before, t1b[...], o_ref, 4 * n, rows)
            before = row

    def own_rows():
        before = before_ref[0]
        if first == 0:
            before = jnp.where(q > 0, before, jnp.zeros_like(before))
        emit([own_ref[e, :, LANES * k : LANES * (k + 1)] for k in range(2) for e in range(2)], before)

    def other_rows():
        four = []
        for k in range(2):
            if far:
                cur = unpack_rows(rest[0][k].astype(F32), 576).astype(BF)
                if k == 0:
                    prev = unpack_rows(rest[1][0].astype(F32), 576).astype(BF)
                    if first == 0:
                        prev = jnp.where(q > 0, prev, jnp.zeros_like(prev))
                for e, part in enumerate(first_diffs(rest[4][...], cur, prev)):
                    m = 2 * q + k
                    soon = rest[2][jnp.minimum(m, EARLY - 1), e]
                    slope = jnp.where(m < EARLY, soon, rest[3][jnp.maximum(m - EARLY, 0), e]).astype(F32)
                    four.append((part * unpack_rows(slope, 640)).astype(BF))
                prev = cur
            else:
                for e in range(2):
                    early_part = rest[0][k, e] if k < ALONE else rest[1][k - ALONE, e]
                    part = jnp.where(q == 0, early_part, rest[1][2 + k - ALONE, e]).astype(F32)
                    four.append(unpack_rows(part, 640).astype(BF))
        emit(four, edge_ref[...])
        edge_ref[...] = four[3]

    more = jnp.logical_not(final) if last else True
    pl.when(own & more)(own_rows)
    pl.when(jnp.logical_not(own) & more)(other_rows)
    if last:

        @pl.when(final)
        def _():
            frame_rows(jnp.zeros((640, LANES), BF), jnp.where(own, before_ref[0], edge_ref[...]), t1b[...], o_ref, 0, rows)


def dframes(flag, own, got, t1b, rows, first, count, edge, out):
    far = len(got) > 2
    last = first + count == 10
    steps = count // 2
    at = lambda q: jnp.minimum(q, steps - 1)
    fixed = lambda shape: pl.BlockSpec(shape, lambda *_: (0,) * len(shape))
    ins = [flag, hbm(own), hbm(own)]
    in_specs = [
        pl.BlockSpec((2, 640, 2 * LANES), lambda q, *_: (0, 0, at(q) + first // 2)),
        pl.BlockSpec((1, 640, LANES), lambda q, *_: (1, 0, jnp.maximum(2 * q + first - 1, 0))),
    ]
    if far:
        r2p, early, late, t2b = got
        ins += [hbm(v) for v in (r2p, r2p, early, late, t2b)]
        in_specs += [
            pl.BlockSpec((2, 1008, 128), lambda q, *_: (q + first // 2, 0, 0)),
            pl.BlockSpec((1, 1008, 128), lambda q, *_: (jnp.maximum(2 * q + first - 1, 0), 0, 0)),
            fixed(early.shape),
            fixed(late.shape),
            fixed((640, 768)),
        ]
    else:
        ins += got
        in_specs += [fixed(v.shape) for v in got]
    ins.append(t1b)
    in_specs.append(fixed((224, 512)))
    aliases = {}
    if first:
        ins += [edge, hbm(out)]
        in_specs += [fixed((640, LANES)), pl.BlockSpec(memory_space=pl.ANY)]
        aliases = {len(ins) - 1: 0}
    return pl.pallas_call(
        functools.partial(dframes_kernel, rows, first, last, far),
        out_shape=(pltpu.HBM((84, 84, 2, rows), BF), sds((640, LANES), BF)),
        grid_spec=pltpu.PrefetchScalarGridSpec(
            num_scalar_prefetch=1,
            grid=(steps + 1 if last else steps,),
            in_specs=in_specs,
            out_specs=[pl.BlockSpec((16, 84, 2, rows), lambda q, *_: (q + first // 2, 0, 0, 0)), fixed((640, LANES))],
        ),
        input_output_aliases=aliases,
        compiler_params=pltpu.CompilerParams(vmem_limit_bytes=VMEM_BIG),
        cost_estimate=cost(1.5 * count),
    )(*ins)


def wdense_kernel(flag_ref, a_ref, rd_ref, rh_ref, h_ref, keep_ref, send_ref):
    core = flag_ref[1]
    grads = []
    for left, right in ((a_ref, rd_ref), (rh_ref, h_ref)):
        grads.append((dot_nt(left[...], right[...]) * (1.0 / LOSS_SCALE)).astype(BF))
    start = 0
    for grad in grads:
        size = grad.shape[0]
        for half in range(2):
            tile0 = grad[:, 256 * half : 256 * half + 128]
            tile1 = grad[:, 256 * half + 128 : 256 * half + 256]
            keep_ref[0, half, start : start + size, :] = jnp.where(core == 0, tile0, tile1)
            send_ref[0, half, start : start + size, :] = jnp.where(core == 0, tile1, tile0)
        start += size


def wdense(flag, a3, rd, rh, h):
    out = pl.BlockSpec((1, 2, 512, 128), lambda i, *_: (i, 0, 0, 0))
    return pl.pallas_call(
        wdense_kernel,
        out_shape=(sds((8, 2, 512, 128), BF), sds((8, 2, 512, 128), BF)),
        grid_spec=pltpu.PrefetchScalarGridSpec(
            num_scalar_prefetch=1,
            grid=(8,),
            in_specs=[
                pl.BlockSpec((392, LANES), lambda i, *_: (i, 0)),
                whole((512, LANES)),
                pl.BlockSpec((120, LANES), lambda i, *_: (i, 0)),
                whole((512, LANES)),
            ],
            out_specs=[out, out],
        ),
        compiler_params=pltpu.CompilerParams(vmem_limit_bytes=VMEM_BIG),
        cost_estimate=cost(8),
    )(flag, a3, rd, rh, h)


def wconv3_kernel(*refs):
    columns, (r_ref, g_ref, acc) = refs[:4], refs[4:]
    q = pl.program_id(0)

    @pl.when(q == 0)
    def _():
        acc[...] = jnp.zeros_like(acc)

    left = jnp.concatenate([ref[:, LANES * u : LANES * (u + 7)] for u in range(3) for ref in columns], axis=0)
    last = jnp.where(q < 3, r_ref[:, 64:, :], jnp.zeros((7, 64, LANES), BF))
    right = jnp.concatenate([jnp.concatenate([r_ref[i, :64], last[i]], axis=0) for i in range(7)], axis=1)
    acc[...] += dot_nt(left, right)

    @pl.when(q == 3)
    def _():
        for u in range(3):
            for v in range(3):
                at = 256 * u + 64 * v
                part = acc[at : at + 64, :64] + acc[at + 64 : at + 128, 64:]
                g_ref[:, 192 * u + 64 * v : 192 * u + 64 * v + 64] = part.T * (1.0 / LOSS_SCALE)


def wconv3(a2, r3):
    return call(
        wconv3_kernel,
        sds((64, 576), F32),
        [pl.BlockSpec((64, 9 * LANES), lambda q, k=k: (jnp.minimum(2 * q + k, 8), 0)) for k in range(4)]
        + [pl.BlockSpec((7, 128, LANES), lambda q: (0, q, 0))],
        whole((64, 576)),
        us=7,
        grid=(4,),
        scratch=[pltpu.VMEM((768, 128), F32)],
    )(a2, a2, a2, a2, r3.reshape(7, 448, LANES))


def wconv2_kernel(a0_ref, a1_ref, r_ref, g_ref, acc):
    q = pl.program_id(0)

    @pl.when(q == 0)
    def _():
        acc[...] = jnp.zeros_like(acc)

    left = jnp.concatenate(
        [ref[e, :, LANES * t : LANES * (t + 9)] for t in range(2) for e in range(2) for ref in (a0_ref, a1_ref)],
        axis=0,
    )
    last = jnp.where(q < 4, r_ref[64:, :], jnp.zeros((64, 9 * LANES), BF))
    acc[...] += dot_nt(left, jnp.concatenate([r_ref[:64, :], last], axis=0))

    @pl.when(q == 4)
    def _():
        for u in range(4):
            at = 192 * u
            g_ref[128 * u : 128 * u + 128, :] = (acc[at : at + 128, :64] + acc[at + 64 : at + 192, 64:]) * (
                1.0 / LOSS_SCALE
            )


def wconv2(a1, r2):
    return call(
        wconv2_kernel,
        sds((512, 64), F32),
        [
            pl.BlockSpec((2, 128, 10 * LANES), lambda q: (0, q, 0)),
            pl.BlockSpec((2, 64, 10 * LANES), lambda q: (0, jnp.minimum(2 * q + 2, 9), 0)),
            pl.BlockSpec((128, 9 * LANES), lambda q: (q, 0)),
        ],
        whole((512, 64)),
        us=9,
        grid=(5,),
        scratch=[pltpu.VMEM((768, 128), F32)],
    )(hbm(a1), hbm(a1), r2)


def wconv1_kernel(x_ref, x0_ref, r_ref, g_ref, acc, before):
    step = pl.program_id(0)

    @pl.when(step == 0)
    def _():
        acc[...] = jnp.zeros_like(acc)
        before[...] = x0_ref[...]

    def column(dy, rows, c):
        if c:
            return x_ref[dy, rows, LANES * (c - 1) : LANES * c]
        return before[dy, rows, :]

    total = acc[...]
    for g in range(5):
        rows = slice(64 * g, 64 * g + 80)
        left = jnp.concatenate(
            [
                jnp.concatenate([column(dy, rows, ii + t) for ii in range(4)], axis=1)
                for t in range(2)
                for dy in range(4)
            ],
            axis=0,
        )
        right = jnp.concatenate(
            [r_ref[ii % 2, 128 * g : 128 * g + 128, LANES * (ii // 2) : LANES * (ii // 2 + 1)] for ii in range(4)],
            axis=1,
        )
        total = total + dot_nt(left, right)
    acc[...] = total
    before[...] = x_ref[:, :, 3 * LANES :]

    @pl.when(step == 4)
    def _():
        for dy in range(8):
            part = jnp.zeros((32, 32), F32)
            for jj in range(4):
                part = part + acc[80 * dy + 16 * jj : 80 * dy + 16 * jj + 32, 32 * jj : 32 * jj + 32]
            g_ref[32 * dy : 32 * dy + 32, :] = part * (1.0 / LOSS_SCALE)


def wconv1(xt, x0, r1):
    return call(
        wconv1_kernel,
        sds((256, 32), F32),
        [
            pl.BlockSpec((4, 336, 4 * LANES), lambda s: (0, 0, s)),
            whole((4, 336, LANES)),
            pl.BlockSpec((2, 640, 2 * LANES), lambda s: (0, 0, s)),
        ],
        whole((256, 32)),
        us=13,
        grid=(5,),
        scratch=[pltpu.VMEM((640, 128), F32), pltpu.VMEM((4, 336, LANES), BF)],
    )(hbm(xt), x0, hbm(r1))


SMALL_ROWS = 704


def lanes_of(shards):
    return max(1, 128 // shards)


def slot_rows(capacity):
    return (capacity + 7) // 8 * 8


def pack_kernel(shards, capacity, flag_ref, *refs):
    b1_refs, (b2_ref, b3_ref, g1_ref, g2_ref, g3_ref, db_ref, hb_ref, loss_ref, owner_ref, p_ref, w) = refs[:-11], refs[-11:]
    scale = 1.0 / LOSS_SCALE
    w[...] = jnp.zeros_like(w)
    for k in range(4):
        w[64 * k : 64 * k + 64, :] = g3_ref[:, 128 * k : 128 * k + 128]
    w[256:320, :64] = g3_ref[:, 512:]
    w[320:576, :64] = g2_ref[:256, :]
    w[320:576, 64:] = g2_ref[256:, :]
    w[576:704, :32] = g1_ref[:128, :]
    w[576:704, 32:64] = g1_ref[128:, :]
    total = b1_refs[0][...]
    for ref in b1_refs[1:]:
        total = total + ref[...]
    for column, value in ((64, total), (65, b2_ref[...]), (66, b3_ref[...])):
        w[576 : 576 + value.shape[0], column : column + 1] = jnp.sum(value, axis=1, keepdims=True) * scale
    for k in range(4):
        w[576:704, 67 + k : 68 + k] = db_ref[128 * k : 128 * k + 128, :] * scale
    for half in range(2):
        for k in range(4):
            start = 459 * half + 128 * k
            size = min(128, 459 * (half + 1) - start)
            w[576 : 576 + size, 71 + 4 * half + k : 72 + 4 * half + k] = hb_ref[start : start + size, :]

    owner = owner_ref[...]
    rows = owner.shape[1]
    owner_f = owner.astype(F32)
    down = jnp.broadcast_to(owner_f, (8, rows)).T[:, :1]
    same = (down == owner_f) & (
        lax.broadcasted_iota(jnp.int32, (rows, rows), 0) < lax.broadcasted_iota(jnp.int32, (rows, rows), 1)
    )
    slot = jnp.sum(same.astype(F32), axis=0, keepdims=True)
    group, height = lanes_of(shards), slot_rows(capacity)
    place = lax.broadcasted_iota(jnp.int32, (height, rows), 0).astype(F32)
    spread = jnp.where(place == slot, loss_ref[...], 0.0).astype(BF)
    lane = lax.broadcasted_iota(jnp.int32, (128, rows), 0)
    here = shards * lax.rem(owner, group) + flag_ref[2]
    for g in range(shards // group):
        hot = ((lane == here) & (owner // group == g)).astype(BF)
        w[SMALL_ROWS + height * g : SMALL_ROWS + height * g + height, :] = dot_nt(spread, hot)
    p_ref[...] = w[...].astype(BF)


def pack(flag, b1s, shards, capacity, *ins):
    total = SMALL_ROWS + shards // lanes_of(shards) * slot_rows(capacity)
    ins = tuple(b1s) + ins
    return call(
        functools.partial(pack_kernel, shards, capacity),
        sds((total, 128), BF),
        [pl.BlockSpec(memory_space=pltpu.SMEM)] + [whole(a.shape) for a in ins],
        whole((total, 128)),
        scratch=[pltpu.VMEM((total, 128), F32)],
        us=3,
    )(flag, *ins)


def split_kernel(shards, capacity, flag_ref, own_ref, got_ref, k1, b1, k2, b2, k3, b3, db, hb, prio, w):
    own = flag_ref[0] == 1
    w[...] = jnp.where(own, own_ref[...].astype(F32), got_ref[...].astype(F32))

    def pick(low, high):
        return jnp.where(own, low, high)

    k1[...] = pick(w[576:704, :32], w[576:704, 32:64])
    k2[...] = pick(w[320:576, :64], w[320:576, 64:])
    for n in range(9):
        rows = slice(64 * (n // 2), 64 * (n // 2) + 64)
        part = w[rows, 64 * (n % 2) : 64 * (n % 2) + 64]
        k3[n] = pick(part[:32], part[32:])
    columns = w[576:704, :].T
    b1[...] = pick(columns[64:65, :16], columns[64:65, 16:32])
    for ref, at in ((b2, 65), (b3, 66)):
        ref[...] = pick(columns[at : at + 1, :32], columns[at : at + 1, 32:64])
    for k in range(2):
        db[:, 128 * k : 128 * k + 128] = pick(columns[67 + k : 68 + k], columns[69 + k : 70 + k])
    for k in range(4):
        size = min(128, 459 - 128 * k)
        hb[:, 128 * k : 128 * k + size] = pick(columns[71 + k : 72 + k, :size], columns[75 + k : 76 + k, :size])
    group, height = lanes_of(shards), slot_rows(capacity)
    me = flag_ref[2]
    block = w[pl.ds(pl.multiple_of(SMALL_ROWS + height * (me // group), 8), height), :]
    if group > 1:
        block = pltpu.roll(block, lax.rem(128 - shards * lax.rem(me, group), 128), 1)
    half = capacity // 2
    prio[:, 0, :] = pick(block[:half, :shards], block[half : 2 * half, :shards])


def split(flag, own, got, shards, capacity):
    shapes = (
        (128, 32),
        (1, 16),
        (256, 64),
        (1, 32),
        (9, 32, 64),
        (1, 32),
        (1, 256),
        (1, 459),
        (capacity // 2, 1, shards),
    )
    return call(
        functools.partial(split_kernel, shards, capacity),
        tuple(sds(s, F32) for s in shapes),
        [pl.BlockSpec(memory_space=pltpu.SMEM), whole(own.shape), whole(got.shape)],
        [whole(s) for s in shapes],
        scratch=[pltpu.VMEM(own.shape, F32)],
        us=2,
    )(flag, own, got)


def unchunk_kernel(flag_ref, cur_ref, other_ref, d_ref, h_ref):
    core, code = flag_ref[1], flag_ref[3]
    for k in range(2):
        block = (2 * pl.program_id(0) + k) ^ code
        cur, other = cur_ref[block].astype(F32), other_ref[block].astype(F32)
        for lane, tile in enumerate((jnp.where(core == 0, cur, other), jnp.where(core == 0, other, cur))):
            d_ref[392 * k : 392 * k + 392, 128 * lane : 128 * lane + 128] = tile[:392]
            h_ref[120 * k : 120 * k + 120, 128 * lane : 128 * lane + 128] = tile[392:]


def unchunk(flag, cur, other):
    return call(
        unchunk_kernel,
        (sds((3136, 256), F32), sds((LOGITS, 256), F32)),
        [pl.BlockSpec(memory_space=pltpu.SMEM), whole(cur.shape), whole(other.shape)],
        [pl.BlockSpec((784, 256), lambda i: (i, 0)), pl.BlockSpec((240, 256), lambda i: (i, 0))],
        us=4,
        grid=(4,),
    )(flag, cur, other)


def after(value, *others):
    return lax.optimization_barrier((value,) + others)[0]


def hand(value):
    return lax.ppermute(value, "pair", [(0, 1)])


def swap(value, bit):
    devices = lax.axis_size("batch")
    return lax.ppermute(value, "batch", [(i, i ^ bit) for i in range(devices)])


def add(left, right):
    return (left.astype(F32) + right.astype(F32)).astype(BF)


def split_blocks(cur):
    devices = lax.axis_size("batch")
    spread = devices // 16
    if spread > 1:
        cur = cur.reshape(8, 2, spread, 512 // spread, 128).transpose(0, 2, 1, 3, 4)
        cur = cur.reshape(devices // 2, 2, 512 // spread, 128)
    return cur


def halve(cur, me, bit):
    mine = (me // bit) % 2
    pairs = cur.reshape((cur.shape[0] // 2, 2) + cur.shape[1:])
    send = lax.dynamic_index_in_dim(pairs, 1 - mine, axis=1, keepdims=False)
    keep = lax.dynamic_index_in_dim(pairs, mine, axis=1, keepdims=False)
    return keep, swap(send, bit)


def unmix(blocks, code):
    bit = 1
    while bit < blocks.shape[0]:
        pairs = blocks.reshape((-1, 2, bit) + blocks.shape[1:])
        blocks = jnp.where((code // bit) % 2 == 1, pairs[:, ::-1], pairs).reshape(blocks.shape)
        bit *= 2
    return blocks


def join(cur, other):
    return jnp.stack([cur, other], axis=1).reshape((2 * cur.shape[0],) + cur.shape[1:])


def local(
    frames,
    kernel_first,
    bias_first,
    kernel_second,
    bias_second,
    kernel_third,
    bias_third,
    dense_weight,
    dense_bias,
    head_weight,
    head_bias,
    taken_actions,
    greedy_actions,
    done_flags,
    bin_lower,
    bin_fraction,
    owner_shard,
):
    online = lax.axis_index("pair") == 0
    me = lax.axis_index("batch")
    shards = lax.axis_size("batch")
    rows = frames.shape[1]
    capacity = 2 * ((rows + shards - 1) // shards)
    block = me // 2 if shards == 16 else me * 0
    flag = jnp.stack([online.astype(jnp.int32), me % 2, me, block]).astype(jnp.int32)
    xv = frames[0].transpose(2, 3, 1, 0)
    k1, k2, k3 = kernel_first[0], kernel_second[0], kernel_third[0]
    ones = jnp.zeros((16, LANES), BF).at[0].set(1)
    t1, t2, t3, b2, kernels = bands(k1, bias_first, k2, bias_second, k3, bias_third)

    kernels = hand(kernels)
    a1, s1, xt, early, x0 = conv1(xv, t1, ones, 0, EARLY, ())
    early = hand(after(early, kernels))
    a1, s1, xt, late = conv1(xv, t1, ones, EARLY, 10, (a1, s1, xt))
    late = hand(late)
    a2, s2, a3, s3 = conv23(a1, t2, b2, t3, ones)
    wd = dense_weight[0]
    wht = head_weight[0].T
    pd = lax.dot_general(wd, a3, (((0,), (0,)), ((), ())), preferred_element_type=F32)
    taken = taken_actions[None, :]
    sel = jnp.where(online, taken, greedy_actions[None, :])
    h, sd, lp, cho = head(pd, dense_bias, wht, head_bias, sel)
    cho = lax.ppermute(cho, "pair", [(1, 0)])
    t3b, t2b, t2b_online, t1b = bands_back(after(flag, lp), k1, k2, k3, kernels)
    row_loss, rh, hb = loss(after(cho, t1b), done_flags[None, :], bin_lower.T, bin_fraction.T, lp, taken)

    diff_dense = lax.dot_general(wht, rh, (((0,), (0,)), ((), ())), preferred_element_type=F32)
    diff_dense = diff_dense * (0.5 * sd.astype(F32))
    rd = diff_dense.astype(BF)
    db = jnp.sum(diff_dense, axis=1, keepdims=True)

    keep, send = wdense(flag, a3, after(rd, early), rh, h)
    cur = split_blocks(add(keep, swap(send, 1)))
    keep, got = halve(cur, me, 2)

    r3, b3g, r2, r2p, b2g = dthird(wd, rd, s3, t3b, s2)
    r2p = hand(r2p)
    r1, near0, near1, b1g = dconv2(r2, t2b, s1, FAR, 10 - FAR, True, None)
    cur = add(after(keep, b1g), got)
    keep, far = halve(cur, me, 4)
    r1, b1g_far = dconv2(after(r2, got, late), t2b, s1, 0, FAR, False, r1)
    b1s = [b1g, b1g_far]
    g3 = wconv3(a2, after(r3, b1g_far))
    bit = 4
    while 2 * bit < shards:
        cur = add(after(keep, g3) if bit == 4 else keep, far)
        bit *= 2
        keep, far = halve(cur, me, bit)
    g1 = wconv1(xt, x0, after(r1, g3))
    chunk = add(after(keep, g1), far)[0]
    far_chunk = hand(chunk[1])
    near0 = hand(after(near0, far))
    near1 = hand(after(near1, far))
    mine = jnp.where(online, chunk[0], far_chunk)
    g2 = wconv2(a1, after(r2, chunk))

    cur = mine[None]
    part = swap(cur, bit)
    small = pack(after(flag, part, r2p), b1s, shards, capacity, b2g, b3g, g1, g2, g3, db, hb, row_loss, owner_shard.T)
    small = add(small, swap(small, 1))
    got = swap(small, 2)
    cur = join(cur, part)
    part = swap(cur, bit // 2)
    out, edge = dframes(flag, after(r1, small, cur, near0), (r2p, early, late, t2b_online), t1b, rows, 0, FAR, None, None)
    cur = join(after(cur, edge), part)
    small = add(after(small, edge), got)
    part, got = swap(cur, bit // 4), swap(small, 4)
    small = add(small, got)
    got = swap(small, 8)
    small = add(after(small, near1), got)
    cur = join(after(cur, got), part)
    lower = 16
    while lower < shards:
        small = add(small, swap(small, lower))
        cur = join(cur, swap(cur, 2 * bit // lower))
        lower *= 2
    other = swap(cur, 1)
    far_small = hand(small)
    out, edge = dframes(flag, after(r1, cur, small), [near0, near1], t1b, rows, FAR, 10 - FAR, edge, out)
    if shards != 16:
        cur, other = (unmix(v, me // 2).reshape(8, 512, 128) for v in (cur, other))
    dense_out, head_out = unchunk(flag, cur, other)
    o = split(flag, small, far_small, shards, capacity)
    return (
        o[0].reshape(4, 8, 4, 32),
        o[1].reshape(16),
        o[2].reshape(2, 4, 32, 64),
        o[3].reshape(32),
        o[4].reshape(3, 3, 32, 64).transpose(0, 1, 3, 2),
        o[5].reshape(32),
        dense_out,
        o[6].reshape(256),
        head_out.T,
        o[7].reshape(459),
        out.transpose(3, 2, 0, 1),
        o[8].transpose(1, 2, 0),
    )


def solution(mesh):
    return jax.shard_map(
        local,
        mesh=mesh,
        in_specs=(
            P("pair", "batch", None, None, None),
            P("pair", None, None, None, None),
            P("pair", None),
            P("pair", None, None, None, None),
            P("pair", None),
            P("pair", None, None, None, None),
            P("pair", None),
            P("pair", None, None),
            P("pair", None),
            P("pair", None, None),
            P("pair", None),
            P("batch"),
            P("batch"),
            P("batch"),
            P("batch", None),
            P("batch", None),
            P("batch", None),
        ),
        out_specs=(
            P("pair", None, None, None),
            P("pair"),
            P("pair", None, None, None),
            P("pair"),
            P(None, None, None, "pair"),
            P("pair"),
            P(None, "pair"),
            P("pair"),
            P("pair", None),
            P("pair"),
            P("batch", "pair", None, None),
            P("batch", None, "pair"),
        ),
        check_vma=False,
    )
```
